32 devices in a mesh: rec: 4 (over x, core), tm: 8 (over z, y).
Axes of the slice: x: 2, y: 2, z: 4, core: 2. Of those that a mesh axis runs over, the one named last changes fastest.
Arguments:
- signal: bfloat16 [8192, 1280], P(('rec', 'tm')), parts along dimension 0, may hold values from -6 to 6
- position_kernel: bfloat16 [1280, 80, 128], P('tm'), may hold values from -0.0625 to 0.0625
- position_bias: float32 [1280], P('tm'), may hold values from -3 to 3
- layer_gain: float32 [1280], replicated, may hold values from 0.5 to 1.5
- layer_shift: float32 [1280], replicated, may hold values from -3 to 3
- query_weight: bfloat16 [1280, 640], P('tm'), may hold values from -0.25 to 0.25
- query_bias: float32 [640], replicated, may hold values from -4 to 4
- key_weight: bfloat16 [1280, 640], P('tm'), may hold values from -0.25 to 0.25
- value_weight: bfloat16 [1280, 640], P('tm'), may hold values from -0.15625 to 0.15625
- value_bias: float32 [640], replicated, may hold values from -3 to 3
- output_weight: bfloat16 [640, 1280], P(None, 'tm'), may hold values from -0.25 to 0.25
- output_bias: float32 [1280], replicated, may hold values from -3 to 3
- key_blocks: int32 [64, 5], P(('rec', 'tm')), parts along dimension 0, may hold values from -1 to 15, as said below
- global_blocks: int32 [16], P('rec'), parts along dimension 0, may hold values from 0 to 15, as said below
Outputs:
- encoded: bfloat16 [8192, 1280], P(('rec', 'tm')), parts along dimension 0
The draws below stay inside these ranges and needn't reach their ends.
There are 4 independent parts, one for each index of `rec`. The reference program is written for one: setup_inputs(seed, part) draws one part's arguments, and reference() takes and returns one part's arrays. A program takes and returns all parts, laid end to end along the dimension named above; an argument that names none is the same for every part. Nothing has to cross between parts.
Inputs may be any that keep to these rules, and one draw needn't show every extreme that they name: `key_blocks`: row b lists distinct blocks in any order, padded with -1; it always holds b itself, and otherwise only blocks c with |c - b| <= 2 that lie in b's segment, segments being runs of consecutive blocks of the recording. `global_blocks`: 4 distinct block numbers of the recording.
All inputs are finite; a program needn't handle non-finite values.
Results may differ from the reference program's by a relative error of at most 0.0055.
Values may be sent and summed in bfloat16 or wider, within the bound.
A program may use at most 128 MiB of HBM per device.

```python
import math
import jax
import jax.numpy as jnp
from jax import lax

D = 1280
GROUPS = 16
KERNEL = 128
HEAD = 80
HEADS = 8
BLOCK = 128
WIN = 2
GLOBALS = 4
GW = 80
FRAMES = 2048
NQB = 16


def draw_query_weight(key, part):
    full = jax.random.normal(jax.random.fold_in(key, 1), (D, HEADS * HEAD), jnp.float32) * (3.0 * D ** (-0.5))
    return jnp.clip(full, -0.25, 0.25).astype(jnp.bfloat16)


def draw_key_weight(key, part):
    full = jax.random.normal(jax.random.fold_in(key, 2), (D, HEADS * HEAD), jnp.float32) * D ** (-0.5)
    return jnp.clip(full, -0.25, 0.25).astype(jnp.bfloat16)


def draw_key_blocks(key, part):
    span = 2 * WIN + 1
    block = jnp.arange(NQB, dtype=jnp.int32)
    cuts = (jax.random.randint(jax.random.fold_in(key, 11), (NQB,), 0, 4) == 0) & (block > span)
    segment = jnp.cumsum(cuts.astype(jnp.int32))
    nearby = block[:, None] + jnp.arange(span, dtype=jnp.int32)[None, :] - WIN
    inside = (nearby >= 0) & (nearby < NQB)
    clamped = jnp.clip(nearby, 0, NQB - 1)
    same = inside & (segment[clamped] == segment[:, None])
    listed = jnp.where(same, nearby, -1)
    ranks = jax.random.randint(jax.random.fold_in(key, 12), (NQB, span), 0, 1 << 20) * span + jnp.arange(span, dtype=jnp.int32)[None, :]
    order = jnp.argsort(ranks, axis=1)
    return jnp.take_along_axis(listed, order, axis=1).astype(jnp.int32)


def draw_global_blocks(key, part):
    return jax.random.permutation(jax.random.fold_in(key, 13), NQB)[:GLOBALS].astype(jnp.int32)


def shard_levels(key, extent, cuts, least, high):
    level, own = 1.0, jax.random.fold_in(key, 6)
    for axis_at, parts in cuts:
        steps = jnp.exp(jax.random.uniform(jax.random.fold_in(own, axis_at), (parts,), jnp.float32, least / len(cuts), high / len(cuts)))
        level = level * jnp.repeat(steps, extent[axis_at] // parts).reshape([-1 if axis == axis_at else 1 for axis in range(len(extent))])
    return level


def gaussian(stream_key, extent, spread, limit, cuts=(), kind=jnp.bfloat16):
    factor_of = shard_levels(stream_key, extent, cuts, -0.22, 0.18) if cuts else 1.0
    result = jax.random.normal(stream_key, extent, jnp.float32) * spread * factor_of
    return jnp.minimum(jnp.maximum(result, -limit), limit).astype(kind)


def setup_inputs(seed: int = 0, part: int = 0) -> dict:
    key_list = jax.random.split(jax.random.key(seed), 15)
    own_keys = jax.random.split(jax.random.fold_in(key_list[14], part), 15)
    return {
        "signal": gaussian(own_keys[0], (FRAMES, D), 1.0, 6.0, ((0, 8),)),
        "position_kernel": gaussian(key_list[1], (D, GW, KERNEL), (GW * KERNEL) ** -0.5, 0.0625, ((0, 8),)),
        "position_bias": gaussian(key_list[2], (D,), 0.5, 3.0, ((0, 8),), jnp.float32),
        "layer_gain": jnp.clip(jax.random.uniform(key_list[3], (D,), jnp.float32, 0.5, 1.5), 0.5, 1.5),
        "layer_shift": gaussian(key_list[4], (D,), 0.5, 3.0, (), jnp.float32),
        "query_weight": draw_query_weight(jax.random.fold_in(key_list[14], 71), part),
        "query_bias": gaussian(key_list[6], (HEADS * HEAD,), 1.0, 4.0, (), jnp.float32),
        "key_weight": draw_key_weight(jax.random.fold_in(key_list[14], 71), part),
        "value_weight": gaussian(key_list[8], (D, HEADS * HEAD), D ** -0.5, 0.15625, ((0, 8),)),
        "value_bias": gaussian(key_list[9], (HEADS * HEAD,), 0.5, 3.0, (), jnp.float32),
        "output_weight": gaussian(key_list[10], (HEADS * HEAD, D), (HEADS * HEAD) ** -0.5, 0.25, ((1, 8),)),
        "output_bias": gaussian(key_list[11], (D,), 0.5, 3.0, (), jnp.float32),
        "key_blocks": draw_key_blocks(jax.random.fold_in(jax.random.fold_in(key_list[14], part), 71), part),
        "global_blocks": draw_global_blocks(jax.random.fold_in(jax.random.fold_in(key_list[14], part), 71), part),
    }


EPSILON = 1e-05

def attend(queries, key_rows, value_rows, allowed):
    block_count, row_count, heads_width = queries.shape
    query_heads = queries.reshape(block_count, row_count, HEADS, HEAD).astype(jnp.float32)
    key_heads = key_rows.reshape(block_count, key_rows.shape[1], HEADS, HEAD).astype(jnp.float32)
    value_heads = value_rows.reshape(block_count, value_rows.shape[1], HEADS, HEAD).astype(jnp.float32)
    scores = jnp.einsum('bqhe,bkhe->bhqk', query_heads, key_heads, precision=lax.Precision.HIGHEST) * (1.0 / math.sqrt(HEAD))
    scores = jnp.where(allowed[:, None, None, :], scores, -jnp.inf)
    row_max = lax.optimization_barrier(jnp.max(scores, axis=-1, keepdims=True))
    weights = jnp.exp(scores - row_max)
    row_total = lax.optimization_barrier(jnp.sum(weights, axis=-1))
    probability = weights.astype(jnp.bfloat16).astype(jnp.float32)
    context_sum = jnp.einsum('bhqk,bkhe->bqhe', probability, value_heads, precision=lax.Precision.HIGHEST)
    context = context_sum / jnp.transpose(row_total, (0, 2, 1))[..., None]
    return context.reshape(block_count, row_count, heads_width).astype(jnp.bfloat16)

def reference(signal, position_kernel, position_bias, layer_gain, layer_shift, query_weight, query_bias, key_weight, value_weight, value_bias, output_weight, output_bias, key_blocks, global_blocks):
    stacked = signal.astype(jnp.float32).T[None]
    kernels = position_kernel.astype(jnp.float32)
    response = lax.conv_general_dilated(stacked, kernels, (1,), [(KERNEL // 2, KERNEL // 2 - 1)], dimension_numbers=('NCH', 'OIH', 'NCH'), feature_group_count=GROUPS, precision=lax.Precision.HIGHEST)[0]
    position = jax.nn.gelu(response + position_bias[:, None], approximate=False).astype(jnp.bfloat16)
    hidden = signal.astype(jnp.float32) + position.T.astype(jnp.float32)
    average = lax.optimization_barrier(jnp.mean(hidden, axis=-1, keepdims=True))
    centered = hidden - average
    variance = lax.optimization_barrier(jnp.mean(centered * centered, axis=-1, keepdims=True))
    normed = (centered * lax.rsqrt(variance + EPSILON) * layer_gain + layer_shift).astype(jnp.bfloat16)
    queries = (jnp.dot(normed, query_weight, preferred_element_type=jnp.float32) + query_bias).astype(jnp.bfloat16)
    keys = jnp.dot(normed, key_weight, preferred_element_type=jnp.float32).astype(jnp.bfloat16)
    values = (jnp.dot(normed, value_weight, preferred_element_type=jnp.float32) + value_bias).astype(jnp.bfloat16)
    heads_width = HEADS * HEAD
    block_ids = jnp.concatenate([key_blocks, jnp.broadcast_to(global_blocks[None, :], (NQB, GLOBALS))], axis=1)
    repeated = jnp.any(global_blocks[None, :, None] == key_blocks[:, None, :], axis=-1)
    allowed = jnp.concatenate([key_blocks >= 0, jnp.logical_not(repeated)], axis=1)
    key_table = keys.reshape(NQB, BLOCK, heads_width)
    value_table = values.reshape(NQB, BLOCK, heads_width)
    query_table = queries.reshape(NQB, BLOCK, heads_width)

    def one_block(operands):
        query_block, identifiers, permitted = operands
        clamped = jnp.maximum(identifiers, 0).astype(jnp.int32)
        key_rows = key_table[clamped].reshape(1, -1, heads_width)
        value_rows = value_table[clamped].reshape(1, -1, heads_width)
        return attend(query_block[None], key_rows, value_rows, jnp.repeat(permitted, BLOCK)[None])[0]
    context = lax.map(one_block, (query_table, block_ids, allowed)).reshape(FRAMES, heads_width)
    projected = jnp.dot(context, output_weight, preferred_element_type=jnp.float32)
    return (hidden + projected + output_bias).astype(jnp.bfloat16)
```

```python
import math

import jax
import jax.numpy as jnp
import numpy as np
from jax import lax
from jax.experimental import pallas as pl
from jax.experimental.pallas import tpu as pltpu
from jax.sharding import PartitionSpec as P

HEAD = 80
HEADS = 8
BLOCK = 128
GLOBALS = 4


EPSILON = 1e-05


def attend(queries, key_rows, value_rows, allowed):
    block_count, row_count, heads_width = queries.shape
    query_heads = queries.reshape(block_count, row_count, HEADS, HEAD)
    key_heads = key_rows.reshape(block_count, key_rows.shape[1], HEADS, HEAD)
    value_heads = value_rows.reshape(block_count, value_rows.shape[1], HEADS, HEAD)
    scores = jnp.einsum(
        "bqhe,bkhe->bhqk", query_heads, key_heads, preferred_element_type=jnp.float32
    ) * (1.0 / math.sqrt(HEAD))
    scores = jnp.where(allowed[:, None, None, :], scores, -jnp.inf)
    row_max = jnp.max(scores, axis=-1, keepdims=True)
    weights = jnp.exp(scores - row_max)
    row_total = jnp.sum(weights, axis=-1)
    probability = weights.astype(jnp.bfloat16)
    context_sum = jnp.einsum(
        "bhqk,bkhe->bqhe", probability, value_heads, preferred_element_type=jnp.float32
    )
    context = context_sum / jnp.transpose(row_total, (0, 2, 1))[..., None]
    return context.reshape(block_count, row_count, heads_width).astype(jnp.bfloat16)


def general(
    signal,
    position_kernel,
    position_bias,
    layer_gain,
    layer_shift,
    query_weight,
    query_bias,
    key_weight,
    value_weight,
    value_bias,
    output_weight,
    output_bias,
    key_blocks,
    global_blocks,
):
    devices = lax.axis_size("tm")
    frame_count, model_width = signal.shape
    channel_share, group_width, kernel_taps = position_kernel.shape
    inner_width = max(channel_share, group_width)
    folded = signal.T
    if channel_share >= group_width:
        outgoing = folded.reshape(devices, channel_share, frame_count)
    else:
        start_groups = np.arange(devices) * channel_share // group_width
        grouped = folded.reshape(model_width // group_width, group_width, frame_count)
        outgoing = jnp.stack(
            [grouped[at * channel_share // group_width] for at in range(devices)]
        )
    incoming = lax.all_to_all(outgoing, "tm", split_axis=0, concat_axis=2, tiled=True)
    outputs = channel_share if channel_share < group_width else group_width
    spread = jnp.pad(
        incoming.reshape(inner_width // group_width, group_width, -1),
        ((0, 0), (0, 0), (kernel_taps // 2, kernel_taps // 2 - 1)),
    )
    frames = incoming.shape[-1]
    by_tap = position_kernel.reshape(-1, outputs, group_width, kernel_taps).transpose(3, 0, 1, 2)

    def tap(at, total):
        window = lax.dynamic_slice_in_dim(spread, at, frames, axis=2)
        return total + jnp.einsum(
            "goi,git->got", by_tap[at], window, preferred_element_type=jnp.float32
        )

    response = lax.fori_loop(
        0, kernel_taps, tap, jnp.zeros((spread.shape[0], outputs, frames), jnp.float32)
    ).reshape(channel_share, frames)
    position = jax.nn.gelu(response + position_bias[:, None], approximate=False).astype(
        jnp.bfloat16
    )
    returned = lax.all_to_all(position, "tm", split_axis=1, concat_axis=0, tiled=True)
    hidden = signal.astype(jnp.float32) + returned.T.astype(jnp.float32)
    average = jnp.mean(hidden, axis=-1, keepdims=True)
    centered = hidden - average
    variance = jnp.mean(centered * centered, axis=-1, keepdims=True)
    normed = (centered * lax.rsqrt(variance + EPSILON) * layer_gain + layer_shift).astype(
        jnp.bfloat16
    )
    heads_width = query_weight.shape[1]
    zero_sums = jnp.zeros((frame_count, heads_width), jnp.float32)
    totals = (zero_sums, zero_sums, zero_sums)
    pieces = (
        lax.all_gather(query_weight, "tm", axis=0, tiled=True),
        lax.all_gather(key_weight, "tm", axis=0, tiled=True),
        lax.all_gather(value_weight, "tm", axis=0, tiled=True),
    )
    columns = lax.slice_in_dim(normed, 0, pieces[0].shape[0], axis=1)
    query_sum, key_sum, value_sum = tuple(
        (
            running + jnp.dot(columns, weight_rows, preferred_element_type=jnp.float32)
            for running, weight_rows in zip(totals, pieces)
        )
    )
    queries = (query_sum + query_bias).astype(jnp.bfloat16)
    key_part = key_sum.astype(jnp.bfloat16)
    value_part = (value_sum + value_bias).astype(jnp.bfloat16)
    key_value = jnp.stack((key_part, value_part), axis=1)
    per_device = frame_count // BLOCK
    repeated = jnp.any(global_blocks[None, :, None] == key_blocks[:, None, :], axis=-1)
    whole = lax.all_gather(key_value, "tm", axis=0, tiled=True)
    block_ids = jnp.concatenate(
        [key_blocks, jnp.broadcast_to(global_blocks[None, :], (per_device, GLOBALS))], axis=1
    )
    allowed = jnp.concatenate([key_blocks >= 0, jnp.logical_not(repeated)], axis=1)
    table = whole.reshape(-1, BLOCK, 2, heads_width)
    chosen = jnp.maximum(block_ids, 0)
    candidates = jnp.stack(
        [
            jnp.stack(
                [
                    lax.dynamic_index_in_dim(table, chosen[row, at], 0, keepdims=False)
                    for at in range(chosen.shape[1])
                ]
            )
            for row in range(per_device)
        ]
    )
    key_rows = candidates[:, :, :, 0].reshape(per_device, -1, heads_width)
    value_rows = candidates[:, :, :, 1].reshape(per_device, -1, heads_width)
    allowed_rows = jnp.repeat(allowed, BLOCK, axis=1)
    context = attend(
        queries.reshape(per_device, BLOCK, heads_width), key_rows, value_rows, allowed_rows
    ).reshape(frame_count, heads_width)
    projected = jnp.dot(
        context,
        lax.all_gather(output_weight, "tm", axis=1, tiled=True),
        preferred_element_type=jnp.float32,
    )
    return (hidden + projected + output_bias).astype(jnp.bfloat16)


PHASES = 3
GROUP = 80
MEMBERS = 8
QUARTERS = 4
LANES = 128
STEP = 4
STEPS = 44
SPAN = 22
PADDED = 144
MESH = pl.DeviceIdType.MESH
BIG = 1e30
F32 = jnp.float32
BF16 = jnp.bfloat16


def flip(member, bits):
    low = bits % 4
    if low == 1:
        turned = member + 1 - 2 * lax.rem(member, 2)
    elif low == 2:
        turned = member + 2 - 4 * lax.rem(lax.div(member, 2), 2)
    elif low == 3:
        turned = 4 * lax.div(member, 4) + 3 - lax.rem(member, 4)
    else:
        turned = member
    return lax.rem(turned + 4, MEMBERS) if bits >= 4 else turned


def remote(source, target, sends, receives, at, device):
    return pltpu.make_async_remote_copy(
        src_ref=source,
        dst_ref=target,
        send_sem=sends.at[at],
        recv_sem=receives.at[at],
        device_id=device,
        device_id_type=MESH,
    )


class Spread:
    def __init__(self, piece, record, member, sends, receives):
        self.piece, self.record, self.member = piece, record, member
        self.sends, self.receives = sends, receives
        self.across = lax.rem(record + 2, QUARTERS)
        self.beside = record + 1 - 2 * lax.rem(record, 2)

    def copy(self, at, share, quarter, device):
        ref = self.piece(share, quarter)
        return remote(ref, ref, self.sends, self.receives, at, device)

    def plane(self, at):
        bits = at + 1
        if bits <= 4:
            return self.copy(at, self.member, self.record, (self.record, flip(self.member, bits)))
        share = flip(self.member, 4)
        return self.copy(at, share, self.record, (self.record, flip(self.member, bits - 4)))

    def other(self, at):
        return self.copy(7 + at, flip(self.member, at + 1), self.record, (self.across, self.member))

    def core(self, at):
        return self.copy(14 + at, flip(self.member, at + 1), self.record, (self.beside, self.member))

    def last(self, at):
        return self.copy(21 + at, flip(self.member, at + 1), self.across, (self.beside, self.member))

    def first(self):
        for at in (3, 0, 1, 2):
            self.plane(at).start()

    def second(self):
        self.plane(3).wait_recv()
        for at in (4, 5, 6):
            self.plane(at).start()
        self.other(3).start()
        self.core(3).start()
        for at in (0, 1, 2):
            self.plane(at).wait_recv()
            self.other(at).start()
            self.core(at).start()

    def third(self):
        for at in (4, 5, 6):
            self.plane(at).wait_recv()
            self.other(at).start()
            self.core(at).start()

    def fourth(self):
        for at in (3, 0, 1, 2, 4, 5, 6):
            self.other(at).wait_recv()
            self.last(at).start()

    def done(self):
        for at in range(7):
            self.core(at).wait_recv()
            self.last(at).wait_recv()

    def sent(self):
        for at in range(7):
            for copy in (self.plane(at), self.other(at), self.core(at), self.last(at)):
                copy.wait_send()


def whole_kernel(
    unlisted_ref,
    globals_ref,
    marks_ref,
    signal_ref,
    taps_hbm,
    tap_bias_ref,
    gain_ref,
    shift_ref,
    query_ref,
    key_ref,
    value_ref,
    bias_ref,
    output_ref,
    output_bias_ref,
    out_ref,
    taps_ref,
    turned_ref,
    matrix_ref,
    send_ref,
    got_ref,
    frames_ref,
    spread_ref,
    total_ref,
    natural_ref,
    back_ref,
    returned_ref,
    hidden_ref,
    normed_ref,
    rows_ref,
    output_rows_ref,
    output_whole_ref,
    slab_ref,
    headed_ref,
    queries_ref,
    keys_ref,
    values_ref,
    chosen_ref,
    context_ref,
    contexts_ref,
    load_sem,
    signal_send,
    signal_recv,
    back_send,
    back_recv,
    rows_send,
    rows_recv,
    outs_send,
    outs_recv,
    head_send,
    head_recv,
    context_send,
    context_recv,
):
    record, member = lax.axis_index("rec"), lax.axis_index("tm")
    load = pltpu.make_async_copy(taps_hbm, taps_ref, load_sem)
    load.start()

    barrier = pltpu.get_barrier_semaphore()
    across = lax.rem(record + 2, QUARTERS)
    beside = record + 1 - 2 * lax.rem(record, 2)
    peers = [(record, lax.rem(member + at, MEMBERS)) for at in range(1, MEMBERS)]
    for peer in peers + [(across, member), (beside, member)]:
        pl.semaphore_signal(barrier, inc=1, device_id=peer, device_id_type=MESH)

    frame_count = signal_ref.shape[0]
    share = 2 * GROUP
    rest = share - LANES
    for to in range(MEMBERS):
        begin = to * share
        send_ref[to, :frame_count, :] = signal_ref[:, begin : begin + LANES]
        send_ref[to, frame_count:, :] = jnp.concatenate(
            [
                signal_ref[64 * at : 64 * at + 64, begin + LANES : begin + share]
                for at in range(4)
            ],
            axis=1,
        )
    pl.semaphore_wait(barrier, 9)

    def signal_copy(at):
        to = lax.rem(member + at, MEMBERS)
        return remote(
            send_ref.at[to], got_ref.at[member], signal_send, signal_recv, at - 1, (record, to)
        )

    for at in range(1, MEMBERS):
        signal_copy(at).start()
    got_ref[member] = send_ref[member]

    mine = pl.ds(pl.multiple_of(member * share, 32), share)
    for head in range(HEADS):
        columns = slice(head * HEAD, (head + 1) * HEAD)
        joined = jnp.concatenate(
            [
                query_ref[:, columns],
                key_ref[:, columns],
                value_ref[:, columns],
                jnp.zeros((share, 16), BF16),
            ],
            axis=1,
        )
        rows_ref[2 * head, mine, :] = joined[:, :LANES]
        rows_ref[2 * head + 1, mine, :] = joined[:, LANES:]
    heads_width = HEADS * HEAD
    output_rows_ref[member, :heads_width, :] = output_ref[:, :LANES]
    output_rows_ref[member, heads_width : heads_width + share, :] = jnp.concatenate(
        [output_ref[share * at : share * at + share, LANES:] for at in range(4)], axis=1
    )
    output_rows_ref[member, heads_width + share :, :] = jnp.zeros((32, LANES), BF16)

    def rows_piece(of, quarter):
        return rows_ref.at[
            pl.ds(quarter * 4, 4), pl.ds(pl.multiple_of(of * share, 32), share), :
        ]

    def output_piece(of, quarter):
        return output_rows_ref.at[of, pl.ds(pl.multiple_of(quarter * 208, 16), 208), :]

    rows = Spread(rows_piece, record, member, rows_send, rows_recv)
    outs = Spread(output_piece, record, member, outs_send, outs_recv)
    rows.first()

    load.wait()
    unit = (
        lax.broadcasted_iota(jnp.int32, (LANES, LANES), 0)
        == lax.broadcasted_iota(jnp.int32, (LANES, LANES), 1)
    ).astype(BF16)
    empty = jnp.zeros((8, LANES), F32)

    def turn(step, _):
        for at in range(4):
            channel = step * 4 + at
            flat = lax.dot_general(
                unit, taps_ref[channel], (((1,), (1,)), ((), ())), preferred_element_type=F32
            )
            flat = jnp.concatenate([flat, jnp.zeros((LANES, LANES - GROUP), F32)], axis=1)
            begin = pl.multiple_of(channel * PADDED, 8)
            turned_ref[pl.ds(begin, 8), :] = empty
            turned_ref[pl.ds(pl.multiple_of(begin + 8, 8), LANES), :] = flat
            turned_ref[pl.ds(pl.multiple_of(begin + 136, 8), 8), :] = empty
        return 0

    lax.fori_loop(0, share // 4, turn, 0)

    def lay(step, _):
        for group in range(2):
            taps = [
                turned_ref[
                    pl.ds(group * GROUP * PADDED + step * 3 + 6 + at, GROUP, stride=PADDED), :
                ].astype(BF16)[:, :GROUP]
                for at in range(5)
            ]
            for phase in range(PHASES):
                row = jnp.concatenate(
                    taps[2 - phase : 5 - phase] + [jnp.zeros((GROUP, 16), BF16)], axis=1
                )
                begin = pl.multiple_of((step * PHASES + phase) * GROUP, 16)
                matrix_ref[group, pl.ds(begin, GROUP), :] = row
        return 0

    lax.fori_loop(0, STEPS, lay, 0)
    rows.second()

    for group in range(2):
        frames_ref[group, :64, :] = jnp.zeros((64, LANES), F32)
        frames_ref[group, 64 + MEMBERS * frame_count :, :] = jnp.zeros(
            (frames_ref.shape[1] - 64 - MEMBERS * frame_count, LANES), F32
        )
    for at in range(1, MEMBERS):
        signal_copy(at).wait_recv()

    def place(of, _):
        for at in range(4):
            main = got_ref[of, 64 * at : 64 * at + 64, :]
            side = got_ref[of, frame_count:, rest * at : rest * at + rest]
            second = jnp.concatenate(
                [main[:, GROUP:], side, jnp.zeros((64, LANES - GROUP), BF16)], axis=1
            )
            begin = pl.multiple_of(64 + of * frame_count + 64 * at, 64)
            frames_ref[0, pl.ds(begin, 64), :] = main.astype(F32)
            frames_ref[1, pl.ds(begin, 64), :] = second.astype(F32)
        return 0

    lax.fori_loop(0, MEMBERS, place, 0)

    def widen(row, _):
        for group in range(2):
            parts = [
                frames_ref[group, pl.ds(row * PHASES + phase, 16, stride=BLOCK), :].astype(BF16)[
                    :, :GROUP
                ]
                for phase in range(PHASES)
            ]
            spread_ref[group, row] = jnp.concatenate(
                parts + [jnp.zeros((16, 16), BF16)], axis=1
            )
        return 0

    lax.fori_loop(0, STEPS + 42, widen, 0)

    def back_copy(half, at):
        to = lax.rem(member + at, MEMBERS)
        return remote(
            back_ref.at[half, to],
            returned_ref.at[half, member],
            back_send,
            back_recv,
            half * 7 + at - 1,
            (record, to),
        )

    for half in range(2):
        first = half * 21
        for group in range(2):
            total_ref[...] = jnp.zeros_like(total_ref)

            def convolve(step, _, group=group, first=first):
                window = jnp.concatenate(
                    [
                        spread_ref[group, pl.ds(step * STEP + at + first, SPAN)].reshape(
                            SPAN * 16, 2 * LANES
                        )
                        for at in range(STEP)
                    ],
                    axis=1,
                )
                weights = jnp.concatenate(
                    [
                        matrix_ref[
                            group,
                            pl.ds(pl.multiple_of((step * STEP + at) * 240, 16), 240),
                            :,
                        ]
                        for at in range(STEP)
                    ],
                    axis=1,
                )
                total_ref[...] += lax.dot_general(
                    window, weights, (((1,), (1,)), ((), ())), preferred_element_type=F32
                )
                return 0

            lax.fori_loop(0, STEPS // STEP, convolve, 0)
            bias = tap_bias_ref[:, group * GROUP : (group + 1) * GROUP]
            bias = jnp.concatenate([bias] * PHASES, axis=1)

            def activate(row, _, group=group, first=first, bias=bias):
                value = total_ref[pl.ds(pl.multiple_of(row * 16, 16), 16), :] + bias
                value = value * (1.0 + lax.erf(value * (0.5**0.5))) * 0.5
                for phase in range(PHASES):
                    part = value[:, phase * GROUP : (phase + 1) * GROUP]
                    part = jnp.concatenate([part, jnp.zeros((16, LANES - GROUP), F32)], axis=1)
                    begin = (first + row) * PHASES + phase
                    natural_ref[group, pl.ds(begin, 16, stride=BLOCK), :] = part
                return 0

            lax.fori_loop(0, SPAN, activate, 0)

        def pack(to, _, half=half):
            for side in range(2):
                begin = pl.multiple_of((2 * to + side) * BLOCK + 64 * half, 64)
                one = natural_ref[0, pl.ds(begin, 64), :].astype(BF16)[:, :GROUP]
                two = natural_ref[1, pl.ds(begin, 64), :].astype(BF16)
                back_ref[half, to, 64 * side : 64 * side + 64, :] = jnp.concatenate(
                    [one, two[:, : LANES - GROUP]], axis=1
                )
                tail = two[:, LANES - GROUP : GROUP]
                back_ref[half, to, 128:, 64 * side : 64 * side + 64] = jnp.concatenate(
                    [tail[:32], tail[32:]], axis=1
                )
            return 0

        lax.fori_loop(0, MEMBERS, pack, 0)
        for at in range(1, MEMBERS):
            back_copy(half, at).start()
        returned_ref[half, member] = back_ref[half, member]
        if half == 0:
            rows.third()
            outs.first()
    rows.fourth()
    outs.second()

    for half in range(2):
        for at in range(1, MEMBERS):
            back_copy(half, at).wait_recv()
        for side in range(2):
            for at in range(2):
                begin = side * BLOCK + half * 64 + at * 32
                pieces = []
                for of in range(MEMBERS):
                    pieces.append(
                        returned_ref[half, of, side * 64 + at * 32 : side * 64 + at * 32 + 32, :]
                    )
                    low = rest * (2 * side + at)
                    pieces.append(returned_ref[half, of, 128:, low : low + rest])
                position = jnp.concatenate(pieces, axis=1)
                hidden = signal_ref[begin : begin + 32, :].astype(F32) + position.astype(F32)
                hidden_ref[begin : begin + 32, :] = hidden
                average = jnp.mean(hidden, axis=-1, keepdims=True)
                centered = hidden - average
                variance = jnp.mean(centered * centered, axis=-1, keepdims=True)
                normed_ref[begin : begin + 32, :] = (
                    centered * lax.rsqrt(variance + EPSILON) * gain_ref[...] + shift_ref[...]
                ).astype(BF16)

    rows.done()
    mask = jnp.concatenate(
        [jnp.broadcast_to(unlisted_ref[at : at + 1, :], (BLOCK, 2 * LANES)) for at in range(2)],
        axis=0,
    )

    def head_copy(at):
        to = lax.rem(member + at, MEMBERS)
        return remote(
            slab_ref.at[to], headed_ref.at[member], head_send, head_recv, at - 1, (record, to)
        )

    def project(at):
        head = lax.rem(member + at, MEMBERS)
        weights = jnp.concatenate([rows_ref[2 * head], rows_ref[2 * head + 1]], axis=1)
        slab = jnp.dot(normed_ref[...], weights, preferred_element_type=F32)
        return (slab + bias_ref[pl.ds(head, 1), :] + mask).astype(BF16)

    def project_and_send(at, _):
        slab_ref[lax.rem(member + at, MEMBERS)] = project(at)
        head_copy(at).start()
        return 0

    lax.fori_loop(1, MEMBERS, project_and_send, 0)
    headed_ref[member] = project(0)

    outs.third()
    outs.fourth()
    outs.done()
    for at in range(4):
        pieces = []
        for of in range(MEMBERS):
            pieces.append(output_rows_ref[of, share * at : share * at + share, :])
            pieces.append(
                output_rows_ref[
                    of, heads_width : heads_width + share, rest * at : rest * at + rest
                ]
            )
        output_whole_ref[share * at : share * at + share, :] = jnp.concatenate(pieces, axis=1)

    frames = MEMBERS * frame_count
    same = lax.broadcasted_iota(jnp.int32, (BLOCK, frames), 0) == lax.rem(
        lax.broadcasted_iota(jnp.int32, (BLOCK, frames), 1), BLOCK
    )
    same = same.astype(F32)
    for at in range(GLOBALS):
        chosen_ref[at * BLOCK : (at + 1) * BLOCK, :] = (
            same * globals_ref[at : at + 1, :]
        ).astype(BF16)

    for at in range(1, MEMBERS):
        head_copy(at).wait_recv()

    def arrange(of, _):
        slab = headed_ref[of]
        begin = pl.multiple_of(of * frame_count, 256)
        unlisted = slab[:, 3 * HEAD :]
        queries_ref[pl.ds(begin, frame_count), :] = jnp.concatenate(
            [slab[:, :HEAD], unlisted, 1.0 - unlisted, jnp.zeros((frame_count, 16), BF16)], axis=1
        )
        row = lax.broadcasted_iota(jnp.int32, (frame_count, 16), 0)
        block = 2 * of + jnp.where(row >= BLOCK, 1, 0)
        here = lax.broadcasted_iota(jnp.int32, (frame_count, 16), 1) == block
        keys_ref[pl.ds(begin, frame_count), :] = jnp.concatenate(
            [
                slab[:, HEAD : 2 * HEAD],
                jnp.where(here, -BIG, 0.0).astype(BF16),
                jnp.zeros((frame_count, 32), BF16),
            ],
            axis=1,
        )
        values_ref[pl.ds(begin, frame_count), :] = jnp.concatenate(
            [
                slab[:, 2 * HEAD : 3 * HEAD],
                jnp.ones((frame_count, 16), BF16),
                jnp.zeros((frame_count, 32), BF16),
            ],
            axis=1,
        )
        return 0

    lax.fori_loop(0, MEMBERS, arrange, 0)
    lane = lax.broadcasted_iota(jnp.int32, (BLOCK, LANES), 1)
    picked = jnp.dot(
        chosen_ref[...],
        jnp.concatenate([keys_ref[:frames, :], values_ref[:frames, :]], axis=1),
        preferred_element_type=F32,
    )
    for at in range(GLOBALS):
        rows_at = slice(at * BLOCK, (at + 1) * BLOCK)
        keys_ref[frames + at * BLOCK : frames + (at + 1) * BLOCK, :] = jnp.where(
            lane < HEAD, picked[rows_at, :LANES], marks_ref[at : at + 1, :]
        ).astype(BF16)
        values_ref[frames + at * BLOCK : frames + (at + 1) * BLOCK, :] = picked[
            rows_at, LANES:
        ].astype(BF16)

    factor = (1.0 / math.sqrt(HEAD)) * math.log2(math.e)

    def context_copy(at):
        to = lax.rem(member + at, MEMBERS)
        return remote(
            context_ref.at[to],
            contexts_ref.at[member],
            context_send,
            context_recv,
            at - 1,
            (record, to),
        )

    def attend_tile(at):
        of = lax.rem(member + at, MEMBERS)
        queries = queries_ref[pl.ds(pl.multiple_of(of * frame_count, 256), frame_count), :]
        low = jnp.minimum(jnp.maximum(2 * of - 2, 0), 10)
        window = pl.ds(pl.multiple_of(low * BLOCK, BLOCK), 6 * BLOCK)
        keys = jnp.concatenate([keys_ref[window, :], keys_ref[frames:, :]], axis=0)
        scores = lax.dot_general(
            queries, keys, (((1,), (1,)), ((), ())), preferred_element_type=F32
        )
        peak = jnp.max(scores, axis=1, keepdims=True)
        weights = jnp.exp2(scores * factor - peak * factor).astype(BF16)
        values = jnp.concatenate([values_ref[window, :], values_ref[frames:, :]], axis=0)
        summed = jnp.dot(weights, values, preferred_element_type=F32)
        return (summed / summed[:, HEAD : HEAD + 1]).astype(BF16)

    def attend_and_send(at, _):
        context_ref[lax.rem(member + at, MEMBERS)] = attend_tile(at)
        context_copy(at).start()
        return 0

    lax.fori_loop(1, MEMBERS, attend_and_send, 0)
    contexts_ref[member] = attend_tile(0)

    for at in range(1, MEMBERS):
        context_copy(at).wait_recv()
    context = jnp.concatenate([contexts_ref[of][:, :HEAD] for of in range(HEADS)], axis=1)
    projected = jnp.dot(context, output_whole_ref[...], preferred_element_type=F32)
    out_ref[...] = (hidden_ref[...] + projected + output_bias_ref[...]).astype(BF16)

    for at in range(1, MEMBERS):
        signal_copy(at).wait_send()
        back_copy(0, at).wait_send()
        back_copy(1, at).wait_send()
        head_copy(at).wait_send()
        context_copy(at).wait_send()
    rows.sent()
    outs.sent()


def by_heads(
    signal,
    position_kernel,
    position_bias,
    layer_gain,
    layer_shift,
    query_weight,
    query_bias,
    key_weight,
    value_weight,
    value_bias,
    output_weight,
    output_bias,
    key_blocks,
    global_blocks,
):
    frame_count, width = signal.shape
    frames = MEMBERS * frame_count
    share = 2 * GROUP
    biases = jnp.stack((query_bias, jnp.zeros_like(query_bias), value_bias))
    biases = biases.reshape(3, HEADS, HEAD).transpose(1, 0, 2).reshape(HEADS, 3 * HEAD)
    biases = jnp.pad(biases, ((0, 0), (0, 16)))
    blocks = frames // BLOCK
    every = jnp.arange(blocks)
    unlisted = 1.0 - jnp.any(key_blocks[:, :, None] == every, axis=1).astype(F32)
    unlisted = jnp.pad(unlisted, ((0, 0), (3 * HEAD, 0)))
    chosen = (global_blocks[:, None] == every).astype(F32)
    marks = jnp.pad(chosen * -BIG, ((0, 0), (HEAD + 16, LANES - HEAD - 32)))
    chosen = jnp.repeat(chosen, BLOCK, axis=1)
    vmem = pl.BlockSpec(memory_space=pltpu.VMEM)
    dma = pltpu.SemaphoreType.DMA
    return pl.pallas_call(
        whole_kernel,
        out_shape=jax.ShapeDtypeStruct((frame_count, width), BF16),
        in_specs=[vmem] * 4 + [pl.BlockSpec(memory_space=pl.ANY)] + [vmem] * 9,
        out_specs=vmem,
        scratch_shapes=[
            pltpu.VMEM((share, GROUP, LANES), BF16),
            pltpu.VMEM((share * PADDED, LANES), F32),
            pltpu.VMEM((2, STEPS * PHASES * GROUP, 2 * LANES), BF16),
            pltpu.VMEM((MEMBERS, frame_count + 64, LANES), BF16),
            pltpu.VMEM((MEMBERS, frame_count + 64, LANES), BF16),
            pltpu.VMEM((2, frames + 136, LANES), F32),
            pltpu.VMEM((2, STEPS + 42, 16, 2 * LANES), BF16),
            pltpu.VMEM((SPAN * 16, PHASES * GROUP), F32),
            pltpu.VMEM((2, frames + 16, LANES), F32),
            pltpu.VMEM((2, MEMBERS, 160, LANES), BF16),
            pltpu.VMEM((2, MEMBERS, 160, LANES), BF16),
            pltpu.VMEM((frame_count, width), F32),
            pltpu.VMEM((frame_count, width), BF16),
            pltpu.VMEM((2 * HEADS, width, LANES), BF16),
            pltpu.VMEM((MEMBERS, 832, LANES), BF16),
            pltpu.VMEM((HEADS * HEAD, width), BF16),
            pltpu.VMEM((MEMBERS, frame_count, 2 * LANES), BF16),
            pltpu.VMEM((MEMBERS, frame_count, 2 * LANES), BF16),
            pltpu.VMEM((frames, LANES), BF16),
            pltpu.VMEM((frames + GLOBALS * BLOCK, LANES), BF16),
            pltpu.VMEM((frames + GLOBALS * BLOCK, LANES), BF16),
            pltpu.VMEM((GLOBALS * BLOCK, frames), BF16),
            pltpu.VMEM((MEMBERS, frame_count, LANES), BF16),
            pltpu.VMEM((MEMBERS, frame_count, LANES), BF16),
            dma,
            dma((7,)),
            dma((7,)),
            dma((14,)),
            dma((14,)),
            dma((28,)),
            dma((28,)),
            dma((28,)),
            dma((28,)),
            dma((7,)),
            dma((7,)),
            dma((7,)),
            dma((7,)),
        ],
        compiler_params=pltpu.CompilerParams(
            collective_id=0, has_side_effects=True, vmem_limit_bytes=60 * 1024 * 1024
        ),
    )(
        unlisted,
        chosen,
        marks,
        signal,
        position_kernel,
        position_bias.reshape(1, -1),
        layer_gain.reshape(1, -1),
        layer_shift.reshape(1, -1),
        query_weight,
        key_weight,
        value_weight,
        biases,
        output_weight,
        output_bias.reshape(1, -1),
    )


def body(*operands):
    share, width, taps = operands[1].shape
    fits = lax.axis_size("tm") == MEMBERS and lax.axis_size("rec") == QUARTERS
    fits = fits and (share, width, taps) == (2 * GROUP, GROUP, LANES)
    fits = fits and operands[0].shape[0] == 2 * BLOCK
    return (by_heads if fits else general)(*operands)


def solution(mesh):
    placed = (
        P(("rec", "tm"), None),
        P("tm", None, None),
        P("tm"),
        P(),
        P(),
        P("tm", None),
        P(),
        P("tm", None),
        P("tm", None),
        P(),
        P(None, "tm"),
        P(),
        P(("rec", "tm"), None),
        P("rec"),
    )
    return jax.shard_map(
        body, mesh=mesh, in_specs=placed, out_specs=P(("rec", "tm"), None), check_vma=False
    )
```

```python
import math

import jax
import jax.numpy as jnp
import numpy as np
from jax import lax
from jax.experimental import pallas as pl
from jax.experimental.pallas import tpu as pltpu
from jax.sharding import PartitionSpec as P

HEAD = 80
HEADS = 8
BLOCK = 128
GLOBALS = 4


EPSILON = 1e-05


def attend(queries, key_rows, value_rows, allowed):
    block_count, row_count, heads_width = queries.shape
    query_heads = queries.reshape(block_count, row_count, HEADS, HEAD)
    key_heads = key_rows.reshape(block_count, key_rows.shape[1], HEADS, HEAD)
    value_heads = value_rows.reshape(block_count, value_rows.shape[1], HEADS, HEAD)
    scores = jnp.einsum(
        "bqhe,bkhe->bhqk", query_heads, key_heads, preferred_element_type=jnp.float32
    ) * (1.0 / math.sqrt(HEAD))
    scores = jnp.where(allowed[:, None, None, :], scores, -jnp.inf)
    row_max = jnp.max(scores, axis=-1, keepdims=True)
    weights = jnp.exp(scores - row_max)
    row_total = jnp.sum(weights, axis=-1)
    probability = weights.astype(jnp.bfloat16)
    context_sum = jnp.einsum(
        "bhqk,bkhe->bqhe", probability, value_heads, preferred_element_type=jnp.float32
    )
    context = context_sum / jnp.transpose(row_total, (0, 2, 1))[..., None]
    return context.reshape(block_count, row_count, heads_width).astype(jnp.bfloat16)


def general(
    signal,
    position_kernel,
    position_bias,
    layer_gain,
    layer_shift,
    query_weight,
    query_bias,
    key_weight,
    value_weight,
    value_bias,
    output_weight,
    output_bias,
    key_blocks,
    global_blocks,
):
    devices = lax.axis_size("tm")
    frame_count, model_width = signal.shape
    channel_share, group_width, kernel_taps = position_kernel.shape
    inner_width = max(channel_share, group_width)
    folded = signal.T
    if channel_share >= group_width:
        outgoing = folded.reshape(devices, channel_share, frame_count)
    else:
        start_groups = np.arange(devices) * channel_share // group_width
        grouped = folded.reshape(model_width // group_width, group_width, frame_count)
        outgoing = jnp.stack(
            [grouped[at * channel_share // group_width] for at in range(devices)]
        )
    incoming = lax.all_to_all(outgoing, "tm", split_axis=0, concat_axis=2, tiled=True)
    outputs = channel_share if channel_share < group_width else group_width
    spread = jnp.pad(
        incoming.reshape(inner_width // group_width, group_width, -1),
        ((0, 0), (0, 0), (kernel_taps // 2, kernel_taps // 2 - 1)),
    )
    frames = incoming.shape[-1]
    by_tap = position_kernel.reshape(-1, outputs, group_width, kernel_taps).transpose(3, 0, 1, 2)

    def tap(at, total):
        window = lax.dynamic_slice_in_dim(spread, at, frames, axis=2)
        return total + jnp.einsum(
            "goi,git->got", by_tap[at], window, preferred_element_type=jnp.float32
        )

    response = lax.fori_loop(
        0, kernel_taps, tap, jnp.zeros((spread.shape[0], outputs, frames), jnp.float32)
    ).reshape(channel_share, frames)
    position = jax.nn.gelu(response + position_bias[:, None], approximate=False).astype(
        jnp.bfloat16
    )
    returned = lax.all_to_all(position, "tm", split_axis=1, concat_axis=0, tiled=True)
    hidden = signal.astype(jnp.float32) + returned.T.astype(jnp.float32)
    average = jnp.mean(hidden, axis=-1, keepdims=True)
    centered = hidden - average
    variance = jnp.mean(centered * centered, axis=-1, keepdims=True)
    normed = (centered * lax.rsqrt(variance + EPSILON) * layer_gain + layer_shift).astype(
        jnp.bfloat16
    )
    heads_width = query_weight.shape[1]
    zero_sums = jnp.zeros((frame_count, heads_width), jnp.float32)
    totals = (zero_sums, zero_sums, zero_sums)
    pieces = (
        lax.all_gather(query_weight, "tm", axis=0, tiled=True),
        lax.all_gather(key_weight, "tm", axis=0, tiled=True),
        lax.all_gather(value_weight, "tm", axis=0, tiled=True),
    )
    columns = lax.slice_in_dim(normed, 0, pieces[0].shape[0], axis=1)
    query_sum, key_sum, value_sum = tuple(
        (
            running + jnp.dot(columns, weight_rows, preferred_element_type=jnp.float32)
            for running, weight_rows in zip(totals, pieces)
        )
    )
    queries = (query_sum + query_bias).astype(jnp.bfloat16)
    key_part = key_sum.astype(jnp.bfloat16)
    value_part = (value_sum + value_bias).astype(jnp.bfloat16)
    key_value = jnp.stack((key_part, value_part), axis=1)
    per_device = frame_count // BLOCK
    repeated = jnp.any(global_blocks[None, :, None] == key_blocks[:, None, :], axis=-1)
    whole = lax.all_gather(key_value, "tm", axis=0, tiled=True)
    block_ids = jnp.concatenate(
        [key_blocks, jnp.broadcast_to(global_blocks[None, :], (per_device, GLOBALS))], axis=1
    )
    allowed = jnp.concatenate([key_blocks >= 0, jnp.logical_not(repeated)], axis=1)
    table = whole.reshape(-1, BLOCK, 2, heads_width)
    chosen = jnp.maximum(block_ids, 0)
    candidates = jnp.stack(
        [
            jnp.stack(
                [
                    lax.dynamic_index_in_dim(table, chosen[row, at], 0, keepdims=False)
                    for at in range(chosen.shape[1])
                ]
            )
            for row in range(per_device)
        ]
    )
    key_rows = candidates[:, :, :, 0].reshape(per_device, -1, heads_width)
    value_rows = candidates[:, :, :, 1].reshape(per_device, -1, heads_width)
    allowed_rows = jnp.repeat(allowed, BLOCK, axis=1)
    context = attend(
        queries.reshape(per_device, BLOCK, heads_width), key_rows, value_rows, allowed_rows
    ).reshape(frame_count, heads_width)
    projected = jnp.dot(
        context,
        lax.all_gather(output_weight, "tm", axis=1, tiled=True),
        preferred_element_type=jnp.float32,
    )
    return (hidden + projected + output_bias).astype(jnp.bfloat16)


PHASES = 3
GROUP = 80
MEMBERS = 8
QUARTERS = 4
LANES = 128
STEP = 4
STEPS = 44
SPAN = 22
PADDED = 145
MESH = pl.DeviceIdType.MESH
BIG = 1e30
F32 = jnp.float32
BF16 = jnp.bfloat16


def flip(member, bits):
    low = bits % 4
    if low == 1:
        turned = member + 1 - 2 * lax.rem(member, 2)
    elif low == 2:
        turned = member + 2 - 4 * lax.rem(lax.div(member, 2), 2)
    elif low == 3:
        turned = 4 * lax.div(member, 4) + 3 - lax.rem(member, 4)
    else:
        turned = member
    return lax.rem(turned + 4, MEMBERS) if bits >= 4 else turned


def loop(begin, end, body, unroll):
    turns = (end - begin) // unroll

    def turn(step, _):
        for at in range(unroll):
            body(begin + step * unroll + at)
        return 0

    if turns > 1:
        lax.fori_loop(0, turns, turn, 0)
    else:
        turns = 0
    for at in range(begin + turns * unroll, end):
        body(at)


def row_of(ref):
    return ref[...].reshape(1, -1)


def remote(source, target, sends, receives, at, device):
    return pltpu.make_async_remote_copy(
        src_ref=source,
        dst_ref=target,
        send_sem=sends.at[at],
        recv_sem=receives.at[at],
        device_id=device,
        device_id_type=MESH,
    )


class Spread:
    def __init__(self, piece, record, member, sends, receives):
        self.piece, self.record, self.member = piece, record, member
        self.sends, self.receives = sends, receives
        self.across = lax.rem(record + 2, QUARTERS)
        self.beside = record + 1 - 2 * lax.rem(record, 2)

    def copy(self, at, share, quarter, device):
        ref = self.piece(share, quarter)
        return remote(ref, ref, self.sends, self.receives, at, device)

    def plane(self, at):
        bits = at + 1
        if bits <= 4:
            return self.copy(at, self.member, self.record, (self.record, flip(self.member, bits)))
        share = flip(self.member, 4)
        return self.copy(at, share, self.record, (self.record, flip(self.member, bits - 4)))

    def other(self, at):
        return self.copy(7 + at, flip(self.member, at + 1), self.record, (self.across, self.member))

    def core(self, at):
        return self.copy(14 + at, flip(self.member, at + 1), self.record, (self.beside, self.member))

    def last(self, at):
        return self.copy(21 + at, flip(self.member, at + 1), self.across, (self.beside, self.member))

    def first(self):
        for at in (3, 0, 1, 2):
            self.plane(at).start()

    def second(self):
        self.plane(3).wait_recv()
        for at in (4, 5, 6):
            self.plane(at).start()
        self.other(3).start()
        self.core(3).start()
        for at in (0, 1, 2):
            self.plane(at).wait_recv()
            self.other(at).start()
            self.core(at).start()

    def third(self):
        for at in (4, 5, 6):
            self.plane(at).wait_recv()
            self.other(at).start()
            self.core(at).start()

    def fourth(self):
        for at in (3, 0, 1, 2, 4, 5, 6):
            self.other(at).wait_recv()
            self.last(at).start()

    def done(self):
        for at in range(7):
            self.core(at).wait_recv()
            self.last(at).wait_recv()

    def sent(self):
        for at in range(7):
            for copy in (self.plane(at), self.other(at), self.core(at), self.last(at)):
                copy.wait_send()


def whole_kernel(
    blocks_ref,
    globals_ref,
    signal_ref,
    taps_hbm,
    tap_bias_ref,
    gain_ref,
    shift_ref,
    query_ref,
    key_ref,
    value_ref,
    query_bias_ref,
    value_bias_ref,
    output_ref,
    output_bias_ref,
    out_ref,
    taps_ref,
    turned_ref,
    matrix_ref,
    send_ref,
    got_ref,
    frames_ref,
    spread_ref,
    total_ref,
    natural_ref,
    back_ref,
    returned_ref,
    hidden_ref,
    normed_ref,
    rows_ref,
    output_rows_ref,
    bias_ref,
    slab_ref,
    headed_ref,
    queries_ref,
    keys_ref,
    values_ref,
    chosen_ref,
    context_ref,
    contexts_ref,
    load_sem,
    signal_send,
    signal_recv,
    back_send,
    back_recv,
    rows_send,
    rows_recv,
    outs_send,
    outs_recv,
    head_send,
    head_recv,
    context_send,
    context_recv,
):
    record, member = lax.axis_index("rec"), lax.axis_index("tm")
    load = pltpu.make_async_copy(taps_hbm, taps_ref, load_sem)
    load.start()

    barrier = pltpu.get_barrier_semaphore()
    across = lax.rem(record + 2, QUARTERS)
    beside = record + 1 - 2 * lax.rem(record, 2)
    peers = [(record, lax.rem(member + at, MEMBERS)) for at in range(1, MEMBERS)]
    for peer in peers + [(across, member), (beside, member)]:
        pl.semaphore_signal(barrier, inc=1, device_id=peer, device_id_type=MESH)

    frame_count = signal_ref.shape[0]
    share = 2 * GROUP
    rest = share - LANES
    for to in range(MEMBERS):
        begin = to * share
        send_ref[to, :frame_count, :] = signal_ref[:, begin : begin + LANES]
        send_ref[to, frame_count:, :] = jnp.concatenate(
            [
                signal_ref[64 * at : 64 * at + 64, begin + LANES : begin + share]
                for at in range(4)
            ],
            axis=1,
        )
    pl.semaphore_wait(barrier, 9)

    def signal_copy(at):
        to = lax.rem(member + at, MEMBERS)
        return remote(
            send_ref.at[to], got_ref.at[member], signal_send, signal_recv, at - 1, (record, to)
        )

    for at in range(1, MEMBERS):
        signal_copy(at).start()
    got_ref[member] = send_ref[member]

    mine = pl.ds(pl.multiple_of(member * share, 32), share)
    for head in range(HEADS):
        columns = slice(head * HEAD, (head + 1) * HEAD)
        joined = jnp.concatenate(
            [
                query_ref[:, columns],
                key_ref[:, columns],
                value_ref[:, columns],
                jnp.zeros((share, 16), BF16),
            ],
            axis=1,
        )
        rows_ref[2 * head, mine, :] = joined[:, :LANES]
        rows_ref[2 * head + 1, mine, :] = joined[:, LANES:]
    heads_width = HEADS * HEAD
    for at in range(heads_width // LANES):
        output_rows_ref[member, share * at : share * at + share, :] = output_ref[
            :, at * LANES : (at + 1) * LANES
        ]
    output_rows_ref[member, 5 * share :, :] = jnp.zeros((32, LANES), BF16)
    empty = jnp.zeros((1, HEAD), F32)
    for head in range(HEADS):
        columns = slice(head * HEAD, (head + 1) * HEAD)
        bias_ref[head : head + 1, :] = jnp.concatenate(
            [
                row_of(query_bias_ref)[:, columns],
                empty,
                row_of(value_bias_ref)[:, columns],
                empty[:, :16],
            ],
            axis=1,
        )

    def rows_piece(of, quarter):
        return rows_ref.at[
            pl.ds(quarter * 4, 4), pl.ds(pl.multiple_of(of * share, 32), share), :
        ]

    def output_piece(of, quarter):
        return output_rows_ref.at[of, pl.ds(pl.multiple_of(quarter * 208, 16), 208), :]

    rows = Spread(rows_piece, record, member, rows_send, rows_recv)
    outs = Spread(output_piece, record, member, outs_send, outs_recv)
    rows.first()

    load.wait()
    empty = jnp.zeros((8, LANES), F32)

    def turn(channel):
        begin = channel * PADDED
        turned_ref[pl.ds(begin, 8), :] = empty
        turned_ref[pl.ds(begin + 136, 8), :] = empty
        turned_ref[pl.ds(begin + 8, LANES), :GROUP] = jnp.transpose(taps_ref[channel]).astype(F32)

    loop(0, share, turn, 16)

    def lay(step):
        for group in range(2):
            taps = [
                turned_ref[
                    pl.ds(group * GROUP * PADDED + step * 3 + 6 + at, GROUP, stride=PADDED), :
                ].astype(BF16)[:, :GROUP]
                for at in range(5)
            ]
            for phase in range(PHASES):
                row = jnp.concatenate(
                    taps[2 - phase : 5 - phase] + [jnp.zeros((GROUP, 16), BF16)], axis=1
                )
                begin = pl.multiple_of((step * PHASES + phase) * GROUP, 16)
                matrix_ref[group, pl.ds(begin, GROUP), :] = row

    loop(0, STEPS, lay, 4)
    rows.second()

    frames = MEMBERS * frame_count
    tail = 64 + frames + (64 + frames) // BLOCK
    for group in range(2):
        frames_ref[group, :64, :] = jnp.zeros((64, LANES), F32)
        frames_ref[group, tail:, :] = jnp.zeros((frames_ref.shape[1] - tail, LANES), F32)
    for at in range(1, MEMBERS):
        signal_copy(at).wait_recv()

    def place(of):
        for at in range(4):
            main = got_ref[of, 64 * at : 64 * at + 64, :]
            side = got_ref[of, frame_count:, rest * at : rest * at + rest]
            second = jnp.concatenate(
                [main[:, GROUP:], side, jnp.zeros((64, LANES - GROUP), BF16)], axis=1
            )
            begin = of * (frame_count + 2) + 64 * (at + 1) + (at + 1) // 2
            frames_ref[0, pl.ds(begin, 64), :] = main.astype(F32)
            frames_ref[1, pl.ds(begin, 64), :] = second.astype(F32)

    loop(0, MEMBERS, place, 2)

    def widen(row):
        for group in range(2):
            parts = []
            for phase in range(PHASES):
                at = row * PHASES + phase
                part = frames_ref[group, pl.ds(at + at // BLOCK, 16, stride=BLOCK + 1), :]
                parts.append(part.astype(BF16)[:, :GROUP])
            spread_ref[group, row] = jnp.concatenate(
                parts + [jnp.zeros((16, 16), BF16)], axis=1
            )

    loop(0, STEPS + 42, widen, 8)

    def back_copy(half, at):
        to = lax.rem(member + at, MEMBERS)
        return remote(
            back_ref.at[half, to],
            returned_ref.at[half, member],
            back_send,
            back_recv,
            half * 7 + at - 1,
            (record, to),
        )

    for half in range(2):
        first = half * 21
        for group in range(2):
            window = jnp.concatenate(
                [
                    spread_ref[group, step + first : step + first + SPAN].reshape(
                        SPAN * 16, 2 * LANES
                    )
                    for step in range(STEPS)
                ],
                axis=1,
            )
            weights = jnp.concatenate(
                [matrix_ref[group, step * 240 : step * 240 + 240, :] for step in range(STEPS)],
                axis=1,
            )
            total_ref[...] = lax.dot_general(
                window, weights, (((1,), (1,)), ((), ())), preferred_element_type=F32
            )
            bias = row_of(tap_bias_ref)[:, group * GROUP : (group + 1) * GROUP]
            bias = jnp.concatenate([bias] * PHASES, axis=1)

            def activate(row, group=group, first=first, bias=bias):
                value = total_ref[pl.ds(pl.multiple_of(row * 16, 16), 16), :] + bias
                value = value * (1.0 + lax.erf(value * (0.5**0.5))) * 0.5
                for phase in range(PHASES):
                    part = value[:, phase * GROUP : (phase + 1) * GROUP]
                    part = jnp.concatenate([part, jnp.zeros((16, LANES - GROUP), F32)], axis=1)
                    begin = (first + row) * PHASES + phase
                    begin = begin + begin // BLOCK
                    natural_ref[group, pl.ds(begin, 16, stride=BLOCK + 1), :] = part

            loop(0, SPAN, activate, 11)

        def pack(to, half=half):
            for side in range(2):
                begin = (2 * to + side) * (BLOCK + 1) + 64 * half
                one = natural_ref[0, pl.ds(begin, 64), :].astype(BF16)[:, :GROUP]
                two = natural_ref[1, pl.ds(begin, 64), :].astype(BF16)
                back_ref[half, to, 64 * side : 64 * side + 64, :] = jnp.concatenate(
                    [one, two[:, : LANES - GROUP]], axis=1
                )
                tail = two[:, LANES - GROUP : GROUP]
                back_ref[half, to, 128:, 64 * side : 64 * side + 64] = jnp.concatenate(
                    [tail[:32], tail[32:]], axis=1
                )

        loop(0, MEMBERS, pack, 4)
        for at in range(1, MEMBERS):
            back_copy(half, at).start()
        returned_ref[half, member] = back_ref[half, member]
        if half == 0:
            rows.third()
            outs.first()
    rows.fourth()
    outs.second()

    for half in range(2):
        for at in range(1, MEMBERS):
            back_copy(half, at).wait_recv()
        for side in range(2):
            for at in range(2):
                begin = side * BLOCK + half * 64 + at * 32
                pieces = []
                for of in range(MEMBERS):
                    pieces.append(
                        returned_ref[half, of, side * 64 + at * 32 : side * 64 + at * 32 + 32, :]
                    )
                    low = rest * (2 * side + at)
                    pieces.append(returned_ref[half, of, 128:, low : low + rest])
                position = jnp.concatenate(pieces, axis=1)
                hidden = signal_ref[begin : begin + 32, :].astype(F32) + position.astype(F32)
                hidden_ref[begin : begin + 32, :] = hidden
                average = jnp.mean(hidden, axis=-1, keepdims=True)
                centered = hidden - average
                variance = jnp.mean(centered * centered, axis=-1, keepdims=True)
                normed_ref[begin : begin + 32, :] = (
                    centered * lax.rsqrt(variance + EPSILON) * row_of(gain_ref) + row_of(shift_ref)
                ).astype(BF16)

    rows.done()
    lane = lax.broadcasted_iota(jnp.int32, (BLOCK, 2 * LANES), 1) - 3 * HEAD
    masks = []
    for block in range(2):
        unlisted = jnp.where(lane >= 0, 1.0, 0.0)
        for at in range(blocks_ref.shape[1]):
            unlisted = jnp.where(lane == jnp.where(lane >= 0, blocks_ref[block, at], -1000), 0.0, unlisted)
        masks.append(unlisted)
    mask = jnp.concatenate(masks, axis=0)

    def head_copy(at):
        to = lax.rem(member + at, MEMBERS)
        return remote(
            slab_ref.at[to], headed_ref.at[member], head_send, head_recv, at - 1, (record, to)
        )

    def project(at):
        head = lax.rem(member + at, MEMBERS)
        weights = jnp.concatenate([rows_ref[2 * head], rows_ref[2 * head + 1]], axis=1)
        slab = jnp.dot(normed_ref[...], weights, preferred_element_type=F32)
        return (slab + bias_ref[pl.ds(head, 1), :] + mask).astype(BF16)

    def project_and_send(at):
        slab_ref[lax.rem(member + at, MEMBERS)] = project(at)
        head_copy(at).start()

    for at in range(1, MEMBERS):
        project_and_send(at)
    headed_ref[member] = project(0)

    outs.third()
    outs.fourth()
    outs.done()
    place_row = lax.broadcasted_iota(jnp.int32, (BLOCK, frames), 0)
    place_column = lax.broadcasted_iota(jnp.int32, (BLOCK, frames), 1)
    for at in range(GLOBALS):
        chosen_ref[at * BLOCK : (at + 1) * BLOCK, :] = jnp.where(
            place_row + globals_ref[at] * BLOCK == place_column, 1.0, 0.0
        ).astype(BF16)

    for at in range(1, MEMBERS):
        head_copy(at).wait_recv()

    def arrange(of):
        slab = headed_ref[of]
        begin = pl.multiple_of(of * frame_count, 256)
        unlisted = slab[:, 3 * HEAD :]
        queries_ref[pl.ds(begin, frame_count), :] = jnp.concatenate(
            [slab[:, :HEAD], unlisted, 1.0 - unlisted, jnp.zeros((frame_count, 16), BF16)], axis=1
        )
        row = lax.broadcasted_iota(jnp.int32, (frame_count, 16), 0)
        block = 2 * of + jnp.where(row >= BLOCK, 1, 0)
        here = lax.broadcasted_iota(jnp.int32, (frame_count, 16), 1) == block
        keys_ref[pl.ds(begin, frame_count), :] = jnp.concatenate(
            [
                slab[:, HEAD : 2 * HEAD],
                jnp.where(here, -BIG, 0.0).astype(BF16),
                jnp.zeros((frame_count, 32), BF16),
            ],
            axis=1,
        )
        values_ref[pl.ds(begin, frame_count), :] = jnp.concatenate(
            [
                slab[:, 2 * HEAD : 3 * HEAD],
                jnp.ones((frame_count, 16), BF16),
                jnp.zeros((frame_count, 32), BF16),
            ],
            axis=1,
        )

    loop(0, MEMBERS, arrange, 4)
    lane = lax.broadcasted_iota(jnp.int32, (BLOCK, LANES), 1)
    picked = jnp.dot(
        chosen_ref[...],
        jnp.concatenate([keys_ref[:frames, :], values_ref[:frames, :]], axis=1),
        preferred_element_type=F32,
    )
    for at in range(GLOBALS):
        rows_at = slice(at * BLOCK, (at + 1) * BLOCK)
        keys_ref[frames + at * BLOCK : frames + (at + 1) * BLOCK, :] = jnp.where(
            lane < HEAD,
            picked[rows_at, :LANES],
            jnp.where(lane == HEAD + 16 + globals_ref[at], -BIG, 0.0),
        ).astype(BF16)
        values_ref[frames + at * BLOCK : frames + (at + 1) * BLOCK, :] = picked[
            rows_at, LANES:
        ].astype(BF16)

    factor = (1.0 / math.sqrt(HEAD)) * math.log2(math.e)

    def context_copy(at):
        to = lax.rem(member + at, MEMBERS)
        return remote(
            context_ref.at[to],
            contexts_ref.at[member],
            context_send,
            context_recv,
            at - 1,
            (record, to),
        )

    def attend_tile(at):
        of = lax.rem(member + at, MEMBERS)
        queries = queries_ref[pl.ds(pl.multiple_of(of * frame_count, 256), frame_count), :]
        low = jnp.minimum(jnp.maximum(2 * of - 2, 0), 10)
        window = pl.ds(pl.multiple_of(low * BLOCK, BLOCK), 6 * BLOCK)
        keys = jnp.concatenate([keys_ref[window, :], keys_ref[frames:, :]], axis=0)
        scores = lax.dot_general(
            queries, keys, (((1,), (1,)), ((), ())), preferred_element_type=F32
        )
        peak = jnp.max(scores, axis=1, keepdims=True)
        weights = jnp.exp2(scores * factor - peak * factor).astype(BF16)
        values = jnp.concatenate([values_ref[window, :], values_ref[frames:, :]], axis=0)
        summed = jnp.dot(weights, values, preferred_element_type=F32)
        return (summed / summed[:, HEAD : HEAD + 1]).astype(BF16)

    def attend_and_send(at):
        context_ref[lax.rem(member + at, MEMBERS)] = attend_tile(at)
        context_copy(at).start()

    for at in range(1, MEMBERS):
        attend_and_send(at)
    contexts_ref[member] = attend_tile(0)

    for at in range(1, MEMBERS):
        context_copy(at).wait_recv()
    context = jnp.concatenate([contexts_ref[of][:, :HEAD] for of in range(HEADS)], axis=1)
    columns = jnp.concatenate(
        [
            jnp.concatenate(
                [output_rows_ref[of, share * at : share * at + share, :] for at in range(5)], axis=1
            )
            for of in range(MEMBERS)
        ],
        axis=0,
    )
    projected = lax.dot_general(
        context, columns, (((1,), (1,)), ((), ())), preferred_element_type=F32
    )
    out_ref[...] = (hidden_ref[...] + projected + row_of(output_bias_ref)).astype(BF16)

    for at in range(1, MEMBERS):
        signal_copy(at).wait_send()
        back_copy(0, at).wait_send()
        back_copy(1, at).wait_send()
        head_copy(at).wait_send()
        context_copy(at).wait_send()
    rows.sent()
    outs.sent()


def by_heads(
    signal,
    position_kernel,
    position_bias,
    layer_gain,
    layer_shift,
    query_weight,
    query_bias,
    key_weight,
    value_weight,
    value_bias,
    output_weight,
    output_bias,
    key_blocks,
    global_blocks,
):
    frame_count, width = signal.shape
    frames = MEMBERS * frame_count
    share = 2 * GROUP
    vmem = pl.BlockSpec(memory_space=pltpu.VMEM)
    smem = pl.BlockSpec(memory_space=pltpu.SMEM)
    dma = pltpu.SemaphoreType.DMA
    return pl.pallas_call(
        whole_kernel,
        out_shape=jax.ShapeDtypeStruct((frame_count, width), BF16),
        in_specs=[smem, smem, vmem, pl.BlockSpec(memory_space=pl.ANY)] + [vmem] * 10,
        out_specs=vmem,
        scratch_shapes=[
            pltpu.VMEM((share, GROUP, LANES), BF16),
            pltpu.VMEM((share * PADDED, LANES), F32),
            pltpu.VMEM((2, STEPS * PHASES * GROUP, 2 * LANES), BF16),
            pltpu.VMEM((MEMBERS, frame_count + 64, LANES), BF16),
            pltpu.VMEM((MEMBERS, frame_count + 64, LANES), BF16),
            pltpu.VMEM((2, frames + 160, LANES), F32),
            pltpu.VMEM((2, STEPS + 42, 16, 2 * LANES), BF16),
            pltpu.VMEM((SPAN * 16, PHASES * GROUP), F32),
            pltpu.VMEM((2, frames + 32, LANES), F32),
            pltpu.VMEM((2, MEMBERS, 160, LANES), BF16),
            pltpu.VMEM((2, MEMBERS, 160, LANES), BF16),
            pltpu.VMEM((frame_count, width), F32),
            pltpu.VMEM((frame_count, width), BF16),
            pltpu.VMEM((2 * HEADS, width, LANES), BF16),
            pltpu.VMEM((MEMBERS, 832, LANES), BF16),
            pltpu.VMEM((HEADS, 2 * LANES), F32),
            pltpu.VMEM((MEMBERS, frame_count, 2 * LANES), BF16),
            pltpu.VMEM((MEMBERS, frame_count, 2 * LANES), BF16),
            pltpu.VMEM((frames, LANES), BF16),
            pltpu.VMEM((frames + GLOBALS * BLOCK, LANES), BF16),
            pltpu.VMEM((frames + GLOBALS * BLOCK, LANES), BF16),
            pltpu.VMEM((GLOBALS * BLOCK, frames), BF16),
            pltpu.VMEM((MEMBERS, frame_count, LANES), BF16),
            pltpu.VMEM((MEMBERS, frame_count, LANES), BF16),
            dma,
            dma((7,)),
            dma((7,)),
            dma((14,)),
            dma((14,)),
            dma((28,)),
            dma((28,)),
            dma((28,)),
            dma((28,)),
            dma((7,)),
            dma((7,)),
            dma((7,)),
            dma((7,)),
        ],
        compiler_params=pltpu.CompilerParams(
            collective_id=0, has_side_effects=True, vmem_limit_bytes=60 * 1024 * 1024
        ),
    )(
        key_blocks,
        global_blocks,
        signal,
        position_kernel,
        position_bias,
        layer_gain,
        layer_shift,
        query_weight,
        key_weight,
        value_weight,
        query_bias,
        value_bias,
        output_weight.T,
        output_bias,
    )


def body(*operands):
    share, width, taps = operands[1].shape
    fits = lax.axis_size("tm") == MEMBERS and lax.axis_size("rec") == QUARTERS
    fits = fits and (share, width, taps) == (2 * GROUP, GROUP, LANES)
    fits = fits and operands[0].shape[0] == 2 * BLOCK
    return (by_heads if fits else general)(*operands)


def solution(mesh):
    placed = (
        P(("rec", "tm"), None),
        P("tm", None, None),
        P("tm"),
        P(),
        P(),
        P("tm", None),
        P(),
        P("tm", None),
        P("tm", None),
        P(),
        P(None, "tm"),
        P(),
        P(("rec", "tm"), None),
        P("rec"),
    )
    return jax.shard_map(
        body, mesh=mesh, in_specs=placed, out_specs=P(("rec", "tm"), None), check_vma=False
    )
```

```python
import math

import jax
import jax.numpy as jnp
import numpy as np
from jax import lax
from jax.experimental import pallas as pl
from jax.experimental.pallas import tpu as pltpu
from jax.sharding import PartitionSpec as P

HEAD = 80
HEADS = 8
BLOCK = 128
GLOBALS = 4


EPSILON = 1e-05


def attend(queries, key_rows, value_rows, allowed):
    block_count, row_count, heads_width = queries.shape
    query_heads = queries.reshape(block_count, row_count, HEADS, HEAD)
    key_heads = key_rows.reshape(block_count, key_rows.shape[1], HEADS, HEAD)
    value_heads = value_rows.reshape(block_count, value_rows.shape[1], HEADS, HEAD)
    scores = jnp.einsum(
        "bqhe,bkhe->bhqk", query_heads, key_heads, preferred_element_type=jnp.float32
    ) * (1.0 / math.sqrt(HEAD))
    scores = jnp.where(allowed[:, None, None, :], scores, -jnp.inf)
    row_max = jnp.max(scores, axis=-1, keepdims=True)
    weights = jnp.exp(scores - row_max)
    row_total = jnp.sum(weights, axis=-1)
    probability = weights.astype(jnp.bfloat16)
    context_sum = jnp.einsum(
        "bhqk,bkhe->bqhe", probability, value_heads, preferred_element_type=jnp.float32
    )
    context = context_sum / jnp.transpose(row_total, (0, 2, 1))[..., None]
    return context.reshape(block_count, row_count, heads_width).astype(jnp.bfloat16)


def general(
    signal,
    position_kernel,
    position_bias,
    layer_gain,
    layer_shift,
    query_weight,
    query_bias,
    key_weight,
    value_weight,
    value_bias,
    output_weight,
    output_bias,
    key_blocks,
    global_blocks,
):
    devices = lax.axis_size("tm")
    frame_count, model_width = signal.shape
    channel_share, group_width, kernel_taps = position_kernel.shape
    inner_width = max(channel_share, group_width)
    folded = signal.T
    if channel_share >= group_width:
        outgoing = folded.reshape(devices, channel_share, frame_count)
    else:
        start_groups = np.arange(devices) * channel_share // group_width
        grouped = folded.reshape(model_width // group_width, group_width, frame_count)
        outgoing = jnp.stack(
            [grouped[at * channel_share // group_width] for at in range(devices)]
        )
    incoming = lax.all_to_all(outgoing, "tm", split_axis=0, concat_axis=2, tiled=True)
    outputs = channel_share if channel_share < group_width else group_width
    spread = jnp.pad(
        incoming.reshape(inner_width // group_width, group_width, -1),
        ((0, 0), (0, 0), (kernel_taps // 2, kernel_taps // 2 - 1)),
    )
    frames = incoming.shape[-1]
    by_tap = position_kernel.reshape(-1, outputs, group_width, kernel_taps).transpose(3, 0, 1, 2)

    def tap(at, total):
        window = lax.dynamic_slice_in_dim(spread, at, frames, axis=2)
        return total + jnp.einsum(
            "goi,git->got", by_tap[at], window, preferred_element_type=jnp.float32
        )

    response = lax.fori_loop(
        0, kernel_taps, tap, jnp.zeros((spread.shape[0], outputs, frames), jnp.float32)
    ).reshape(channel_share, frames)
    position = jax.nn.gelu(response + position_bias[:, None], approximate=False).astype(
        jnp.bfloat16
    )
    returned = lax.all_to_all(position, "tm", split_axis=1, concat_axis=0, tiled=True)
    hidden = signal.astype(jnp.float32) + returned.T.astype(jnp.float32)
    average = jnp.mean(hidden, axis=-1, keepdims=True)
    centered = hidden - average
    variance = jnp.mean(centered * centered, axis=-1, keepdims=True)
    normed = (centered * lax.rsqrt(variance + EPSILON) * layer_gain + layer_shift).astype(
        jnp.bfloat16
    )
    heads_width = query_weight.shape[1]
    zero_sums = jnp.zeros((frame_count, heads_width), jnp.float32)
    totals = (zero_sums, zero_sums, zero_sums)
    pieces = (
        lax.all_gather(query_weight, "tm", axis=0, tiled=True),
        lax.all_gather(key_weight, "tm", axis=0, tiled=True),
        lax.all_gather(value_weight, "tm", axis=0, tiled=True),
    )
    columns = lax.slice_in_dim(normed, 0, pieces[0].shape[0], axis=1)
    query_sum, key_sum, value_sum = tuple(
        (
            running + jnp.dot(columns, weight_rows, preferred_element_type=jnp.float32)
            for running, weight_rows in zip(totals, pieces)
        )
    )
    queries = (query_sum + query_bias).astype(jnp.bfloat16)
    key_part = key_sum.astype(jnp.bfloat16)
    value_part = (value_sum + value_bias).astype(jnp.bfloat16)
    key_value = jnp.stack((key_part, value_part), axis=1)
    per_device = frame_count // BLOCK
    repeated = jnp.any(global_blocks[None, :, None] == key_blocks[:, None, :], axis=-1)
    whole = lax.all_gather(key_value, "tm", axis=0, tiled=True)
    block_ids = jnp.concatenate(
        [key_blocks, jnp.broadcast_to(global_blocks[None, :], (per_device, GLOBALS))], axis=1
    )
    allowed = jnp.concatenate([key_blocks >= 0, jnp.logical_not(repeated)], axis=1)
    table = whole.reshape(-1, BLOCK, 2, heads_width)
    chosen = jnp.maximum(block_ids, 0)
    candidates = jnp.stack(
        [
            jnp.stack(
                [
                    lax.dynamic_index_in_dim(table, chosen[row, at], 0, keepdims=False)
                    for at in range(chosen.shape[1])
                ]
            )
            for row in range(per_device)
        ]
    )
    key_rows = candidates[:, :, :, 0].reshape(per_device, -1, heads_width)
    value_rows = candidates[:, :, :, 1].reshape(per_device, -1, heads_width)
    allowed_rows = jnp.repeat(allowed, BLOCK, axis=1)
    context = attend(
        queries.reshape(per_device, BLOCK, heads_width), key_rows, value_rows, allowed_rows
    ).reshape(frame_count, heads_width)
    projected = jnp.dot(
        context,
        lax.all_gather(output_weight, "tm", axis=1, tiled=True),
        preferred_element_type=jnp.float32,
    )
    return (hidden + projected + output_bias).astype(jnp.bfloat16)


PHASES = 3
GROUP = 80
MEMBERS = 8
QUARTERS = 4
LANES = 128
STEP = 4
STEPS = 44
SPAN = 43
PACKED = 160
PADDED = 145
MESH = pl.DeviceIdType.MESH
BIG = 1e30
F32 = jnp.float32
BF16 = jnp.bfloat16


def flip(member, bits):
    low = bits % 4
    if low == 1:
        turned = member + 1 - 2 * lax.rem(member, 2)
    elif low == 2:
        turned = member + 2 - 4 * lax.rem(lax.div(member, 2), 2)
    elif low == 3:
        turned = 4 * lax.div(member, 4) + 3 - lax.rem(member, 4)
    else:
        turned = member
    return lax.rem(turned + 4, MEMBERS) if bits >= 4 else turned


def loop(begin, end, body, unroll):
    turns = (end - begin) // unroll

    def turn(step, _):
        for at in range(unroll):
            body(begin + step * unroll + at)
        return 0

    if turns > 1:
        lax.fori_loop(0, turns, turn, 0)
    else:
        turns = 0
    for at in range(begin + turns * unroll, end):
        body(at)


def row_of(ref):
    return ref[...].reshape(1, -1)


def pack(value):
    return jnp.concatenate(
        [
            jnp.concatenate([value[:96], value[160:, :48]], axis=1),
            jnp.concatenate([value[96:128], value[160:192, 48:], value[224:, 48:64]], axis=1),
            jnp.concatenate([value[128:160], value[192:224, 48:], value[224:, 64:]], axis=1),
        ],
        axis=0,
    )


def unpack(ref, begin, end):
    if end <= 160:
        return ref[begin:end, :GROUP]
    if end <= 224:
        return jnp.concatenate(
            [ref[begin - 160 : end - 160, GROUP:], ref[begin - 64 : end - 64, GROUP:112]], axis=1
        )
    return jnp.concatenate(
        [ref[64:96, GROUP:], ref[96:128, 112:], ref[128:160, 112:]], axis=1
    )


def remote(source, target, send, receive, device):
    return pltpu.make_async_remote_copy(
        src_ref=source,
        dst_ref=target,
        send_sem=send,
        recv_sem=receive,
        device_id=device,
        device_id_type=MESH,
    )


class Spread:
    def __init__(self, piece, record, member, sends, receives):
        self.piece, self.record, self.member = piece, record, member
        self.sends, self.receives = sends, receives
        self.across = lax.rem(record + 2, QUARTERS)
        self.beside = record + 1 - 2 * lax.rem(record, 2)

    def copy(self, at, share, quarter, device):
        ref = self.piece(share, quarter)
        return remote(ref, ref, self.sends.at[at], self.receives.at[at], device)

    def plane(self, at):
        bits = at + 1
        if bits <= 4:
            return self.copy(at, self.member, self.record, (self.record, flip(self.member, bits)))
        share = flip(self.member, 4)
        return self.copy(at, share, self.record, (self.record, flip(self.member, bits - 4)))

    def other(self, at):
        return self.copy(7 + at, flip(self.member, at + 1), self.record, (self.across, self.member))

    def core(self, at):
        return self.copy(14 + at, flip(self.member, at + 1), self.record, (self.beside, self.member))

    def last(self, at):
        return self.copy(21 + at, flip(self.member, at + 1), self.across, (self.beside, self.member))

    def first(self):
        for at in (3, 0, 1, 2):
            self.plane(at).start()

    def second(self):
        self.plane(3).wait_recv()
        for at in (4, 5, 6):
            self.plane(at).start()
        self.other(3).start()
        self.core(3).start()
        for at in (0, 1, 2):
            self.plane(at).wait_recv()
            self.other(at).start()
            self.core(at).start()

    def third(self):
        for at in (4, 5, 6):
            self.plane(at).wait_recv()
            self.other(at).start()
            self.core(at).start()

    def fourth(self, which):
        for at in which:
            self.other(at).wait_recv()
            self.last(at).start()

    def near(self):
        for at in range(7):
            self.core(at).wait_recv()

    def far(self):
        for at in range(7):
            self.last(at).wait_recv()

    def sent(self):
        for at in range(7):
            for copy in (self.plane(at), self.other(at), self.core(at), self.last(at)):
                copy.wait_send()


def whole_kernel(
    blocks_ref,
    globals_ref,
    signal_ref,
    taps_hbm,
    tap_bias_ref,
    gain_ref,
    shift_ref,
    query_ref,
    key_ref,
    value_ref,
    query_bias_ref,
    value_bias_ref,
    output_ref,
    output_bias_ref,
    out_ref,
    taps_ref,
    turned_ref,
    matrix_ref,
    send_ref,
    got_ref,
    frames_ref,
    spread_ref,
    total_ref,
    natural_ref,
    back_ref,
    returned_ref,
    hidden_ref,
    normed_ref,
    rows_ref,
    output_rows_ref,
    bias_ref,
    slab_ref,
    headed_ref,
    asked_ref,
    asking_ref,
    keys_ref,
    values_ref,
    chosen_ref,
    context_ref,
    contexts_ref,
    load_sem,
    signal_send,
    signal_recv,
    back_send,
    back_recv,
    rows_send,
    rows_recv,
    outs_send,
    outs_recv,
    head_send,
    head_recv,
    ask_send,
    ask_recv,
    context_send,
    context_recv,
):
    record, member = lax.axis_index("rec"), lax.axis_index("tm")
    load = pltpu.make_async_copy(taps_hbm, taps_ref, load_sem)
    load.start()

    barrier = pltpu.get_barrier_semaphore()
    across = lax.rem(record + 2, QUARTERS)
    beside = record + 1 - 2 * lax.rem(record, 2)
    peers = [(record, lax.rem(member + at, MEMBERS)) for at in range(1, MEMBERS)]
    for peer in peers + [(across, member), (beside, member)]:
        pl.semaphore_signal(barrier, inc=1, device_id=peer, device_id_type=MESH)

    frame_count = signal_ref.shape[0]
    share = 2 * GROUP
    rest = share - LANES

    def signal_copy(group, at):
        to = lax.rem(member + at, MEMBERS)
        return remote(
            send_ref.at[group, to],
            got_ref.at[group, member],
            signal_send.at[group * 7 + at - 1],
            signal_recv.at[group * 7 + at - 1],
            (record, to),
        )

    for group in range(2):
        for to in range(MEMBERS):
            begin = to * share + group * GROUP
            send_ref[group, to] = pack(signal_ref[:, begin : begin + GROUP])
        if group == 0:
            pl.semaphore_wait(barrier, 9)
        for at in range(1, MEMBERS):
            signal_copy(group, at).start()
        got_ref[group, member] = send_ref[group, member]

    mine = pl.ds(pl.multiple_of(member * share, 32), share)
    for head in range(HEADS):
        columns = slice(head * HEAD, (head + 1) * HEAD)
        joined = jnp.concatenate(
            [
                key_ref[:, columns],
                value_ref[:, columns],
                query_ref[:, columns],
                jnp.zeros((share, 16), BF16),
            ],
            axis=1,
        )
        tile = head % QUARTERS * 4 + head // QUARTERS * 2
        rows_ref[tile, mine, :] = joined[:, :LANES]
        rows_ref[tile + 1, mine, :] = joined[:, LANES:]
    heads_width = HEADS * HEAD
    for at in range(heads_width // LANES):
        output_rows_ref[member, share * at : share * at + share, :] = output_ref[
            :, at * LANES : (at + 1) * LANES
        ]
    output_rows_ref[member, 5 * share :, :] = jnp.zeros((32, LANES), BF16)
    empty = jnp.zeros((1, HEAD), F32)
    for head in range(HEADS):
        columns = slice(head * HEAD, (head + 1) * HEAD)
        bias_ref[head : head + 1, :] = jnp.concatenate(
            [
                empty,
                row_of(value_bias_ref)[:, columns],
                row_of(query_bias_ref)[:, columns],
                empty[:, :16],
            ],
            axis=1,
        )

    def rows_piece(of, quarter):
        return rows_ref.at[
            pl.ds(quarter * 4, 4), pl.ds(pl.multiple_of(of * share, 32), share), :
        ]

    def output_piece(of, quarter):
        return output_rows_ref.at[of, pl.ds(pl.multiple_of(quarter * 208, 16), 208), :]

    rows = Spread(rows_piece, record, member, rows_send, rows_recv)
    outs = Spread(output_piece, record, member, outs_send, outs_recv)
    rows.first()

    load.wait()
    empty = jnp.zeros((8, LANES), F32)

    def turn(channel):
        begin = channel * PADDED
        turned_ref[pl.ds(begin, 8), :] = empty
        turned_ref[pl.ds(begin + 136, 8), :] = empty
        turned_ref[pl.ds(begin + 8, LANES), :GROUP] = jnp.transpose(taps_ref[channel]).astype(F32)

    loop(0, share, turn, 16)

    def lay(step):
        for group in range(2):
            taps = [
                turned_ref[
                    pl.ds(group * GROUP * PADDED + step * 3 + 6 + at, GROUP, stride=PADDED), :
                ].astype(BF16)[:, :GROUP]
                for at in range(5)
            ]
            for phase in range(PHASES):
                row = jnp.concatenate(
                    taps[2 - phase : 5 - phase] + [jnp.zeros((GROUP, 16), BF16)], axis=1
                )
                begin = pl.multiple_of((step * PHASES + phase) * GROUP, 16)
                matrix_ref[group, pl.ds(begin, GROUP), :] = row

    loop(0, STEPS, lay, 4)

    frames = MEMBERS * frame_count
    tail = 64 + frames + (64 + frames) // BLOCK

    def back_copy(group, at):
        to = lax.rem(member + at, MEMBERS)
        return remote(
            back_ref.at[group, to],
            returned_ref.at[group, member],
            back_send.at[group * 7 + at - 1],
            back_recv.at[group * 7 + at - 1],
            (record, to),
        )

    for group in range(2):
        frames_ref[:64, :] = jnp.zeros((64, LANES), F32)
        frames_ref[tail:, :] = jnp.zeros((frames_ref.shape[0] - tail, LANES), F32)
        for at in range(1, MEMBERS):
            signal_copy(group, at).wait_recv()

        def place(of, group=group):
            begin = of * (frame_count + 2) + 64
            packed = got_ref.at[group, of]
            for low, high, skew in (
                (0, 64, 0),
                (64, 160, 1),
                (160, 192, 1),
                (192, 224, 2),
                (224, 256, 2),
            ):
                frames_ref[pl.ds(begin + low + skew, high - low), :GROUP] = unpack(
                    packed, low, high
                ).astype(F32)

        loop(0, MEMBERS, place, 2)

        def widen(row):
            parts = []
            for phase in range(PHASES):
                at = row * PHASES + phase
                part = frames_ref[pl.ds(at + at // BLOCK, 16, stride=BLOCK + 1), :]
                parts.append(part.astype(BF16)[:, :GROUP])
            spread_ref[row] = jnp.concatenate(parts + [jnp.zeros((16, 16), BF16)], axis=1)

        loop(0, STEPS * 2, widen, 11)
        if group == 0:
            rows.second()
        window = jnp.concatenate(
            [
                spread_ref[step : step + SPAN].reshape(SPAN * 16, 2 * LANES)
                for step in range(STEPS)
            ],
            axis=1,
        )
        weights = jnp.concatenate(
            [matrix_ref[group, step * 240 : step * 240 + 240, :] for step in range(STEPS)],
            axis=1,
        )
        total_ref[...] = lax.dot_general(
            window, weights, (((1,), (1,)), ((), ())), preferred_element_type=F32
        )
        bias = row_of(tap_bias_ref)[:, group * GROUP : (group + 1) * GROUP]
        bias = jnp.concatenate([bias] * PHASES, axis=1)

        def activate(row, bias=bias):
            value = total_ref[pl.ds(pl.multiple_of(row * 16, 16), 16), :] + bias
            value = value * (1.0 + lax.erf(value * (0.5**0.5))) * 0.5
            for phase in range(PHASES):
                part = value[:, phase * GROUP : (phase + 1) * GROUP]
                part = jnp.concatenate([part, jnp.zeros((16, LANES - GROUP), F32)], axis=1)
                begin = row * PHASES + phase
                begin = begin + begin // BLOCK
                natural_ref[pl.ds(begin, 16, stride=BLOCK + 1), :] = part

        loop(0, SPAN, activate, 11)

        def pack_back(to, group=group):
            begin = 2 * to * (BLOCK + 1)
            halves = [
                natural_ref[pl.ds(begin + side * (BLOCK + 1), BLOCK), :].astype(BF16)[:, :GROUP]
                for side in range(2)
            ]
            back_ref[group, to] = pack(jnp.concatenate(halves, axis=0))

        loop(0, MEMBERS, pack_back, 4)
        for at in range(1, MEMBERS):
            back_copy(group, at).start()
        returned_ref[group, member] = back_ref[group, member]
        if group == 0:
            rows.third()
    outs.first()
    rows.fourth((3, 0, 1, 2))

    for group in range(2):
        for at in range(1, MEMBERS):
            back_copy(group, at).wait_recv()
    for begin in range(0, frame_count, 32):
        pieces = [
            unpack(returned_ref.at[group, of], begin, begin + 32)
            for of in range(MEMBERS)
            for group in range(2)
        ]
        position = jnp.concatenate(pieces, axis=1)
        hidden = signal_ref[begin : begin + 32, :].astype(F32) + position.astype(F32)
        hidden_ref[begin : begin + 32, :] = hidden
        average = jnp.mean(hidden, axis=-1, keepdims=True)
        centered = hidden - average
        variance = jnp.mean(centered * centered, axis=-1, keepdims=True)
        normed_ref[begin : begin + 32, :] = (
            centered * lax.rsqrt(variance + EPSILON) * row_of(gain_ref) + row_of(shift_ref)
        ).astype(BF16)

    rows.near()
    lane = lax.broadcasted_iota(jnp.int32, (BLOCK, 2 * LANES), 1) - 3 * HEAD
    masks = []
    for block in range(2):
        unlisted = jnp.where(lane >= 0, 1.0, 0.0)
        for at in range(blocks_ref.shape[1]):
            unlisted = jnp.where(lane == jnp.where(lane >= 0, blocks_ref[block, at], -1000), 0.0, unlisted)
        masks.append(unlisted)
    mask = jnp.concatenate(masks, axis=0)

    rest = share - LANES

    def head_copy(source, to, at):
        return remote(
            slab_ref.at[to],
            headed_ref.at[source],
            head_send.at[at],
            head_recv.at[source],
            (record, to),
        )

    def ask_copy(at):
        to = lax.rem(member + at, MEMBERS)
        return remote(
            asked_ref.at[to],
            asking_ref.at[member],
            ask_send.at[at - 1],
            ask_recv.at[at - 1],
            (record, to),
        )

    def chosen_head(at):
        turned = lax.rem(member + at, 4)
        first = jnp.where(at < 4, record, across)
        second = first + 1 - 2 * lax.rem(first, 2)
        quarter = jnp.where(turned < 2, first, second)
        return quarter, lax.rem(turned, 2)

    def project(at):
        quarter, side = chosen_head(at)
        head, tile = quarter + 4 * side, 4 * quarter + 2 * side
        weights = jnp.concatenate([rows_ref[tile], rows_ref[tile + 1]], axis=1)
        slab = jnp.dot(normed_ref[...], weights, preferred_element_type=F32)
        slab = (slab + bias_ref[pl.ds(head, 1), :] + mask).astype(BF16)
        slab_ref[head, :frame_count, :] = slab[:, :LANES]
        slab_ref[head, frame_count:, :] = jnp.concatenate(
            [slab[64 * part : 64 * part + 64, LANES:share] for part in range(4)], axis=1
        )
        asked = slab[:, share:]
        asked_ref[head] = jnp.concatenate(
            [
                asked[:192],
                jnp.concatenate(
                    [asked[192:, part * 32 : part * 32 + 32] for part in range(3)], axis=0
                ),
            ],
            axis=1,
        )

        @pl.when(head != member)
        def _():
            head_copy(member, head, at).start()

        @pl.when(head == member)
        def _():
            headed_ref[member] = slab_ref[head]

    for at in range(4):
        project(at)
    rows.fourth((4, 5, 6))
    rows.far()
    for at in range(4, 8):
        project(at)
    for at in range(1, MEMBERS):
        ask_copy(at).start()
    asking_ref[member] = asked_ref[member]

    outs.second()
    place_row = lax.broadcasted_iota(jnp.int32, (BLOCK, frames), 0)
    place_column = lax.broadcasted_iota(jnp.int32, (BLOCK, frames), 1)
    for at in range(GLOBALS):
        chosen_ref[at * BLOCK : (at + 1) * BLOCK, :] = jnp.where(
            place_row + globals_ref[at] * BLOCK == place_column, 1.0, 0.0
        ).astype(BF16)

    def arrange(of):
        slab = headed_ref[of]
        begin = pl.multiple_of(of * frame_count, 256)
        row = lax.broadcasted_iota(jnp.int32, (frame_count, 16), 0)
        block = 2 * of + jnp.where(row >= BLOCK, 1, 0)
        here = lax.broadcasted_iota(jnp.int32, (frame_count, 16), 1) == block
        keys_ref[pl.ds(begin, frame_count), :] = jnp.concatenate(
            [
                slab[:frame_count, :HEAD],
                jnp.where(here, -BIG, 0.0).astype(BF16),
                jnp.zeros((frame_count, 32), BF16),
            ],
            axis=1,
        )
        side = jnp.concatenate(
            [slab[frame_count:, rest * part : rest * part + rest] for part in range(4)], axis=0
        )
        values_ref[pl.ds(begin, frame_count), :] = jnp.concatenate(
            [
                slab[:frame_count, HEAD:],
                side,
                jnp.ones((frame_count, 16), BF16),
                jnp.zeros((frame_count, 32), BF16),
            ],
            axis=1,
        )

    arrange(member)
    for at in range(1, MEMBERS):
        of = lax.rem(member + at, MEMBERS)
        head_copy(of, member, 0).wait_recv()
        arrange(of)
    outs.third()
    lane = lax.broadcasted_iota(jnp.int32, (BLOCK, LANES), 1)
    picked = jnp.dot(
        chosen_ref[...],
        jnp.concatenate([keys_ref[:frames, :], values_ref[:frames, :]], axis=1),
        preferred_element_type=F32,
    )
    for at in range(GLOBALS):
        rows_at = slice(at * BLOCK, (at + 1) * BLOCK)
        keys_ref[frames + at * BLOCK : frames + (at + 1) * BLOCK, :] = jnp.where(
            lane < HEAD,
            picked[rows_at, :LANES],
            jnp.where(lane == HEAD + 16 + globals_ref[at], -BIG, 0.0),
        ).astype(BF16)
        values_ref[frames + at * BLOCK : frames + (at + 1) * BLOCK, :] = picked[
            rows_at, LANES:
        ].astype(BF16)

    factor = (1.0 / math.sqrt(HEAD)) * math.log2(math.e)

    def context_copy(at):
        to = lax.rem(member + at, MEMBERS)
        return remote(
            context_ref.at[to],
            contexts_ref.at[member],
            context_send.at[at - 1],
            context_recv.at[at - 1],
            (record, to),
        )

    def attend_tile(of):
        asked = asking_ref[of]
        last = jnp.concatenate(
            [asked[64 * part : 64 * part + 64, 96:] for part in range(3)], axis=1
        )
        asked = jnp.concatenate([asked[:, :96], last], axis=0)
        queries = jnp.concatenate(
            [asked, 1.0 - asked[:, HEAD:], jnp.zeros((frame_count, 16), BF16)], axis=1
        )
        low = jnp.minimum(jnp.maximum(2 * of - 2, 0), 10)
        window = pl.ds(pl.multiple_of(low * BLOCK, BLOCK), 6 * BLOCK)
        keys = jnp.concatenate([keys_ref[window, :], keys_ref[frames:, :]], axis=0)
        scores = lax.dot_general(
            queries, keys, (((1,), (1,)), ((), ())), preferred_element_type=F32
        )
        peak = jnp.max(scores, axis=1, keepdims=True)
        weights = jnp.exp2(scores * factor - peak * factor).astype(BF16)
        values = jnp.concatenate([values_ref[window, :], values_ref[frames:, :]], axis=0)
        summed = jnp.dot(weights, values, preferred_element_type=F32)
        return pack((summed[:, :HEAD] / summed[:, HEAD : HEAD + 1]).astype(BF16))

    contexts_ref[member] = attend_tile(member)
    for pair in ((7,), (6, 5), (4, 3), (2, 1)):
        for at in pair:
            ask_copy(at).wait_recv()
        for at in pair:
            of = lax.rem(member - at + MEMBERS, MEMBERS)
            context_ref[of] = attend_tile(of)
        for at in pair:
            context_copy(MEMBERS - at).start()
    outs.fourth(range(7))

    for at in range(1, MEMBERS):
        context_copy(at).wait_recv()
    outs.near()
    outs.far()
    context = jnp.concatenate(
        [
            jnp.concatenate(
                [
                    unpack(contexts_ref.at[of], 0, 160),
                    unpack(contexts_ref.at[of], 160, 224),
                    unpack(contexts_ref.at[of], 224, 256),
                ],
                axis=0,
            )
            for of in range(HEADS)
        ],
        axis=1,
    )
    columns = jnp.concatenate(
        [
            jnp.concatenate(
                [output_rows_ref[of, share * at : share * at + share, :] for at in range(5)], axis=1
            )
            for of in range(MEMBERS)
        ],
        axis=0,
    )
    projected = lax.dot_general(
        context, columns, (((1,), (1,)), ((), ())), preferred_element_type=F32
    )
    out_ref[...] = (hidden_ref[...] + projected + row_of(output_bias_ref)).astype(BF16)

    for at in range(1, MEMBERS):
        for group in range(2):
            signal_copy(group, at).wait_send()
            back_copy(group, at).wait_send()
        ask_copy(at).wait_send()
        context_copy(at).wait_send()
    for at in range(MEMBERS):
        quarter, side = chosen_head(at)

        @pl.when(quarter + 4 * side != member)
        def _(head=quarter + 4 * side, at=at):
            head_copy(member, head, at).wait_send()

    rows.sent()
    outs.sent()


def by_heads(
    signal,
    position_kernel,
    position_bias,
    layer_gain,
    layer_shift,
    query_weight,
    query_bias,
    key_weight,
    value_weight,
    value_bias,
    output_weight,
    output_bias,
    key_blocks,
    global_blocks,
):
    frame_count, width = signal.shape
    frames = MEMBERS * frame_count
    share = 2 * GROUP
    vmem = pl.BlockSpec(memory_space=pltpu.VMEM)
    smem = pl.BlockSpec(memory_space=pltpu.SMEM)
    dma = pltpu.SemaphoreType.DMA
    return pl.pallas_call(
        whole_kernel,
        out_shape=jax.ShapeDtypeStruct((frame_count, width), BF16),
        in_specs=[smem, smem, vmem, pl.BlockSpec(memory_space=pl.ANY)] + [vmem] * 10,
        out_specs=vmem,
        scratch_shapes=[
            pltpu.VMEM((share, GROUP, LANES), BF16),
            pltpu.VMEM((share * PADDED, LANES), F32),
            pltpu.VMEM((2, STEPS * PHASES * GROUP, 2 * LANES), BF16),
            pltpu.VMEM((2, MEMBERS, PACKED, LANES), BF16),
            pltpu.VMEM((2, MEMBERS, PACKED, LANES), BF16),
            pltpu.VMEM((frames + 160, LANES), F32),
            pltpu.VMEM((STEPS * 2, 16, 2 * LANES), BF16),
            pltpu.VMEM((SPAN * 16, PHASES * GROUP), F32),
            pltpu.VMEM((frames + 32, LANES), F32),
            pltpu.VMEM((2, MEMBERS, PACKED, LANES), BF16),
            pltpu.VMEM((2, MEMBERS, PACKED, LANES), BF16),
            pltpu.VMEM((frame_count, width), F32),
            pltpu.VMEM((frame_count, width), BF16),
            pltpu.VMEM((2 * HEADS, width, LANES), BF16),
            pltpu.VMEM((MEMBERS, 832, LANES), BF16),
            pltpu.VMEM((HEADS, 2 * LANES), F32),
            pltpu.VMEM((MEMBERS, frame_count + 64, LANES), BF16),
            pltpu.VMEM((MEMBERS, frame_count + 64, LANES), BF16),
            pltpu.VMEM((MEMBERS, 192, LANES), BF16),
            pltpu.VMEM((MEMBERS, 192, LANES), BF16),
            pltpu.VMEM((frames + GLOBALS * BLOCK, LANES), BF16),
            pltpu.VMEM((frames + GLOBALS * BLOCK, LANES), BF16),
            pltpu.VMEM((GLOBALS * BLOCK, frames), BF16),
            pltpu.VMEM((MEMBERS, PACKED, LANES), BF16),
            pltpu.VMEM((MEMBERS, PACKED, LANES), BF16),
            dma,
            dma((14,)),
            dma((14,)),
            dma((14,)),
            dma((14,)),
            dma((28,)),
            dma((28,)),
            dma((28,)),
            dma((28,)),
            dma((8,)),
            dma((8,)),
            dma((7,)),
            dma((7,)),
            dma((7,)),
            dma((7,)),
        ],
        compiler_params=pltpu.CompilerParams(
            collective_id=0, has_side_effects=True, vmem_limit_bytes=60 * 1024 * 1024
        ),
    )(
        key_blocks,
        global_blocks,
        signal,
        position_kernel,
        position_bias,
        layer_gain,
        layer_shift,
        query_weight,
        key_weight,
        value_weight,
        query_bias,
        value_bias,
        output_weight.T,
        output_bias,
    )


def body(*operands):
    share, width, taps = operands[1].shape
    fits = lax.axis_size("tm") == MEMBERS and lax.axis_size("rec") == QUARTERS
    fits = fits and (share, width, taps) == (2 * GROUP, GROUP, LANES)
    fits = fits and operands[0].shape[0] == 2 * BLOCK
    return (by_heads if fits else general)(*operands)


def solution(mesh):
    placed = (
        P(("rec", "tm"), None),
        P("tm", None, None),
        P("tm"),
        P(),
        P(),
        P("tm", None),
        P(),
        P("tm", None),
        P("tm", None),
        P(),
        P(None, "tm"),
        P(),
        P(("rec", "tm"), None),
        P("rec"),
    )
    return jax.shard_map(
        body, mesh=mesh, in_specs=placed, out_specs=P(("rec", "tm"), None), check_vma=False
    )
```

```python
import math

import jax
import jax.numpy as jnp
import numpy as np
from jax import lax
from jax.experimental import pallas as pl
from jax.experimental.pallas import tpu as pltpu
from jax.sharding import PartitionSpec as P

HEAD = 80
HEADS = 8
BLOCK = 128
GLOBALS = 4


EPSILON = 1e-05


def attend(queries, key_rows, value_rows, allowed):
    block_count, row_count, heads_width = queries.shape
    query_heads = queries.reshape(block_count, row_count, HEADS, HEAD)
    key_heads = key_rows.reshape(block_count, key_rows.shape[1], HEADS, HEAD)
    value_heads = value_rows.reshape(block_count, value_rows.shape[1], HEADS, HEAD)
    scores = jnp.einsum(
        "bqhe,bkhe->bhqk", query_heads, key_heads, preferred_element_type=jnp.float32
    ) * (1.0 / math.sqrt(HEAD))
    scores = jnp.where(allowed[:, None, None, :], scores, -jnp.inf)
    row_max = jnp.max(scores, axis=-1, keepdims=True)
    weights = jnp.exp(scores - row_max)
    row_total = jnp.sum(weights, axis=-1)
    probability = weights.astype(jnp.bfloat16)
    context_sum = jnp.einsum(
        "bhqk,bkhe->bqhe", probability, value_heads, preferred_element_type=jnp.float32
    )
    context = context_sum / jnp.transpose(row_total, (0, 2, 1))[..., None]
    return context.reshape(block_count, row_count, heads_width).astype(jnp.bfloat16)


def general(
    signal,
    position_kernel,
    position_bias,
    layer_gain,
    layer_shift,
    query_weight,
    query_bias,
    key_weight,
    value_weight,
    value_bias,
    output_weight,
    output_bias,
    key_blocks,
    global_blocks,
):
    devices = lax.axis_size("tm")
    frame_count, model_width = signal.shape
    channel_share, group_width, kernel_taps = position_kernel.shape
    inner_width = max(channel_share, group_width)
    folded = signal.T
    if channel_share >= group_width:
        outgoing = folded.reshape(devices, channel_share, frame_count)
    else:
        start_groups = np.arange(devices) * channel_share // group_width
        grouped = folded.reshape(model_width // group_width, group_width, frame_count)
        outgoing = jnp.stack(
            [grouped[at * channel_share // group_width] for at in range(devices)]
        )
    incoming = lax.all_to_all(outgoing, "tm", split_axis=0, concat_axis=2, tiled=True)
    outputs = channel_share if channel_share < group_width else group_width
    spread = jnp.pad(
        incoming.reshape(inner_width // group_width, group_width, -1),
        ((0, 0), (0, 0), (kernel_taps // 2, kernel_taps // 2 - 1)),
    )
    frames = incoming.shape[-1]
    by_tap = position_kernel.reshape(-1, outputs, group_width, kernel_taps).transpose(3, 0, 1, 2)

    def tap(at, total):
        window = lax.dynamic_slice_in_dim(spread, at, frames, axis=2)
        return total + jnp.einsum(
            "goi,git->got", by_tap[at], window, preferred_element_type=jnp.float32
        )

    response = lax.fori_loop(
        0, kernel_taps, tap, jnp.zeros((spread.shape[0], outputs, frames), jnp.float32)
    ).reshape(channel_share, frames)
    position = jax.nn.gelu(response + position_bias[:, None], approximate=False).astype(
        jnp.bfloat16
    )
    returned = lax.all_to_all(position, "tm", split_axis=1, concat_axis=0, tiled=True)
    hidden = signal.astype(jnp.float32) + returned.T.astype(jnp.float32)
    average = jnp.mean(hidden, axis=-1, keepdims=True)
    centered = hidden - average
    variance = jnp.mean(centered * centered, axis=-1, keepdims=True)
    normed = (centered * lax.rsqrt(variance + EPSILON) * layer_gain + layer_shift).astype(
        jnp.bfloat16
    )
    heads_width = query_weight.shape[1]
    zero_sums = jnp.zeros((frame_count, heads_width), jnp.float32)
    totals = (zero_sums, zero_sums, zero_sums)
    pieces = (
        lax.all_gather(query_weight, "tm", axis=0, tiled=True),
        lax.all_gather(key_weight, "tm", axis=0, tiled=True),
        lax.all_gather(value_weight, "tm", axis=0, tiled=True),
    )
    columns = lax.slice_in_dim(normed, 0, pieces[0].shape[0], axis=1)
    query_sum, key_sum, value_sum = tuple(
        (
            running + jnp.dot(columns, weight_rows, preferred_element_type=jnp.float32)
            for running, weight_rows in zip(totals, pieces)
        )
    )
    queries = (query_sum + query_bias).astype(jnp.bfloat16)
    key_part = key_sum.astype(jnp.bfloat16)
    value_part = (value_sum + value_bias).astype(jnp.bfloat16)
    key_value = jnp.stack((key_part, value_part), axis=1)
    per_device = frame_count // BLOCK
    repeated = jnp.any(global_blocks[None, :, None] == key_blocks[:, None, :], axis=-1)
    whole = lax.all_gather(key_value, "tm", axis=0, tiled=True)
    block_ids = jnp.concatenate(
        [key_blocks, jnp.broadcast_to(global_blocks[None, :], (per_device, GLOBALS))], axis=1
    )
    allowed = jnp.concatenate([key_blocks >= 0, jnp.logical_not(repeated)], axis=1)
    table = whole.reshape(-1, BLOCK, 2, heads_width)
    chosen = jnp.maximum(block_ids, 0)
    candidates = jnp.stack(
        [
            jnp.stack(
                [
                    lax.dynamic_index_in_dim(table, chosen[row, at], 0, keepdims=False)
                    for at in range(chosen.shape[1])
                ]
            )
            for row in range(per_device)
        ]
    )
    key_rows = candidates[:, :, :, 0].reshape(per_device, -1, heads_width)
    value_rows = candidates[:, :, :, 1].reshape(per_device, -1, heads_width)
    allowed_rows = jnp.repeat(allowed, BLOCK, axis=1)
    context = attend(
        queries.reshape(per_device, BLOCK, heads_width), key_rows, value_rows, allowed_rows
    ).reshape(frame_count, heads_width)
    projected = jnp.dot(
        context,
        lax.all_gather(output_weight, "tm", axis=1, tiled=True),
        preferred_element_type=jnp.float32,
    )
    return (hidden + projected + output_bias).astype(jnp.bfloat16)


PHASES = 3
GROUP = 80
MEMBERS = 8
QUARTERS = 4
LANES = 128
STEP = 4
STEPS = 44
SPAN = 43
PACKED = 160
PADDED = 145
MESH = pl.DeviceIdType.MESH
BIG = 1e30
F32 = jnp.float32
BF16 = jnp.bfloat16


def flip(member, bits):
    low = bits % 4
    if low == 1:
        turned = member + 1 - 2 * lax.rem(member, 2)
    elif low == 2:
        turned = member + 2 - 4 * lax.rem(lax.div(member, 2), 2)
    elif low == 3:
        turned = 4 * lax.div(member, 4) + 3 - lax.rem(member, 4)
    else:
        turned = member
    return lax.rem(turned + 4, MEMBERS) if bits >= 4 else turned


def loop(begin, end, body, unroll):
    turns = (end - begin) // unroll

    def turn(step, _):
        for at in range(unroll):
            body(begin + step * unroll + at)
        return 0

    if turns > 1:
        lax.fori_loop(0, turns, turn, 0)
    else:
        turns = 0
    for at in range(begin + turns * unroll, end):
        body(at)


def row_of(ref):
    return ref[...].reshape(1, -1)


def pack(value):
    return jnp.concatenate(
        [
            jnp.concatenate([value[:96], value[160:, :48]], axis=1),
            jnp.concatenate([value[96:128], value[160:192, 48:], value[224:, 48:64]], axis=1),
            jnp.concatenate([value[128:160], value[192:224, 48:], value[224:, 64:]], axis=1),
        ],
        axis=0,
    )


def unpack(ref, begin, end):
    if end <= 160:
        return ref[begin:end, :GROUP]
    if end <= 224:
        return jnp.concatenate(
            [ref[begin - 160 : end - 160, GROUP:], ref[begin - 64 : end - 64, GROUP:112]], axis=1
        )
    return jnp.concatenate(
        [ref[64:96, GROUP:], ref[96:128, 112:], ref[128:160, 112:]], axis=1
    )


def remote(source, target, send, receive, device):
    return pltpu.make_async_remote_copy(
        src_ref=source,
        dst_ref=target,
        send_sem=send,
        recv_sem=receive,
        device_id=device,
        device_id_type=MESH,
    )


class Spread:
    def __init__(self, piece, record, member, sends, receives):
        self.piece, self.record, self.member = piece, record, member
        self.sends, self.receives = sends, receives
        self.across = lax.rem(record + 2, QUARTERS)
        self.beside = record + 1 - 2 * lax.rem(record, 2)

    def copy(self, at, share, quarter, device):
        ref = self.piece(share, quarter)
        return remote(ref, ref, self.sends.at[at], self.receives.at[at], device)

    def plane(self, at):
        bits = at + 1
        if bits <= 4:
            return self.copy(at, self.member, self.record, (self.record, flip(self.member, bits)))
        share = flip(self.member, 4)
        return self.copy(at, share, self.record, (self.record, flip(self.member, bits - 4)))

    def other(self, at):
        return self.copy(7 + at, flip(self.member, at + 1), self.record, (self.across, self.member))

    def core(self, at):
        return self.copy(14 + at, flip(self.member, at + 1), self.record, (self.beside, self.member))

    def last(self, at):
        return self.copy(21 + at, flip(self.member, at + 1), self.across, (self.beside, self.member))

    def first(self):
        for at in (3, 0, 1, 2):
            self.plane(at).start()

    def second(self):
        for at in (0, 1, 2):
            self.plane(at).wait_recv()
            self.other(at).start()
            self.core(at).start()
        self.plane(3).wait_recv()
        for at in (4, 5, 6):
            self.plane(at).start()
        self.other(3).start()
        self.core(3).start()

    def third(self):
        for at in (4, 5, 6):
            self.plane(at).wait_recv()
            self.other(at).start()
            self.core(at).start()

    def fourth(self, which):
        for at in which:
            self.other(at).wait_recv()
            self.last(at).start()

    def near(self):
        for at in range(7):
            self.core(at).wait_recv()

    def far(self):
        for at in range(7):
            self.last(at).wait_recv()

    def sent(self):
        for at in range(7):
            for copy in (self.plane(at), self.other(at), self.core(at), self.last(at)):
                copy.wait_send()


def whole_kernel(
    blocks_ref,
    globals_ref,
    signal_ref,
    taps_hbm,
    tap_bias_ref,
    gain_ref,
    shift_ref,
    query_ref,
    key_ref,
    value_ref,
    query_bias_ref,
    value_bias_ref,
    output_ref,
    output_bias_ref,
    out_ref,
    taps_ref,
    turned_ref,
    matrix_ref,
    send_ref,
    got_ref,
    frames_ref,
    spread_ref,
    total_ref,
    natural_ref,
    back_ref,
    returned_ref,
    hidden_ref,
    normed_ref,
    rows_ref,
    output_rows_ref,
    bias_ref,
    slab_ref,
    headed_ref,
    asked_ref,
    asking_ref,
    keys_ref,
    values_ref,
    chosen_ref,
    context_ref,
    contexts_ref,
    load_sem,
    signal_send,
    signal_recv,
    back_send,
    back_recv,
    rows_send,
    rows_recv,
    outs_send,
    outs_recv,
    head_send,
    head_recv,
    ask_send,
    ask_recv,
    context_send,
    context_recv,
):
    record, member = lax.axis_index("rec"), lax.axis_index("tm")
    load = pltpu.make_async_copy(taps_hbm, taps_ref, load_sem)
    load.start()

    barrier = pltpu.get_barrier_semaphore()
    across = lax.rem(record + 2, QUARTERS)
    beside = record + 1 - 2 * lax.rem(record, 2)
    peers = [(record, lax.rem(member + at, MEMBERS)) for at in range(1, MEMBERS)]
    for peer in peers + [(across, member), (beside, member)]:
        pl.semaphore_signal(barrier, inc=1, device_id=peer, device_id_type=MESH)

    frame_count = signal_ref.shape[0]
    share = 2 * GROUP
    rest = share - LANES

    def signal_copy(group, at):
        to = lax.rem(member + at, MEMBERS)
        return remote(
            send_ref.at[group, to],
            got_ref.at[group, member],
            signal_send.at[group * 7 + at - 1],
            signal_recv.at[group * 7 + at - 1],
            (record, to),
        )

    def send_signal(group):
        for to in range(MEMBERS):
            begin = to * share + group * GROUP
            send_ref[group, to] = pack(signal_ref[:, begin : begin + GROUP])
        if group == 0:
            pl.semaphore_wait(barrier, 9)
        for at in (4, 3, 5, 2, 6, 1, 7):
            signal_copy(group, at).start()
        got_ref[group, member] = send_ref[group, member]

    send_signal(0)

    mine = pl.ds(pl.multiple_of(member * share, 32), share)
    for head in range(HEADS):
        columns = slice(head * HEAD, (head + 1) * HEAD)
        joined = jnp.concatenate(
            [
                key_ref[:, columns],
                value_ref[:, columns],
                query_ref[:, columns],
                jnp.zeros((share, 16), BF16),
            ],
            axis=1,
        )
        tile = head % QUARTERS * 4 + head // QUARTERS * 2
        rows_ref[tile, mine, :] = joined[:, :LANES]
        rows_ref[tile + 1, mine, :] = joined[:, LANES:]
    def rows_piece(of, quarter):
        return rows_ref.at[
            pl.ds(quarter * 4, 4), pl.ds(pl.multiple_of(of * share, 32), share), :
        ]

    def output_piece(of, quarter):
        return output_rows_ref.at[of, pl.ds(pl.multiple_of(quarter * 208, 16), 208), :]

    rows = Spread(rows_piece, record, member, rows_send, rows_recv)
    outs = Spread(output_piece, record, member, outs_send, outs_recv)
    rows.first()
    send_signal(1)

    heads_width = HEADS * HEAD
    for at in range(heads_width // LANES):
        output_rows_ref[member, share * at : share * at + share, :] = output_ref[
            :, at * LANES : (at + 1) * LANES
        ]
    output_rows_ref[member, 5 * share :, :] = jnp.zeros((32, LANES), BF16)
    empty = jnp.zeros((1, HEAD), F32)
    for head in range(HEADS):
        columns = slice(head * HEAD, (head + 1) * HEAD)
        bias_ref[head : head + 1, :] = jnp.concatenate(
            [
                empty,
                row_of(value_bias_ref)[:, columns],
                row_of(query_bias_ref)[:, columns],
                empty[:, :16],
            ],
            axis=1,
        )


    load.wait()
    empty = jnp.zeros((8, LANES), F32)

    def turn(channel):
        begin = channel * PADDED
        turned_ref[pl.ds(begin, 8), :] = empty
        turned_ref[pl.ds(begin + 136, 8), :] = empty
        turned_ref[pl.ds(begin + 8, LANES), :GROUP] = jnp.transpose(taps_ref[channel]).astype(F32)

    loop(0, share, turn, 16)

    def lay(step):
        for group in range(2):
            taps = [
                turned_ref[
                    pl.ds(group * GROUP * PADDED + step * 3 + 6 + at, GROUP, stride=PADDED), :
                ].astype(BF16)[:, :GROUP]
                for at in range(5)
            ]
            for phase in range(PHASES):
                row = jnp.concatenate(
                    taps[2 - phase : 5 - phase] + [jnp.zeros((GROUP, 16), BF16)], axis=1
                )
                begin = pl.multiple_of((step * PHASES + phase) * GROUP, 16)
                matrix_ref[group, pl.ds(begin, GROUP), :] = row

    loop(0, STEPS, lay, 4)
    rows.second()

    frames = MEMBERS * frame_count
    tail = 64 + frames + (64 + frames) // BLOCK

    def back_copy(group, at):
        to = lax.rem(member + at, MEMBERS)
        return remote(
            back_ref.at[group, to],
            returned_ref.at[group, member],
            back_send.at[group * 7 + at - 1],
            back_recv.at[group * 7 + at - 1],
            (record, to),
        )

    for group in range(2):
        frames_ref[:64, :] = jnp.zeros((64, LANES), F32)
        frames_ref[tail:, :] = jnp.zeros((frames_ref.shape[0] - tail, LANES), F32)
        for at in range(1, MEMBERS):
            signal_copy(group, at).wait_recv()

        def place(of, group=group):
            begin = of * (frame_count + 2) + 64
            packed = got_ref.at[group, of]
            for low, high, skew in (
                (0, 64, 0),
                (64, 160, 1),
                (160, 192, 1),
                (192, 224, 2),
                (224, 256, 2),
            ):
                frames_ref[pl.ds(begin + low + skew, high - low), :GROUP] = unpack(
                    packed, low, high
                ).astype(F32)

        loop(0, MEMBERS, place, 2)

        def widen(row):
            parts = []
            for phase in range(PHASES):
                at = row * PHASES + phase
                part = frames_ref[pl.ds(at + at // BLOCK, 16, stride=BLOCK + 1), :]
                parts.append(part.astype(BF16)[:, :GROUP])
            spread_ref[row] = jnp.concatenate(parts + [jnp.zeros((16, 16), BF16)], axis=1)

        loop(0, STEPS * 2, widen, 11)
        if group == 0:
            outs.first()
        window = jnp.concatenate(
            [
                spread_ref[step : step + SPAN].reshape(SPAN * 16, 2 * LANES)
                for step in range(STEPS)
            ],
            axis=1,
        )
        weights = jnp.concatenate(
            [matrix_ref[group, step * 240 : step * 240 + 240, :] for step in range(STEPS)],
            axis=1,
        )
        total_ref[...] = lax.dot_general(
            window, weights, (((1,), (1,)), ((), ())), preferred_element_type=F32
        )
        bias = row_of(tap_bias_ref)[:, group * GROUP : (group + 1) * GROUP]
        bias = jnp.concatenate([bias] * PHASES, axis=1)

        def activate(row, bias=bias):
            value = total_ref[pl.ds(pl.multiple_of(row * 16, 16), 16), :] + bias
            value = value * (1.0 + lax.erf(value * (0.5**0.5))) * 0.5
            for phase in range(PHASES):
                part = value[:, phase * GROUP : (phase + 1) * GROUP]
                part = jnp.concatenate([part, jnp.zeros((16, LANES - GROUP), F32)], axis=1)
                begin = row * PHASES + phase
                begin = begin + begin // BLOCK
                natural_ref[pl.ds(begin, 16, stride=BLOCK + 1), :] = part

        loop(0, SPAN, activate, 11)

        def pack_back(to, group=group):
            begin = 2 * to * (BLOCK + 1)
            halves = [
                natural_ref[pl.ds(begin + side * (BLOCK + 1), BLOCK), :].astype(BF16)[:, :GROUP]
                for side in range(2)
            ]
            back_ref[group, to] = pack(jnp.concatenate(halves, axis=0))

        loop(0, MEMBERS, pack_back, 4)
        for at in range(1, MEMBERS):
            back_copy(group, at).start()
        returned_ref[group, member] = back_ref[group, member]
        if group == 0:
            rows.third()
    rows.fourth((0, 1, 2, 3))
    outs.second()

    for group in range(2):
        for at in range(1, MEMBERS):
            back_copy(group, at).wait_recv()
    for begin in range(0, frame_count, 32):
        pieces = [
            unpack(returned_ref.at[group, of], begin, begin + 32)
            for of in range(MEMBERS)
            for group in range(2)
        ]
        position = jnp.concatenate(pieces, axis=1)
        hidden = signal_ref[begin : begin + 32, :].astype(F32) + position.astype(F32)
        hidden_ref[begin : begin + 32, :] = hidden
        average = jnp.mean(hidden, axis=-1, keepdims=True)
        centered = hidden - average
        variance = jnp.mean(centered * centered, axis=-1, keepdims=True)
        normed_ref[begin : begin + 32, :] = (
            centered * lax.rsqrt(variance + EPSILON) * row_of(gain_ref) + row_of(shift_ref)
        ).astype(BF16)

    rows.near()
    lane = lax.broadcasted_iota(jnp.int32, (BLOCK, 2 * LANES), 1) - 3 * HEAD
    masks = []
    for block in range(2):
        unlisted = jnp.where(lane >= 0, 1.0, 0.0)
        for at in range(blocks_ref.shape[1]):
            unlisted = jnp.where(lane == jnp.where(lane >= 0, blocks_ref[block, at], -1000), 0.0, unlisted)
        masks.append(unlisted)
    mask = jnp.concatenate(masks, axis=0)

    rest = share - LANES

    def head_copy(source, to, at):
        return remote(
            slab_ref.at[to],
            headed_ref.at[source],
            head_send.at[at],
            head_recv.at[source],
            (record, to),
        )

    def ask_copy(bits):
        to = flip(member, bits)
        return remote(
            asked_ref.at[to],
            asking_ref.at[member],
            ask_send.at[bits - 1],
            ask_recv.at[bits - 1],
            (record, to),
        )

    def chosen_head(at):
        turned = lax.rem(member + at, 4)
        first = jnp.where(at < 4, record, across)
        second = first + 1 - 2 * lax.rem(first, 2)
        quarter = jnp.where(turned < 2, first, second)
        return quarter, lax.rem(turned, 2)

    def project(at):
        quarter, side = chosen_head(at)
        head, tile = quarter + 4 * side, 4 * quarter + 2 * side
        weights = jnp.concatenate([rows_ref[tile], rows_ref[tile + 1]], axis=1)
        slab = jnp.dot(normed_ref[...], weights, preferred_element_type=F32)
        slab = (slab + bias_ref[pl.ds(head, 1), :] + mask).astype(BF16)
        slab_ref[head, :frame_count, :] = slab[:, :LANES]
        slab_ref[head, frame_count:, :] = jnp.concatenate(
            [slab[64 * part : 64 * part + 64, LANES:share] for part in range(4)], axis=1
        )
        asked = slab[:, share:]
        asked_ref[head] = jnp.concatenate(
            [
                asked[:192],
                jnp.concatenate(
                    [asked[192:, part * 32 : part * 32 + 32] for part in range(3)], axis=0
                ),
            ],
            axis=1,
        )

        @pl.when(head != member)
        def _():
            head_copy(member, head, at).start()

        @pl.when(head == member)
        def _():
            headed_ref[member] = slab_ref[head]

    for at in range(4):
        project(at)
    outs.third()
    rows.fourth((4, 5, 6))
    rows.far()
    for at in range(4, 8):
        project(at)
    for bits in (4, 5, 6, 7, 3, 2, 1):
        ask_copy(bits).start()
    asking_ref[member] = asked_ref[member]

    place_row = lax.broadcasted_iota(jnp.int32, (BLOCK, frames), 0)
    place_column = lax.broadcasted_iota(jnp.int32, (BLOCK, frames), 1)
    for at in range(GLOBALS):
        chosen_ref[at * BLOCK : (at + 1) * BLOCK, :] = jnp.where(
            place_row + globals_ref[at] * BLOCK == place_column, 1.0, 0.0
        ).astype(BF16)

    def arrange(of):
        slab = headed_ref[of]
        begin = pl.multiple_of(of * frame_count, 256)
        row = lax.broadcasted_iota(jnp.int32, (frame_count, 16), 0)
        block = 2 * of + jnp.where(row >= BLOCK, 1, 0)
        here = lax.broadcasted_iota(jnp.int32, (frame_count, 16), 1) == block
        keys_ref[pl.ds(begin, frame_count), :] = jnp.concatenate(
            [
                slab[:frame_count, :HEAD],
                jnp.where(here, -BIG, 0.0).astype(BF16),
                jnp.zeros((frame_count, 32), BF16),
            ],
            axis=1,
        )
        side = jnp.concatenate(
            [slab[frame_count:, rest * part : rest * part + rest] for part in range(4)], axis=0
        )
        values_ref[pl.ds(begin, frame_count), :] = jnp.concatenate(
            [
                slab[:frame_count, HEAD:],
                side,
                jnp.ones((frame_count, 16), BF16),
                jnp.zeros((frame_count, 32), BF16),
            ],
            axis=1,
        )

    arrange(member)
    for at in range(1, MEMBERS):
        of = lax.rem(member + at, MEMBERS)
        head_copy(of, member, 0).wait_recv()
        arrange(of)
    lane = lax.broadcasted_iota(jnp.int32, (BLOCK, LANES), 1)
    picked = jnp.dot(
        chosen_ref[...],
        jnp.concatenate([keys_ref[:frames, :], values_ref[:frames, :]], axis=1),
        preferred_element_type=F32,
    )
    for at in range(GLOBALS):
        rows_at = slice(at * BLOCK, (at + 1) * BLOCK)
        keys_ref[frames + at * BLOCK : frames + (at + 1) * BLOCK, :] = jnp.where(
            lane < HEAD,
            picked[rows_at, :LANES],
            jnp.where(lane == HEAD + 16 + globals_ref[at], -BIG, 0.0),
        ).astype(BF16)
        values_ref[frames + at * BLOCK : frames + (at + 1) * BLOCK, :] = picked[
            rows_at, LANES:
        ].astype(BF16)

    factor = (1.0 / math.sqrt(HEAD)) * math.log2(math.e)

    def context_copy(bits):
        to = flip(member, bits)
        return remote(
            context_ref.at[to],
            contexts_ref.at[member],
            context_send.at[bits - 1],
            context_recv.at[bits - 1],
            (record, to),
        )

    def attend_tile(of):
        asked = asking_ref[of]
        last = jnp.concatenate(
            [asked[64 * part : 64 * part + 64, 96:] for part in range(3)], axis=1
        )
        asked = jnp.concatenate([asked[:, :96], last], axis=0)
        queries = jnp.concatenate(
            [asked, 1.0 - asked[:, HEAD:], jnp.zeros((frame_count, 16), BF16)], axis=1
        )
        low = jnp.minimum(jnp.maximum(2 * of - 2, 0), 10)
        window = pl.ds(pl.multiple_of(low * BLOCK, BLOCK), 6 * BLOCK)
        keys = jnp.concatenate([keys_ref[window, :], keys_ref[frames:, :]], axis=0)
        scores = lax.dot_general(
            queries, keys, (((1,), (1,)), ((), ())), preferred_element_type=F32
        )
        peak = jnp.max(scores, axis=1, keepdims=True)
        weights = jnp.exp2(scores * factor - peak * factor).astype(BF16)
        values = jnp.concatenate([values_ref[window, :], values_ref[frames:, :]], axis=0)
        summed = jnp.dot(weights, values, preferred_element_type=F32)
        return pack((summed[:, :HEAD] / summed[:, HEAD : HEAD + 1]).astype(BF16))

    contexts_ref[member] = attend_tile(member)
    for pair in ((1,), (2, 3), (4, 5), (6, 7)):
        for bits in pair:
            ask_copy(bits).wait_recv()
        for bits in pair:
            of = flip(member, bits)
            context_ref[of] = attend_tile(of)
            context_copy(bits).start()
    outs.fourth(range(7))

    for at in range(1, MEMBERS):
        context_copy(at).wait_recv()
    outs.near()
    outs.far()
    context = jnp.concatenate(
        [
            jnp.concatenate(
                [
                    unpack(contexts_ref.at[of], 0, 160),
                    unpack(contexts_ref.at[of], 160, 224),
                    unpack(contexts_ref.at[of], 224, 256),
                ],
                axis=0,
            )
            for of in range(HEADS)
        ],
        axis=1,
    )
    columns = jnp.concatenate(
        [
            jnp.concatenate(
                [output_rows_ref[of, share * at : share * at + share, :] for at in range(5)], axis=1
            )
            for of in range(MEMBERS)
        ],
        axis=0,
    )
    projected = lax.dot_general(
        context, columns, (((1,), (1,)), ((), ())), preferred_element_type=F32
    )
    out_ref[...] = (hidden_ref[...] + projected + row_of(output_bias_ref)).astype(BF16)

    for at in range(1, MEMBERS):
        for group in range(2):
            signal_copy(group, at).wait_send()
            back_copy(group, at).wait_send()
        ask_copy(at).wait_send()
        context_copy(at).wait_send()
    for at in range(MEMBERS):
        quarter, side = chosen_head(at)

        @pl.when(quarter + 4 * side != member)
        def _(head=quarter + 4 * side, at=at):
            head_copy(member, head, at).wait_send()

    rows.sent()
    outs.sent()


def by_heads(
    signal,
    position_kernel,
    position_bias,
    layer_gain,
    layer_shift,
    query_weight,
    query_bias,
    key_weight,
    value_weight,
    value_bias,
    output_weight,
    output_bias,
    key_blocks,
    global_blocks,
):
    frame_count, width = signal.shape
    frames = MEMBERS * frame_count
    share = 2 * GROUP
    vmem = pl.BlockSpec(memory_space=pltpu.VMEM)
    smem = pl.BlockSpec(memory_space=pltpu.SMEM)
    dma = pltpu.SemaphoreType.DMA
    return pl.pallas_call(
        whole_kernel,
        out_shape=jax.ShapeDtypeStruct((frame_count, width), BF16),
        in_specs=[smem, smem, vmem, pl.BlockSpec(memory_space=pl.ANY)] + [vmem] * 10,
        out_specs=vmem,
        scratch_shapes=[
            pltpu.VMEM((share, GROUP, LANES), BF16),
            pltpu.VMEM((share * PADDED, LANES), F32),
            pltpu.VMEM((2, STEPS * PHASES * GROUP, 2 * LANES), BF16),
            pltpu.VMEM((2, MEMBERS, PACKED, LANES), BF16),
            pltpu.VMEM((2, MEMBERS, PACKED, LANES), BF16),
            pltpu.VMEM((frames + 160, LANES), F32),
            pltpu.VMEM((STEPS * 2, 16, 2 * LANES), BF16),
            pltpu.VMEM((SPAN * 16, PHASES * GROUP), F32),
            pltpu.VMEM((frames + 32, LANES), F32),
            pltpu.VMEM((2, MEMBERS, PACKED, LANES), BF16),
            pltpu.VMEM((2, MEMBERS, PACKED, LANES), BF16),
            pltpu.VMEM((frame_count, width), F32),
            pltpu.VMEM((frame_count, width), BF16),
            pltpu.VMEM((2 * HEADS, width, LANES), BF16),
            pltpu.VMEM((MEMBERS, 832, LANES), BF16),
            pltpu.VMEM((HEADS, 2 * LANES), F32),
            pltpu.VMEM((MEMBERS, frame_count + 64, LANES), BF16),
            pltpu.VMEM((MEMBERS, frame_count + 64, LANES), BF16),
            pltpu.VMEM((MEMBERS, 192, LANES), BF16),
            pltpu.VMEM((MEMBERS, 192, LANES), BF16),
            pltpu.VMEM((frames + GLOBALS * BLOCK, LANES), BF16),
            pltpu.VMEM((frames + GLOBALS * BLOCK, LANES), BF16),
            pltpu.VMEM((GLOBALS * BLOCK, frames), BF16),
            pltpu.VMEM((MEMBERS, PACKED, LANES), BF16),
            pltpu.VMEM((MEMBERS, PACKED, LANES), BF16),
            dma,
            dma((14,)),
            dma((14,)),
            dma((14,)),
            dma((14,)),
            dma((28,)),
            dma((28,)),
            dma((28,)),
            dma((28,)),
            dma((8,)),
            dma((8,)),
            dma((7,)),
            dma((7,)),
            dma((7,)),
            dma((7,)),
        ],
        compiler_params=pltpu.CompilerParams(
            collective_id=0, has_side_effects=True, vmem_limit_bytes=60 * 1024 * 1024
        ),
    )(
        key_blocks,
        global_blocks,
        signal,
        position_kernel,
        position_bias,
        layer_gain,
        layer_shift,
        query_weight,
        key_weight,
        value_weight,
        query_bias,
        value_bias,
        output_weight.T,
        output_bias,
    )


def body(*operands):
    share, width, taps = operands[1].shape
    fits = lax.axis_size("tm") == MEMBERS and lax.axis_size("rec") == QUARTERS
    fits = fits and (share, width, taps) == (2 * GROUP, GROUP, LANES)
    fits = fits and operands[0].shape[0] == 2 * BLOCK
    return (by_heads if fits else general)(*operands)


def solution(mesh):
    placed = (
        P(("rec", "tm"), None),
        P("tm", None, None),
        P("tm"),
        P(),
        P(),
        P("tm", None),
        P(),
        P("tm", None),
        P("tm", None),
        P(),
        P(None, "tm"),
        P(),
        P(("rec", "tm"), None),
        P("rec"),
    )
    return jax.shard_map(
        body, mesh=mesh, in_specs=placed, out_specs=P(("rec", "tm"), None), check_vma=False
    )
```

```python
import math

import jax
import jax.numpy as jnp
import numpy as np
from jax import lax
from jax.experimental import pallas as pl
from jax.experimental.pallas import tpu as pltpu
from jax.sharding import PartitionSpec as P

HEAD = 80
HEADS = 8
BLOCK = 128
GLOBALS = 4


EPSILON = 1e-05


def attend(queries, key_rows, value_rows, allowed):
    block_count, row_count, heads_width = queries.shape
    query_heads = queries.reshape(block_count, row_count, HEADS, HEAD)
    key_heads = key_rows.reshape(block_count, key_rows.shape[1], HEADS, HEAD)
    value_heads = value_rows.reshape(block_count, value_rows.shape[1], HEADS, HEAD)
    scores = jnp.einsum(
        "bqhe,bkhe->bhqk", query_heads, key_heads, preferred_element_type=jnp.float32
    ) * (1.0 / math.sqrt(HEAD))
    scores = jnp.where(allowed[:, None, None, :], scores, -jnp.inf)
    row_max = jnp.max(scores, axis=-1, keepdims=True)
    weights = jnp.exp(scores - row_max)
    row_total = jnp.sum(weights, axis=-1)
    probability = weights.astype(jnp.bfloat16)
    context_sum = jnp.einsum(
        "bhqk,bkhe->bqhe", probability, value_heads, preferred_element_type=jnp.float32
    )
    context = context_sum / jnp.transpose(row_total, (0, 2, 1))[..., None]
    return context.reshape(block_count, row_count, heads_width).astype(jnp.bfloat16)


def general(
    signal,
    position_kernel,
    position_bias,
    layer_gain,
    layer_shift,
    query_weight,
    query_bias,
    key_weight,
    value_weight,
    value_bias,
    output_weight,
    output_bias,
    key_blocks,
    global_blocks,
):
    devices = lax.axis_size("tm")
    frame_count, model_width = signal.shape
    channel_share, group_width, kernel_taps = position_kernel.shape
    inner_width = max(channel_share, group_width)
    folded = signal.T
    if channel_share >= group_width:
        outgoing = folded.reshape(devices, channel_share, frame_count)
    else:
        start_groups = np.arange(devices) * channel_share // group_width
        grouped = folded.reshape(model_width // group_width, group_width, frame_count)
        outgoing = jnp.stack(
            [grouped[at * channel_share // group_width] for at in range(devices)]
        )
    incoming = lax.all_to_all(outgoing, "tm", split_axis=0, concat_axis=2, tiled=True)
    outputs = channel_share if channel_share < group_width else group_width
    spread = jnp.pad(
        incoming.reshape(inner_width // group_width, group_width, -1),
        ((0, 0), (0, 0), (kernel_taps // 2, kernel_taps // 2 - 1)),
    )
    frames = incoming.shape[-1]
    by_tap = position_kernel.reshape(-1, outputs, group_width, kernel_taps).transpose(3, 0, 1, 2)

    def tap(at, total):
        window = lax.dynamic_slice_in_dim(spread, at, frames, axis=2)
        return total + jnp.einsum(
            "goi,git->got", by_tap[at], window, preferred_element_type=jnp.float32
        )

    response = lax.fori_loop(
        0, kernel_taps, tap, jnp.zeros((spread.shape[0], outputs, frames), jnp.float32)
    ).reshape(channel_share, frames)
    position = jax.nn.gelu(response + position_bias[:, None], approximate=False).astype(
        jnp.bfloat16
    )
    returned = lax.all_to_all(position, "tm", split_axis=1, concat_axis=0, tiled=True)
    hidden = signal.astype(jnp.float32) + returned.T.astype(jnp.float32)
    average = jnp.mean(hidden, axis=-1, keepdims=True)
    centered = hidden - average
    variance = jnp.mean(centered * centered, axis=-1, keepdims=True)
    normed = (centered * lax.rsqrt(variance + EPSILON) * layer_gain + layer_shift).astype(
        jnp.bfloat16
    )
    heads_width = query_weight.shape[1]
    zero_sums = jnp.zeros((frame_count, heads_width), jnp.float32)
    totals = (zero_sums, zero_sums, zero_sums)
    pieces = (
        lax.all_gather(query_weight, "tm", axis=0, tiled=True),
        lax.all_gather(key_weight, "tm", axis=0, tiled=True),
        lax.all_gather(value_weight, "tm", axis=0, tiled=True),
    )
    columns = lax.slice_in_dim(normed, 0, pieces[0].shape[0], axis=1)
    query_sum, key_sum, value_sum = tuple(
        (
            running + jnp.dot(columns, weight_rows, preferred_element_type=jnp.float32)
            for running, weight_rows in zip(totals, pieces)
        )
    )
    queries = (query_sum + query_bias).astype(jnp.bfloat16)
    key_part = key_sum.astype(jnp.bfloat16)
    value_part = (value_sum + value_bias).astype(jnp.bfloat16)
    key_value = jnp.stack((key_part, value_part), axis=1)
    per_device = frame_count // BLOCK
    repeated = jnp.any(global_blocks[None, :, None] == key_blocks[:, None, :], axis=-1)
    whole = lax.all_gather(key_value, "tm", axis=0, tiled=True)
    block_ids = jnp.concatenate(
        [key_blocks, jnp.broadcast_to(global_blocks[None, :], (per_device, GLOBALS))], axis=1
    )
    allowed = jnp.concatenate([key_blocks >= 0, jnp.logical_not(repeated)], axis=1)
    table = whole.reshape(-1, BLOCK, 2, heads_width)
    chosen = jnp.maximum(block_ids, 0)
    candidates = jnp.stack(
        [
            jnp.stack(
                [
                    lax.dynamic_index_in_dim(table, chosen[row, at], 0, keepdims=False)
                    for at in range(chosen.shape[1])
                ]
            )
            for row in range(per_device)
        ]
    )
    key_rows = candidates[:, :, :, 0].reshape(per_device, -1, heads_width)
    value_rows = candidates[:, :, :, 1].reshape(per_device, -1, heads_width)
    allowed_rows = jnp.repeat(allowed, BLOCK, axis=1)
    context = attend(
        queries.reshape(per_device, BLOCK, heads_width), key_rows, value_rows, allowed_rows
    ).reshape(frame_count, heads_width)
    projected = jnp.dot(
        context,
        lax.all_gather(output_weight, "tm", axis=1, tiled=True),
        preferred_element_type=jnp.float32,
    )
    return (hidden + projected + output_bias).astype(jnp.bfloat16)


PHASES = 3
GROUP = 80
MEMBERS = 8
QUARTERS = 4
LANES = 128
STEP = 4
STEPS = 44
SPAN = 43
PACKED = 160
PADDED = 145
MESH = pl.DeviceIdType.MESH
BIG = 1e30
F32 = jnp.float32
BF16 = jnp.bfloat16


def flip(member, bits):
    low = bits % 4
    if low == 1:
        turned = member + 1 - 2 * lax.rem(member, 2)
    elif low == 2:
        turned = member + 2 - 4 * lax.rem(lax.div(member, 2), 2)
    elif low == 3:
        turned = 4 * lax.div(member, 4) + 3 - lax.rem(member, 4)
    else:
        turned = member
    return lax.rem(turned + 4, MEMBERS) if bits >= 4 else turned


def loop(begin, end, body, unroll):
    turns = (end - begin) // unroll

    def turn(step, _):
        for at in range(unroll):
            body(begin + step * unroll + at)
        return 0

    if turns > 1:
        lax.fori_loop(0, turns, turn, 0)
    else:
        turns = 0
    for at in range(begin + turns * unroll, end):
        body(at)


def row_of(ref):
    return ref[...].reshape(1, -1)


def pack(value):
    return jnp.concatenate(
        [
            jnp.concatenate([value[:96], value[160:, :48]], axis=1),
            jnp.concatenate([value[96:128], value[160:192, 48:], value[224:, 48:64]], axis=1),
            jnp.concatenate([value[128:160], value[192:224, 48:], value[224:, 64:]], axis=1),
        ],
        axis=0,
    )


def unpack(ref, begin, end):
    if end <= 160:
        return ref[begin:end, :GROUP]
    if end <= 224:
        return jnp.concatenate(
            [ref[begin - 160 : end - 160, GROUP:], ref[begin - 64 : end - 64, GROUP:112]], axis=1
        )
    return jnp.concatenate(
        [ref[64:96, GROUP:], ref[96:128, 112:], ref[128:160, 112:]], axis=1
    )


def remote(source, target, send, receive, device):
    return pltpu.make_async_remote_copy(
        src_ref=source,
        dst_ref=target,
        send_sem=send,
        recv_sem=receive,
        device_id=device,
        device_id_type=MESH,
    )


class Spread:
    def __init__(self, piece, record, member, sends, receives):
        self.piece, self.record, self.member = piece, record, member
        self.sends, self.receives = sends, receives
        self.across = lax.rem(record + 2, QUARTERS)
        self.beside = record + 1 - 2 * lax.rem(record, 2)

    def copy(self, at, share, quarter, device):
        ref = self.piece(share, quarter)
        return remote(ref, ref, self.sends.at[at], self.receives.at[at], device)

    def plane(self, at):
        bits = at + 1
        if bits <= 4:
            return self.copy(at, self.member, self.record, (self.record, flip(self.member, bits)))
        share = flip(self.member, 4)
        return self.copy(at, share, self.record, (self.record, flip(self.member, bits - 4)))

    def other(self, at):
        return self.copy(7 + at, flip(self.member, at + 1), self.record, (self.across, self.member))

    def core(self, at):
        return self.copy(14 + at, flip(self.member, at + 1), self.record, (self.beside, self.member))

    def last(self, at):
        return self.copy(21 + at, flip(self.member, at + 1), self.across, (self.beside, self.member))

    def first(self):
        for at in (3, 0, 1, 2):
            self.plane(at).start()

    def second(self):
        for at in (0, 1, 2):
            self.plane(at).wait_recv()
            self.other(at).start()
            self.core(at).start()

    def second_far(self):
        self.plane(3).wait_recv()
        for at in (4, 5, 6):
            self.plane(at).start()
        self.other(3).start()
        self.core(3).start()

    def third(self):
        for at in (4, 5, 6):
            self.plane(at).wait_recv()
            self.other(at).start()
            self.core(at).start()

    def fourth(self, which):
        for at in which:
            self.other(at).wait_recv()
            self.last(at).start()

    def near(self):
        for at in range(7):
            self.core(at).wait_recv()

    def far(self):
        for at in range(7):
            self.last(at).wait_recv()

    def sent(self):
        for at in range(7):
            for copy in (self.plane(at), self.other(at), self.core(at), self.last(at)):
                copy.wait_send()


def whole_kernel(
    blocks_ref,
    globals_ref,
    signal_hbm,
    taps_hbm,
    tap_bias_ref,
    gain_ref,
    shift_ref,
    query_hbm,
    key_hbm,
    value_hbm,
    query_bias_ref,
    value_bias_ref,
    output_hbm,
    output_bias_ref,
    out_ref,
    signal_ref,
    query_ref,
    key_ref,
    value_ref,
    output_ref,
    taps_ref,
    turned_ref,
    matrix_ref,
    send_ref,
    got_ref,
    frames_ref,
    spread_ref,
    total_ref,
    natural_ref,
    back_ref,
    returned_ref,
    hidden_ref,
    normed_ref,
    rows_ref,
    output_rows_ref,
    bias_ref,
    slab_ref,
    headed_ref,
    asked_ref,
    asking_ref,
    keys_ref,
    values_ref,
    chosen_ref,
    context_ref,
    contexts_ref,
    load_sem,
    signal_send,
    signal_recv,
    back_send,
    back_recv,
    rows_send,
    rows_recv,
    outs_send,
    outs_recv,
    head_send,
    head_recv,
    ask_send,
    ask_recv,
    context_send,
    context_recv,
):
    record, member = lax.axis_index("rec"), lax.axis_index("tm")
    loads = [
        pltpu.make_async_copy(source, target, load_sem.at[at])
        for at, (source, target) in enumerate(
            (
                (signal_hbm, signal_ref),
                (query_hbm, query_ref),
                (key_hbm, key_ref),
                (value_hbm, value_ref),
                (taps_hbm, taps_ref),
                (output_hbm, output_ref),
            )
        )
    ]
    for load in loads:
        load.start()

    barrier = pltpu.get_barrier_semaphore()
    across = lax.rem(record + 2, QUARTERS)
    beside = record + 1 - 2 * lax.rem(record, 2)
    peers = [(record, lax.rem(member + at, MEMBERS)) for at in range(1, MEMBERS)]
    for peer in peers + [(across, member), (beside, member)]:
        pl.semaphore_signal(barrier, inc=1, device_id=peer, device_id_type=MESH)

    loads[0].wait()
    frame_count = signal_ref.shape[0]
    share = 2 * GROUP
    rest = share - LANES

    def signal_copy(group, at):
        to = lax.rem(member + at, MEMBERS)
        return remote(
            send_ref.at[group, to],
            got_ref.at[group, member],
            signal_send.at[group * 7 + at - 1],
            signal_recv.at[group * 7 + at - 1],
            (record, to),
        )

    def send_signal(group):
        for to in range(MEMBERS):
            begin = to * share + group * GROUP
            send_ref[group, to] = pack(signal_ref[:, begin : begin + GROUP])
        for at in (4, 3, 5, 2, 6, 1, 7):
            signal_copy(group, at).start()
        got_ref[group, member] = send_ref[group, member]


    for load in loads[1:4]:
        load.wait()
    mine = pl.ds(pl.multiple_of(member * share, 32), share)
    for head in range(HEADS):
        columns = slice(head * HEAD, (head + 1) * HEAD)
        joined = jnp.concatenate(
            [
                key_ref[:, columns],
                value_ref[:, columns],
                query_ref[:, columns],
                jnp.zeros((share, 16), BF16),
            ],
            axis=1,
        )
        tile = head % QUARTERS * 4 + head // QUARTERS * 2
        rows_ref[tile, mine, :] = joined[:, :LANES]
        rows_ref[tile + 1, mine, :] = joined[:, LANES:]
    def rows_piece(of, quarter):
        return rows_ref.at[
            pl.ds(quarter * 4, 4), pl.ds(pl.multiple_of(of * share, 32), share), :
        ]

    def output_piece(of, quarter):
        return output_rows_ref.at[of, pl.ds(pl.multiple_of(quarter * 208, 16), 208), :]

    rows = Spread(rows_piece, record, member, rows_send, rows_recv)
    outs = Spread(output_piece, record, member, outs_send, outs_recv)
    pl.semaphore_wait(barrier, 9)
    rows.first()
    send_signal(0)

    heads_width = HEADS * HEAD
    loads[5].wait()
    for at in range(heads_width // LANES):
        output_rows_ref[member, share * at : share * at + share, :] = output_ref[
            :, at * LANES : (at + 1) * LANES
        ]
    output_rows_ref[member, 5 * share :, :] = jnp.zeros((32, LANES), BF16)
    empty = jnp.zeros((1, HEAD), F32)
    for head in range(HEADS):
        columns = slice(head * HEAD, (head + 1) * HEAD)
        bias_ref[head : head + 1, :] = jnp.concatenate(
            [
                empty,
                row_of(value_bias_ref)[:, columns],
                row_of(query_bias_ref)[:, columns],
                empty[:, :16],
            ],
            axis=1,
        )


    loads[4].wait()
    empty = jnp.zeros((8, LANES), F32)

    def turn(channel):
        begin = channel * PADDED
        turned_ref[pl.ds(begin, 8), :] = empty
        turned_ref[pl.ds(begin + 136, 8), :] = empty
        turned_ref[pl.ds(begin + 8, LANES), :GROUP] = jnp.transpose(taps_ref[channel]).astype(F32)

    loop(0, share, turn, 16)
    send_signal(1)

    def lay(step):
        for group in range(2):
            taps = [
                turned_ref[
                    pl.ds(group * GROUP * PADDED + step * 3 + 6 + at, GROUP, stride=PADDED), :
                ].astype(BF16)[:, :GROUP]
                for at in range(5)
            ]
            for phase in range(PHASES):
                row = jnp.concatenate(
                    taps[2 - phase : 5 - phase] + [jnp.zeros((GROUP, 16), BF16)], axis=1
                )
                begin = pl.multiple_of((step * PHASES + phase) * GROUP, 16)
                matrix_ref[group, pl.ds(begin, GROUP), :] = row

    rows.second()
    loop(0, STEPS, lay, 4)
    rows.second_far()

    frames = MEMBERS * frame_count
    tail = 64 + frames + (64 + frames) // BLOCK

    def back_copy(group, at):
        to = lax.rem(member + at, MEMBERS)
        return remote(
            back_ref.at[group, to],
            returned_ref.at[group, member],
            back_send.at[group * 7 + at - 1],
            back_recv.at[group * 7 + at - 1],
            (record, to),
        )

    for group in range(2):
        frames_ref[:64, :] = jnp.zeros((64, LANES), F32)
        frames_ref[tail:, :] = jnp.zeros((frames_ref.shape[0] - tail, LANES), F32)
        for at in range(1, MEMBERS):
            signal_copy(group, at).wait_recv()

        def place(of, group=group):
            begin = of * (frame_count + 2) + 64
            packed = got_ref.at[group, of]
            for low, high, skew in (
                (0, 64, 0),
                (64, 160, 1),
                (160, 192, 1),
                (192, 224, 2),
                (224, 256, 2),
            ):
                frames_ref[pl.ds(begin + low + skew, high - low), :GROUP] = unpack(
                    packed, low, high
                ).astype(F32)

        loop(0, MEMBERS, place, 2)

        def widen(row):
            parts = []
            for phase in range(PHASES):
                at = row * PHASES + phase
                part = frames_ref[pl.ds(at + at // BLOCK, 16, stride=BLOCK + 1), :]
                parts.append(part.astype(BF16)[:, :GROUP])
            spread_ref[row] = jnp.concatenate(parts + [jnp.zeros((16, 16), BF16)], axis=1)

        loop(0, STEPS * 2, widen, 11)
        if group == 0:
            outs.first()
        window = jnp.concatenate(
            [
                spread_ref[step : step + SPAN].reshape(SPAN * 16, 2 * LANES)
                for step in range(STEPS)
            ],
            axis=1,
        )
        weights = jnp.concatenate(
            [matrix_ref[group, step * 240 : step * 240 + 240, :] for step in range(STEPS)],
            axis=1,
        )
        total_ref[...] = lax.dot_general(
            window, weights, (((1,), (1,)), ((), ())), preferred_element_type=F32
        )
        bias = row_of(tap_bias_ref)[:, group * GROUP : (group + 1) * GROUP]
        bias = jnp.concatenate([bias] * PHASES, axis=1)

        def activate(row, bias=bias):
            value = total_ref[pl.ds(pl.multiple_of(row * 16, 16), 16), :] + bias
            value = value * (1.0 + lax.erf(value * (0.5**0.5))) * 0.5
            for phase in range(PHASES):
                part = value[:, phase * GROUP : (phase + 1) * GROUP]
                part = jnp.concatenate([part, jnp.zeros((16, LANES - GROUP), F32)], axis=1)
                begin = row * PHASES + phase
                begin = begin + begin // BLOCK
                natural_ref[pl.ds(begin, 16, stride=BLOCK + 1), :] = part

        loop(0, SPAN, activate, 11)

        def pack_back(to, group=group):
            begin = 2 * to * (BLOCK + 1)
            halves = [
                natural_ref[pl.ds(begin + side * (BLOCK + 1), BLOCK), :].astype(BF16)[:, :GROUP]
                for side in range(2)
            ]
            back_ref[group, to] = pack(jnp.concatenate(halves, axis=0))

        loop(0, MEMBERS, pack_back, 4)
        for at in (4, 3, 5, 2, 6, 1, 7):
            back_copy(group, at).start()
        returned_ref[group, member] = back_ref[group, member]
        if group == 0:
            rows.third()

    for group in range(2):
        for at in range(1, MEMBERS):
            back_copy(group, at).wait_recv()
    for begin in range(0, frame_count, 32):
        pieces = [
            unpack(returned_ref.at[group, of], begin, begin + 32)
            for of in range(MEMBERS)
            for group in range(2)
        ]
        position = jnp.concatenate(pieces, axis=1)
        hidden = signal_ref[begin : begin + 32, :].astype(F32) + position.astype(F32)
        hidden_ref[begin : begin + 32, :] = hidden
        average = jnp.mean(hidden, axis=-1, keepdims=True)
        centered = hidden - average
        variance = jnp.mean(centered * centered, axis=-1, keepdims=True)
        normed_ref[begin : begin + 32, :] = (
            centered * lax.rsqrt(variance + EPSILON) * row_of(gain_ref) + row_of(shift_ref)
        ).astype(BF16)

    rows.fourth((0, 1, 2, 3))
    rows.near()
    lane = lax.broadcasted_iota(jnp.int32, (BLOCK, 2 * LANES), 1) - 3 * HEAD
    masks = []
    for block in range(2):
        unlisted = jnp.where(lane >= 0, 1.0, 0.0)
        for at in range(blocks_ref.shape[1]):
            unlisted = jnp.where(lane == jnp.where(lane >= 0, blocks_ref[block, at], -1000), 0.0, unlisted)
        masks.append(unlisted)
    mask = jnp.concatenate(masks, axis=0)

    rest = share - LANES

    def head_copy(source, to, at):
        return remote(
            slab_ref.at[to],
            headed_ref.at[source],
            head_send.at[at],
            head_recv.at[source],
            (record, to),
        )

    def ask_copy(bits):
        to = flip(member, bits)
        return remote(
            asked_ref.at[to],
            asking_ref.at[member],
            ask_send.at[bits - 1],
            ask_recv.at[bits - 1],
            (record, to),
        )

    def chosen_head(at):
        turned = lax.rem(member + at, 4)
        first = jnp.where(at < 4, record, across)
        second = first + 1 - 2 * lax.rem(first, 2)
        quarter = jnp.where(turned < 2, first, second)
        return quarter, lax.rem(turned, 2)

    def project(at):
        quarter, side = chosen_head(at)
        head, tile = quarter + 4 * side, 4 * quarter + 2 * side
        weights = jnp.concatenate([rows_ref[tile], rows_ref[tile + 1]], axis=1)
        slab = jnp.dot(normed_ref[...], weights, preferred_element_type=F32)
        slab = (slab + bias_ref[pl.ds(head, 1), :] + mask).astype(BF16)
        slab_ref[head, :frame_count, :] = slab[:, :LANES]
        slab_ref[head, frame_count:, :] = jnp.concatenate(
            [slab[64 * part : 64 * part + 64, LANES:share] for part in range(4)], axis=1
        )
        asked = slab[:, share:]
        asked_ref[head] = jnp.concatenate(
            [
                asked[:192],
                jnp.concatenate(
                    [asked[192:, part * 32 : part * 32 + 32] for part in range(3)], axis=0
                ),
            ],
            axis=1,
        )

        @pl.when(head != member)
        def _():
            head_copy(member, head, at).start()

        @pl.when(head == member)
        def _():
            headed_ref[member] = slab_ref[head]

    for at in range(4):
        project(at)
    rows.fourth((4, 5, 6))
    outs.second()
    outs.second_far()
    rows.far()
    for at in range(4, 8):
        project(at)
    for bits in (4, 5, 6, 7, 3, 2, 1):
        ask_copy(bits).start()
    asking_ref[member] = asked_ref[member]
    outs.third()

    place_row = lax.broadcasted_iota(jnp.int32, (BLOCK, frames), 0)
    place_column = lax.broadcasted_iota(jnp.int32, (BLOCK, frames), 1)
    for at in range(GLOBALS):
        chosen_ref[at * BLOCK : (at + 1) * BLOCK, :] = jnp.where(
            place_row + globals_ref[at] * BLOCK == place_column, 1.0, 0.0
        ).astype(BF16)

    def arrange(of):
        slab = headed_ref[of]
        begin = pl.multiple_of(of * frame_count, 256)
        row = lax.broadcasted_iota(jnp.int32, (frame_count, 16), 0)
        block = 2 * of + jnp.where(row >= BLOCK, 1, 0)
        here = lax.broadcasted_iota(jnp.int32, (frame_count, 16), 1) == block
        keys_ref[pl.ds(begin, frame_count), :] = jnp.concatenate(
            [
                slab[:frame_count, :HEAD],
                jnp.where(here, -BIG, 0.0).astype(BF16),
                jnp.zeros((frame_count, 32), BF16),
            ],
            axis=1,
        )
        side = jnp.concatenate(
            [slab[frame_count:, rest * part : rest * part + rest] for part in range(4)], axis=0
        )
        values_ref[pl.ds(begin, frame_count), :] = jnp.concatenate(
            [
                slab[:frame_count, HEAD:],
                side,
                jnp.ones((frame_count, 16), BF16),
                jnp.zeros((frame_count, 32), BF16),
            ],
            axis=1,
        )

    arrange(member)
    for at in range(1, MEMBERS):
        of = lax.rem(member + at, MEMBERS)
        head_copy(of, member, 0).wait_recv()
        arrange(of)
    lane = lax.broadcasted_iota(jnp.int32, (BLOCK, LANES), 1)
    picked = jnp.dot(
        chosen_ref[...],
        jnp.concatenate([keys_ref[:frames, :], values_ref[:frames, :]], axis=1),
        preferred_element_type=F32,
    )
    for at in range(GLOBALS):
        rows_at = slice(at * BLOCK, (at + 1) * BLOCK)
        keys_ref[frames + at * BLOCK : frames + (at + 1) * BLOCK, :] = jnp.where(
            lane < HEAD,
            picked[rows_at, :LANES],
            jnp.where(lane == HEAD + 16 + globals_ref[at], -BIG, 0.0),
        ).astype(BF16)
        values_ref[frames + at * BLOCK : frames + (at + 1) * BLOCK, :] = picked[
            rows_at, LANES:
        ].astype(BF16)

    factor = (1.0 / math.sqrt(HEAD)) * math.log2(math.e)

    def context_copy(bits):
        to = flip(member, bits)
        return remote(
            context_ref.at[to],
            contexts_ref.at[member],
            context_send.at[bits - 1],
            context_recv.at[bits - 1],
            (record, to),
        )

    def attend_tile(of):
        asked = asking_ref[of]
        last = jnp.concatenate(
            [asked[64 * part : 64 * part + 64, 96:] for part in range(3)], axis=1
        )
        asked = jnp.concatenate([asked[:, :96], last], axis=0)
        queries = jnp.concatenate(
            [asked, 1.0 - asked[:, HEAD:], jnp.zeros((frame_count, 16), BF16)], axis=1
        )
        low = jnp.minimum(jnp.maximum(2 * of - 2, 0), 10)
        window = pl.ds(pl.multiple_of(low * BLOCK, BLOCK), 6 * BLOCK)
        keys = jnp.concatenate([keys_ref[window, :], keys_ref[frames:, :]], axis=0)
        scores = lax.dot_general(
            queries, keys, (((1,), (1,)), ((), ())), preferred_element_type=F32
        )
        peak = jnp.max(scores, axis=1, keepdims=True)
        weights = jnp.exp2(scores * factor - peak * factor).astype(BF16)
        values = jnp.concatenate([values_ref[window, :], values_ref[frames:, :]], axis=0)
        summed = jnp.dot(weights, values, preferred_element_type=F32)
        return pack((summed[:, :HEAD] / summed[:, HEAD : HEAD + 1]).astype(BF16))

    contexts_ref[member] = attend_tile(member)
    for pair in ((1,), (2, 3), (4, 5), (6, 7)):
        for bits in pair:
            ask_copy(bits).wait_recv()
        for bits in pair:
            of = flip(member, bits)
            context_ref[of] = attend_tile(of)
            context_copy(bits).start()
    outs.fourth(range(7))

    for at in range(1, MEMBERS):
        context_copy(at).wait_recv()
    outs.near()
    outs.far()
    context = jnp.concatenate(
        [
            jnp.concatenate(
                [
                    unpack(contexts_ref.at[of], 0, 160),
                    unpack(contexts_ref.at[of], 160, 224),
                    unpack(contexts_ref.at[of], 224, 256),
                ],
                axis=0,
            )
            for of in range(HEADS)
        ],
        axis=1,
    )
    columns = jnp.concatenate(
        [
            jnp.concatenate(
                [output_rows_ref[of, share * at : share * at + share, :] for at in range(5)], axis=1
            )
            for of in range(MEMBERS)
        ],
        axis=0,
    )
    projected = lax.dot_general(
        context, columns, (((1,), (1,)), ((), ())), preferred_element_type=F32
    )
    out_ref[...] = (hidden_ref[...] + projected + row_of(output_bias_ref)).astype(BF16)

    for at in range(1, MEMBERS):
        for group in range(2):
            signal_copy(group, at).wait_send()
            back_copy(group, at).wait_send()
        ask_copy(at).wait_send()
        context_copy(at).wait_send()
    for at in range(MEMBERS):
        quarter, side = chosen_head(at)

        @pl.when(quarter + 4 * side != member)
        def _(head=quarter + 4 * side, at=at):
            head_copy(member, head, at).wait_send()

    rows.sent()
    outs.sent()


def by_heads(
    signal,
    position_kernel,
    position_bias,
    layer_gain,
    layer_shift,
    query_weight,
    query_bias,
    key_weight,
    value_weight,
    value_bias,
    output_weight,
    output_bias,
    key_blocks,
    global_blocks,
):
    frame_count, width = signal.shape
    frames = MEMBERS * frame_count
    share = 2 * GROUP
    vmem = pl.BlockSpec(memory_space=pltpu.VMEM)
    smem = pl.BlockSpec(memory_space=pltpu.SMEM)
    hbm = pl.BlockSpec(memory_space=pl.ANY)
    dma = pltpu.SemaphoreType.DMA
    return pl.pallas_call(
        whole_kernel,
        out_shape=jax.ShapeDtypeStruct((frame_count, width), BF16),
        in_specs=[smem, smem, hbm, hbm] + [vmem] * 3 + [hbm] * 3 + [vmem] * 2 + [hbm, vmem],
        out_specs=vmem,
        scratch_shapes=[
            pltpu.VMEM((frame_count, width), BF16),
            pltpu.VMEM((share, HEADS * HEAD), BF16),
            pltpu.VMEM((share, HEADS * HEAD), BF16),
            pltpu.VMEM((share, HEADS * HEAD), BF16),
            pltpu.VMEM((share, HEADS * HEAD), BF16),
            pltpu.VMEM((share, GROUP, LANES), BF16),
            pltpu.VMEM((share * PADDED, LANES), F32),
            pltpu.VMEM((2, STEPS * PHASES * GROUP, 2 * LANES), BF16),
            pltpu.VMEM((2, MEMBERS, PACKED, LANES), BF16),
            pltpu.VMEM((2, MEMBERS, PACKED, LANES), BF16),
            pltpu.VMEM((frames + 160, LANES), F32),
            pltpu.VMEM((STEPS * 2, 16, 2 * LANES), BF16),
            pltpu.VMEM((SPAN * 16, PHASES * GROUP), F32),
            pltpu.VMEM((frames + 32, LANES), F32),
            pltpu.VMEM((2, MEMBERS, PACKED, LANES), BF16),
            pltpu.VMEM((2, MEMBERS, PACKED, LANES), BF16),
            pltpu.VMEM((frame_count, width), F32),
            pltpu.VMEM((frame_count, width), BF16),
            pltpu.VMEM((2 * HEADS, width, LANES), BF16),
            pltpu.VMEM((MEMBERS, 832, LANES), BF16),
            pltpu.VMEM((HEADS, 2 * LANES), F32),
            pltpu.VMEM((MEMBERS, frame_count + 64, LANES), BF16),
            pltpu.VMEM((MEMBERS, frame_count + 64, LANES), BF16),
            pltpu.VMEM((MEMBERS, 192, LANES), BF16),
            pltpu.VMEM((MEMBERS, 192, LANES), BF16),
            pltpu.VMEM((frames + GLOBALS * BLOCK, LANES), BF16),
            pltpu.VMEM((frames + GLOBALS * BLOCK, LANES), BF16),
            pltpu.VMEM((GLOBALS * BLOCK, frames), BF16),
            pltpu.VMEM((MEMBERS, PACKED, LANES), BF16),
            pltpu.VMEM((MEMBERS, PACKED, LANES), BF16),
            dma((6,)),
            dma((14,)),
            dma((14,)),
            dma((14,)),
            dma((14,)),
            dma((28,)),
            dma((28,)),
            dma((28,)),
            dma((28,)),
            dma((8,)),
            dma((8,)),
            dma((7,)),
            dma((7,)),
            dma((7,)),
            dma((7,)),
        ],
        compiler_params=pltpu.CompilerParams(
            collective_id=0, has_side_effects=True, vmem_limit_bytes=60 * 1024 * 1024
        ),
    )(
        key_blocks,
        global_blocks,
        signal,
        position_kernel,
        position_bias,
        layer_gain,
        layer_shift,
        query_weight,
        key_weight,
        value_weight,
        query_bias,
        value_bias,
        output_weight.T,
        output_bias,
    )


def body(*operands):
    share, width, taps = operands[1].shape
    fits = lax.axis_size("tm") == MEMBERS and lax.axis_size("rec") == QUARTERS
    fits = fits and (share, width, taps) == (2 * GROUP, GROUP, LANES)
    fits = fits and operands[0].shape[0] == 2 * BLOCK
    return (by_heads if fits else general)(*operands)


def solution(mesh):
    placed = (
        P(("rec", "tm"), None),
        P("tm", None, None),
        P("tm"),
        P(),
        P(),
        P("tm", None),
        P(),
        P("tm", None),
        P("tm", None),
        P(),
        P(None, "tm"),
        P(),
        P(("rec", "tm"), None),
        P("rec"),
    )
    return jax.shard_map(
        body, mesh=mesh, in_specs=placed, out_specs=P(("rec", "tm"), None), check_vma=False
    )
```

```python
import math

import jax
import jax.numpy as jnp
import numpy as np
from jax import lax
from jax.experimental import pallas as pl
from jax.experimental.pallas import tpu as pltpu
from jax.sharding import PartitionSpec as P

HEAD = 80
HEADS = 8
BLOCK = 128
GLOBALS = 4


EPSILON = 1e-05


def attend(queries, key_rows, value_rows, allowed):
    block_count, row_count, heads_width = queries.shape
    query_heads = queries.reshape(block_count, row_count, HEADS, HEAD)
    key_heads = key_rows.reshape(block_count, key_rows.shape[1], HEADS, HEAD)
    value_heads = value_rows.reshape(block_count, value_rows.shape[1], HEADS, HEAD)
    scores = jnp.einsum(
        "bqhe,bkhe->bhqk", query_heads, key_heads, preferred_element_type=jnp.float32
    ) * (1.0 / math.sqrt(HEAD))
    scores = jnp.where(allowed[:, None, None, :], scores, -jnp.inf)
    row_max = jnp.max(scores, axis=-1, keepdims=True)
    weights = jnp.exp(scores - row_max)
    row_total = jnp.sum(weights, axis=-1)
    probability = weights.astype(jnp.bfloat16)
    context_sum = jnp.einsum(
        "bhqk,bkhe->bqhe", probability, value_heads, preferred_element_type=jnp.float32
    )
    context = context_sum / jnp.transpose(row_total, (0, 2, 1))[..., None]
    return context.reshape(block_count, row_count, heads_width).astype(jnp.bfloat16)


def general(
    signal,
    position_kernel,
    position_bias,
    layer_gain,
    layer_shift,
    query_weight,
    query_bias,
    key_weight,
    value_weight,
    value_bias,
    output_weight,
    output_bias,
    key_blocks,
    global_blocks,
):
    devices = lax.axis_size("tm")
    frame_count, model_width = signal.shape
    channel_share, group_width, kernel_taps = position_kernel.shape
    inner_width = max(channel_share, group_width)
    folded = signal.T
    if channel_share >= group_width:
        outgoing = folded.reshape(devices, channel_share, frame_count)
    else:
        start_groups = np.arange(devices) * channel_share // group_width
        grouped = folded.reshape(model_width // group_width, group_width, frame_count)
        outgoing = jnp.stack(
            [grouped[at * channel_share // group_width] for at in range(devices)]
        )
    incoming = lax.all_to_all(outgoing, "tm", split_axis=0, concat_axis=2, tiled=True)
    outputs = channel_share if channel_share < group_width else group_width
    spread = jnp.pad(
        incoming.reshape(inner_width // group_width, group_width, -1),
        ((0, 0), (0, 0), (kernel_taps // 2, kernel_taps // 2 - 1)),
    )
    frames = incoming.shape[-1]
    by_tap = position_kernel.reshape(-1, outputs, group_width, kernel_taps).transpose(3, 0, 1, 2)

    def tap(at, total):
        window = lax.dynamic_slice_in_dim(spread, at, frames, axis=2)
        return total + jnp.einsum(
            "goi,git->got", by_tap[at], window, preferred_element_type=jnp.float32
        )

    response = lax.fori_loop(
        0, kernel_taps, tap, jnp.zeros((spread.shape[0], outputs, frames), jnp.float32)
    ).reshape(channel_share, frames)
    position = jax.nn.gelu(response + position_bias[:, None], approximate=False).astype(
        jnp.bfloat16
    )
    returned = lax.all_to_all(position, "tm", split_axis=1, concat_axis=0, tiled=True)
    hidden = signal.astype(jnp.float32) + returned.T.astype(jnp.float32)
    average = jnp.mean(hidden, axis=-1, keepdims=True)
    centered = hidden - average
    variance = jnp.mean(centered * centered, axis=-1, keepdims=True)
    normed = (centered * lax.rsqrt(variance + EPSILON) * layer_gain + layer_shift).astype(
        jnp.bfloat16
    )
    heads_width = query_weight.shape[1]
    zero_sums = jnp.zeros((frame_count, heads_width), jnp.float32)
    totals = (zero_sums, zero_sums, zero_sums)
    pieces = (
        lax.all_gather(query_weight, "tm", axis=0, tiled=True),
        lax.all_gather(key_weight, "tm", axis=0, tiled=True),
        lax.all_gather(value_weight, "tm", axis=0, tiled=True),
    )
    columns = lax.slice_in_dim(normed, 0, pieces[0].shape[0], axis=1)
    query_sum, key_sum, value_sum = tuple(
        (
            running + jnp.dot(columns, weight_rows, preferred_element_type=jnp.float32)
            for running, weight_rows in zip(totals, pieces)
        )
    )
    queries = (query_sum + query_bias).astype(jnp.bfloat16)
    key_part = key_sum.astype(jnp.bfloat16)
    value_part = (value_sum + value_bias).astype(jnp.bfloat16)
    key_value = jnp.stack((key_part, value_part), axis=1)
    per_device = frame_count // BLOCK
    repeated = jnp.any(global_blocks[None, :, None] == key_blocks[:, None, :], axis=-1)
    whole = lax.all_gather(key_value, "tm", axis=0, tiled=True)
    block_ids = jnp.concatenate(
        [key_blocks, jnp.broadcast_to(global_blocks[None, :], (per_device, GLOBALS))], axis=1
    )
    allowed = jnp.concatenate([key_blocks >= 0, jnp.logical_not(repeated)], axis=1)
    table = whole.reshape(-1, BLOCK, 2, heads_width)
    chosen = jnp.maximum(block_ids, 0)
    candidates = jnp.stack(
        [
            jnp.stack(
                [
                    lax.dynamic_index_in_dim(table, chosen[row, at], 0, keepdims=False)
                    for at in range(chosen.shape[1])
                ]
            )
            for row in range(per_device)
        ]
    )
    key_rows = candidates[:, :, :, 0].reshape(per_device, -1, heads_width)
    value_rows = candidates[:, :, :, 1].reshape(per_device, -1, heads_width)
    allowed_rows = jnp.repeat(allowed, BLOCK, axis=1)
    context = attend(
        queries.reshape(per_device, BLOCK, heads_width), key_rows, value_rows, allowed_rows
    ).reshape(frame_count, heads_width)
    projected = jnp.dot(
        context,
        lax.all_gather(output_weight, "tm", axis=1, tiled=True),
        preferred_element_type=jnp.float32,
    )
    return (hidden + projected + output_bias).astype(jnp.bfloat16)


PHASES = 3
GROUP = 80
MEMBERS = 8
QUARTERS = 4
LANES = 128
STEP = 4
STEPS = 44
SPAN = 43
PACKED = 160
PADDED = 145
MESH = pl.DeviceIdType.MESH
BIG = 1e30
F32 = jnp.float32
BF16 = jnp.bfloat16


def flip(member, bits):
    low = bits % 4
    if low == 1:
        turned = member + 1 - 2 * lax.rem(member, 2)
    elif low == 2:
        turned = member + 2 - 4 * lax.rem(lax.div(member, 2), 2)
    elif low == 3:
        turned = 4 * lax.div(member, 4) + 3 - lax.rem(member, 4)
    else:
        turned = member
    return lax.rem(turned + 4, MEMBERS) if bits >= 4 else turned


def loop(begin, end, body, unroll):
    turns = (end - begin) // unroll

    def turn(step, _):
        for at in range(unroll):
            body(begin + step * unroll + at)
        return 0

    if turns > 1:
        lax.fori_loop(0, turns, turn, 0)
    else:
        turns = 0
    for at in range(begin + turns * unroll, end):
        body(at)


def row_of(ref):
    return ref[...].reshape(1, -1)


def pack(value):
    return jnp.concatenate(
        [
            jnp.concatenate([value[:96], value[160:, :48]], axis=1),
            jnp.concatenate([value[96:128], value[160:192, 48:], value[224:, 48:64]], axis=1),
            jnp.concatenate([value[128:160], value[192:224, 48:], value[224:, 64:]], axis=1),
        ],
        axis=0,
    )


def unpack(ref, begin, end):
    if end <= 160:
        return ref[begin:end, :GROUP]
    if end <= 224:
        return jnp.concatenate(
            [ref[begin - 160 : end - 160, GROUP:], ref[begin - 64 : end - 64, GROUP:112]], axis=1
        )
    return jnp.concatenate(
        [ref[64:96, GROUP:], ref[96:128, 112:], ref[128:160, 112:]], axis=1
    )


def remote(source, target, send, receive, device):
    return pltpu.make_async_remote_copy(
        src_ref=source,
        dst_ref=target,
        send_sem=send,
        recv_sem=receive,
        device_id=device,
        device_id_type=MESH,
    )


class Spread:
    def __init__(self, piece, record, member, sends, receives):
        self.piece, self.record, self.member = piece, record, member
        self.sends, self.receives = sends, receives
        self.across = lax.rem(record + 2, QUARTERS)
        self.beside = record + 1 - 2 * lax.rem(record, 2)

    def copy(self, at, share, quarter, device):
        ref = self.piece(share, quarter)
        return remote(ref, ref, self.sends.at[at], self.receives.at[at], device)

    def plane(self, at):
        bits = at + 1
        if bits <= 4:
            return self.copy(at, self.member, self.record, (self.record, flip(self.member, bits)))
        share = flip(self.member, 4)
        return self.copy(at, share, self.record, (self.record, flip(self.member, bits - 4)))

    def other(self, at):
        return self.copy(7 + at, flip(self.member, at + 1), self.record, (self.across, self.member))

    def core(self, at):
        return self.copy(14 + at, flip(self.member, at + 1), self.record, (self.beside, self.member))

    def last(self, at):
        return self.copy(21 + at, flip(self.member, at + 1), self.across, (self.beside, self.member))

    def first(self):
        for at in (3, 0, 1, 2):
            self.plane(at).start()

    def second(self):
        for at in (0, 1, 2):
            self.plane(at).wait_recv()
            self.other(at).start()
            self.core(at).start()

    def second_far(self):
        self.plane(3).wait_recv()
        for at in (4, 5, 6):
            self.plane(at).start()
        self.other(3).start()
        self.core(3).start()

    def third(self):
        for at in (4, 5, 6):
            self.plane(at).wait_recv()
            self.other(at).start()
            self.core(at).start()

    def fourth(self, which):
        for at in which:
            self.other(at).wait_recv()
            self.last(at).start()

    def near(self):
        for at in range(7):
            self.core(at).wait_recv()

    def far(self):
        for at in range(7):
            self.last(at).wait_recv()

    def sent(self):
        for at in range(7):
            for copy in (self.plane(at), self.other(at), self.core(at), self.last(at)):
                copy.wait_send()


def whole_kernel(
    blocks_ref,
    globals_ref,
    signal_hbm,
    taps_hbm,
    tap_bias_ref,
    gain_ref,
    shift_ref,
    query_hbm,
    key_hbm,
    value_hbm,
    query_bias_ref,
    value_bias_ref,
    output_hbm,
    output_bias_ref,
    out_ref,
    signal_ref,
    query_ref,
    key_ref,
    value_ref,
    output_ref,
    taps_ref,
    turned_ref,
    matrix_ref,
    send_ref,
    got_ref,
    frames_ref,
    spread_ref,
    total_ref,
    natural_ref,
    back_ref,
    returned_ref,
    hidden_ref,
    normed_ref,
    rows_ref,
    output_rows_ref,
    bias_ref,
    slab_ref,
    headed_ref,
    asked_ref,
    asking_ref,
    keys_ref,
    values_ref,
    chosen_ref,
    context_ref,
    contexts_ref,
    load_sem,
    signal_send,
    signal_recv,
    back_send,
    back_recv,
    rows_send,
    rows_recv,
    outs_send,
    outs_recv,
    head_send,
    head_recv,
    ask_send,
    ask_recv,
    context_send,
    context_recv,
):
    record, member = lax.axis_index("rec"), lax.axis_index("tm")
    loads = [
        pltpu.make_async_copy(source, target, load_sem.at[at])
        for at, (source, target) in enumerate(
            (
                (signal_hbm, signal_ref),
                (query_hbm, query_ref),
                (key_hbm, key_ref),
                (value_hbm, value_ref),
                (taps_hbm, taps_ref),
                (output_hbm, output_ref),
            )
        )
    ]
    for load in loads:
        load.start()

    barrier = pltpu.get_barrier_semaphore()
    across = lax.rem(record + 2, QUARTERS)
    beside = record + 1 - 2 * lax.rem(record, 2)
    peers = [(record, lax.rem(member + at, MEMBERS)) for at in range(1, MEMBERS)]
    for peer in peers + [(across, member), (beside, member)]:
        pl.semaphore_signal(barrier, inc=1, device_id=peer, device_id_type=MESH)

    loads[0].wait()
    frame_count = signal_ref.shape[0]
    share = 2 * GROUP
    rest = share - LANES

    def signal_copy(group, at):
        to = lax.rem(member + at, MEMBERS)
        return remote(
            send_ref.at[group, to],
            got_ref.at[group, member],
            signal_send.at[group * 7 + at - 1],
            signal_recv.at[group * 7 + at - 1],
            (record, to),
        )

    def send_signal(group):
        for to in range(MEMBERS):
            begin = to * share + group * GROUP
            send_ref[group, to] = pack(signal_ref[:, begin : begin + GROUP])
        for at in (4, 3, 5, 2, 6, 1, 7):
            signal_copy(group, at).start()
        got_ref[group, member] = send_ref[group, member]


    for load in loads[1:4]:
        load.wait()
    mine = pl.ds(pl.multiple_of(member * share, 32), share)
    for head in range(HEADS):
        columns = slice(head * HEAD, (head + 1) * HEAD)
        joined = jnp.concatenate(
            [
                key_ref[:, columns],
                value_ref[:, columns],
                query_ref[:, columns],
                jnp.zeros((share, 16), BF16),
            ],
            axis=1,
        )
        tile = head % QUARTERS * 4 + head // QUARTERS * 2
        rows_ref[tile, mine, :] = joined[:, :LANES]
        rows_ref[tile + 1, mine, :] = joined[:, LANES:]
    def rows_piece(of, quarter):
        return rows_ref.at[
            pl.ds(quarter * 4, 4), pl.ds(pl.multiple_of(of * share, 32), share), :
        ]

    def output_piece(of, quarter):
        return output_rows_ref.at[of, pl.ds(pl.multiple_of(quarter * 208, 16), 208), :]

    rows = Spread(rows_piece, record, member, rows_send, rows_recv)
    outs = Spread(output_piece, record, member, outs_send, outs_recv)
    pl.semaphore_wait(barrier, 9)
    rows.first()
    send_signal(0)

    heads_width = HEADS * HEAD
    loads[5].wait()
    for at in range(heads_width // LANES):
        output_rows_ref[member, share * at : share * at + share, :] = output_ref[
            :, at * LANES : (at + 1) * LANES
        ]
    output_rows_ref[member, 5 * share :, :] = jnp.zeros((32, LANES), BF16)
    empty = jnp.zeros((1, HEAD), F32)
    for head in range(HEADS):
        columns = slice(head * HEAD, (head + 1) * HEAD)
        bias_ref[head : head + 1, :] = jnp.concatenate(
            [
                empty,
                row_of(value_bias_ref)[:, columns],
                row_of(query_bias_ref)[:, columns],
                empty[:, :16],
            ],
            axis=1,
        )


    loads[4].wait()
    empty = jnp.zeros((8, LANES), F32)

    def turn(channel):
        begin = channel * PADDED
        turned_ref[pl.ds(begin, 8), :] = empty
        turned_ref[pl.ds(begin + 136, 8), :] = empty
        turned_ref[pl.ds(begin + 8, LANES), :GROUP] = jnp.transpose(taps_ref[channel]).astype(F32)

    loop(0, share, turn, 16)
    send_signal(1)

    def lay(step):
        for group in range(2):
            taps = [
                turned_ref[
                    pl.ds(group * GROUP * PADDED + step * 3 + 6 + at, GROUP, stride=PADDED), :
                ].astype(BF16)[:, :GROUP]
                for at in range(5)
            ]
            for phase in range(PHASES):
                row = jnp.concatenate(
                    taps[2 - phase : 5 - phase] + [jnp.zeros((GROUP, 16), BF16)], axis=1
                )
                begin = pl.multiple_of((step * PHASES + phase) * GROUP, 16)
                matrix_ref[group, pl.ds(begin, GROUP), :] = row

    rows.second()
    loop(0, STEPS, lay, 4)
    rows.second_far()

    frames = MEMBERS * frame_count
    tail = 64 + frames + (64 + frames) // BLOCK

    def back_copy(group, at):
        to = lax.rem(member + at, MEMBERS)
        return remote(
            back_ref.at[group, to],
            returned_ref.at[group, member],
            back_send.at[group * 7 + at - 1],
            back_recv.at[group * 7 + at - 1],
            (record, to),
        )

    for group in range(2):
        frames_ref[:64, :] = jnp.zeros((64, LANES), F32)
        frames_ref[tail:, :] = jnp.zeros((frames_ref.shape[0] - tail, LANES), F32)
        for at in range(1, MEMBERS):
            signal_copy(group, at).wait_recv()

        def place(of, group=group):
            begin = of * (frame_count + 2) + 64
            packed = got_ref.at[group, of]
            for low, high, skew in (
                (0, 64, 0),
                (64, 160, 1),
                (160, 192, 1),
                (192, 224, 2),
                (224, 256, 2),
            ):
                frames_ref[pl.ds(begin + low + skew, high - low), :GROUP] = unpack(
                    packed, low, high
                ).astype(F32)

        loop(0, MEMBERS, place, 2)

        def widen(row):
            parts = []
            for phase in range(PHASES):
                at = row * PHASES + phase
                part = frames_ref[pl.ds(at + at // BLOCK, 16, stride=BLOCK + 1), :]
                parts.append(part.astype(BF16)[:, :GROUP])
            spread_ref[row] = jnp.concatenate(parts + [jnp.zeros((16, 16), BF16)], axis=1)

        loop(0, STEPS * 2, widen, 11)
        if group == 0:
            outs.first()
        window = jnp.concatenate(
            [
                spread_ref[step : step + SPAN].reshape(SPAN * 16, 2 * LANES)
                for step in range(STEPS)
            ],
            axis=1,
        )
        weights = jnp.concatenate(
            [matrix_ref[group, step * 240 : step * 240 + 240, :] for step in range(STEPS)],
            axis=1,
        )
        total_ref[...] = lax.dot_general(
            window, weights, (((1,), (1,)), ((), ())), preferred_element_type=F32
        )
        bias = row_of(tap_bias_ref)[:, group * GROUP : (group + 1) * GROUP]
        bias = jnp.concatenate([bias] * PHASES, axis=1)

        def activate(row, bias=bias):
            value = total_ref[pl.ds(pl.multiple_of(row * 16, 16), 16), :] + bias
            value = value * (1.0 + lax.erf(value * (0.5**0.5))) * 0.5
            for phase in range(PHASES):
                part = value[:, phase * GROUP : (phase + 1) * GROUP]
                part = jnp.concatenate([part, jnp.zeros((16, LANES - GROUP), F32)], axis=1)
                begin = row * PHASES + phase
                begin = begin + begin // BLOCK
                natural_ref[pl.ds(begin, 16, stride=BLOCK + 1), :] = part

        loop(0, SPAN, activate, 11)

        def pack_back(to, group=group):
            begin = 2 * to * (BLOCK + 1)
            halves = [
                natural_ref[pl.ds(begin + side * (BLOCK + 1), BLOCK), :].astype(BF16)[:, :GROUP]
                for side in range(2)
            ]
            back_ref[group, to] = pack(jnp.concatenate(halves, axis=0))

        loop(0, MEMBERS, pack_back, 4)
        for at in (4, 3, 5, 2, 6, 1, 7):
            back_copy(group, at).start()
        returned_ref[group, member] = back_ref[group, member]
        if group == 0:
            rows.third()
    outs.second()
    outs.second_far()

    for group in range(2):
        for at in range(1, MEMBERS):
            back_copy(group, at).wait_recv()
    for begin in range(0, frame_count, 32):
        pieces = [
            unpack(returned_ref.at[group, of], begin, begin + 32)
            for of in range(MEMBERS)
            for group in range(2)
        ]
        position = jnp.concatenate(pieces, axis=1)
        hidden = signal_ref[begin : begin + 32, :].astype(F32) + position.astype(F32)
        hidden_ref[begin : begin + 32, :] = hidden
        average = jnp.mean(hidden, axis=-1, keepdims=True)
        centered = hidden - average
        variance = jnp.mean(centered * centered, axis=-1, keepdims=True)
        normed_ref[begin : begin + 32, :] = (
            centered * lax.rsqrt(variance + EPSILON) * row_of(gain_ref) + row_of(shift_ref)
        ).astype(BF16)

    rows.fourth((0, 1, 2, 3))
    rows.near()
    lane = lax.broadcasted_iota(jnp.int32, (BLOCK, 2 * LANES), 1) - 3 * HEAD
    masks = []
    for block in range(2):
        unlisted = jnp.where(lane >= 0, 1.0, 0.0)
        for at in range(blocks_ref.shape[1]):
            unlisted = jnp.where(lane == jnp.where(lane >= 0, blocks_ref[block, at], -1000), 0.0, unlisted)
        masks.append(unlisted)
    mask = jnp.concatenate(masks, axis=0)

    rest = share - LANES

    def head_copy(source, to, at):
        return remote(
            slab_ref.at[to],
            headed_ref.at[source],
            head_send.at[at],
            head_recv.at[source],
            (record, to),
        )

    def ask_copy(bits):
        to = flip(member, bits)
        return remote(
            asked_ref.at[to],
            asking_ref.at[member],
            ask_send.at[bits - 1],
            ask_recv.at[bits - 1],
            (record, to),
        )

    def chosen_head(at):
        turned = lax.rem(member + at, 4)
        first = jnp.where(at < 4, record, across)
        second = first + 1 - 2 * lax.rem(first, 2)
        quarter = jnp.where(turned < 2, first, second)
        return quarter, lax.rem(turned, 2)

    def project(at):
        quarter, side = chosen_head(at)
        head, tile = quarter + 4 * side, 4 * quarter + 2 * side
        weights = jnp.concatenate([rows_ref[tile], rows_ref[tile + 1]], axis=1)
        slab = jnp.dot(normed_ref[...], weights, preferred_element_type=F32)
        slab = (slab + bias_ref[pl.ds(head, 1), :] + mask).astype(BF16)
        slab_ref[head, :frame_count, :] = slab[:, :LANES]
        slab_ref[head, frame_count:, :] = jnp.concatenate(
            [slab[64 * part : 64 * part + 64, LANES:share] for part in range(4)], axis=1
        )
        asked = slab[:, share:]
        asked_ref[head] = jnp.concatenate(
            [
                asked[:192],
                jnp.concatenate(
                    [asked[192:, part * 32 : part * 32 + 32] for part in range(3)], axis=0
                ),
            ],
            axis=1,
        )

        @pl.when(head != member)
        def _():
            head_copy(member, head, at).start()

        @pl.when(head == member)
        def _():
            headed_ref[member] = slab_ref[head]

    for at in range(4):
        project(at)
    outs.third()
    rows.fourth((4, 5, 6))
    rows.far()
    for at in range(4, 8):
        project(at)
    for bits in (4, 5, 6, 7, 3, 2, 1):
        ask_copy(bits).start()
    asking_ref[member] = asked_ref[member]

    place_row = lax.broadcasted_iota(jnp.int32, (BLOCK, frames), 0)
    place_column = lax.broadcasted_iota(jnp.int32, (BLOCK, frames), 1)
    for at in range(GLOBALS):
        chosen_ref[at * BLOCK : (at + 1) * BLOCK, :] = jnp.where(
            place_row + globals_ref[at] * BLOCK == place_column, 1.0, 0.0
        ).astype(BF16)

    def arrange(of):
        slab = headed_ref[of]
        begin = pl.multiple_of(of * frame_count, 256)
        row = lax.broadcasted_iota(jnp.int32, (frame_count, 16), 0)
        block = 2 * of + jnp.where(row >= BLOCK, 1, 0)
        here = lax.broadcasted_iota(jnp.int32, (frame_count, 16), 1) == block
        keys_ref[pl.ds(begin, frame_count), :] = jnp.concatenate(
            [
                slab[:frame_count, :HEAD],
                jnp.where(here, -BIG, 0.0).astype(BF16),
                jnp.zeros((frame_count, 32), BF16),
            ],
            axis=1,
        )
        side = jnp.concatenate(
            [slab[frame_count:, rest * part : rest * part + rest] for part in range(4)], axis=0
        )
        values_ref[pl.ds(begin, frame_count), :] = jnp.concatenate(
            [
                slab[:frame_count, HEAD:],
                side,
                jnp.ones((frame_count, 16), BF16),
                jnp.zeros((frame_count, 32), BF16),
            ],
            axis=1,
        )

    arrange(member)
    for at in range(1, MEMBERS):
        of = lax.rem(member + at, MEMBERS)
        head_copy(of, member, 0).wait_recv()
        arrange(of)
    lane = lax.broadcasted_iota(jnp.int32, (BLOCK, LANES), 1)
    picked = jnp.dot(
        chosen_ref[...],
        jnp.concatenate([keys_ref[:frames, :], values_ref[:frames, :]], axis=1),
        preferred_element_type=F32,
    )
    for at in range(GLOBALS):
        rows_at = slice(at * BLOCK, (at + 1) * BLOCK)
        keys_ref[frames + at * BLOCK : frames + (at + 1) * BLOCK, :] = jnp.where(
            lane < HEAD,
            picked[rows_at, :LANES],
            jnp.where(lane == HEAD + 16 + globals_ref[at], -BIG, 0.0),
        ).astype(BF16)
        values_ref[frames + at * BLOCK : frames + (at + 1) * BLOCK, :] = picked[
            rows_at, LANES:
        ].astype(BF16)

    factor = (1.0 / math.sqrt(HEAD)) * math.log2(math.e)

    def context_copy(bits):
        to = flip(member, bits)
        return remote(
            context_ref.at[to],
            contexts_ref.at[member],
            context_send.at[bits - 1],
            context_recv.at[bits - 1],
            (record, to),
        )

    def attend_tile(of):
        asked = asking_ref[of]
        last = jnp.concatenate(
            [asked[64 * part : 64 * part + 64, 96:] for part in range(3)], axis=1
        )
        asked = jnp.concatenate([asked[:, :96], last], axis=0)
        queries = jnp.concatenate(
            [asked, 1.0 - asked[:, HEAD:], jnp.zeros((frame_count, 16), BF16)], axis=1
        )
        low = jnp.minimum(jnp.maximum(2 * of - 2, 0), 10)
        window = pl.ds(pl.multiple_of(low * BLOCK, BLOCK), 6 * BLOCK)
        keys = jnp.concatenate([keys_ref[window, :], keys_ref[frames:, :]], axis=0)
        scores = lax.dot_general(
            queries, keys, (((1,), (1,)), ((), ())), preferred_element_type=F32
        )
        peak = jnp.max(scores, axis=1, keepdims=True)
        weights = jnp.exp2(scores * factor - peak * factor).astype(BF16)
        values = jnp.concatenate([values_ref[window, :], values_ref[frames:, :]], axis=0)
        summed = jnp.dot(weights, values, preferred_element_type=F32)
        return pack((summed[:, :HEAD] / summed[:, HEAD : HEAD + 1]).astype(BF16))

    contexts_ref[member] = attend_tile(member)
    for pair in ((1,), (2, 3), (4, 5), (6, 7)):
        for bits in pair:
            ask_copy(bits).wait_recv()
        for bits in pair:
            of = flip(member, bits)
            context_ref[of] = attend_tile(of)
            context_copy(bits).start()
    outs.fourth(range(7))

    for at in range(1, MEMBERS):
        context_copy(at).wait_recv()
    outs.near()
    outs.far()
    context = jnp.concatenate(
        [
            jnp.concatenate(
                [
                    unpack(contexts_ref.at[of], 0, 160),
                    unpack(contexts_ref.at[of], 160, 224),
                    unpack(contexts_ref.at[of], 224, 256),
                ],
                axis=0,
            )
            for of in range(HEADS)
        ],
        axis=1,
    )
    columns = jnp.concatenate(
        [
            jnp.concatenate(
                [output_rows_ref[of, share * at : share * at + share, :] for at in range(5)], axis=1
            )
            for of in range(MEMBERS)
        ],
        axis=0,
    )
    projected = lax.dot_general(
        context, columns, (((1,), (1,)), ((), ())), preferred_element_type=F32
    )
    out_ref[...] = (hidden_ref[...] + projected + row_of(output_bias_ref)).astype(BF16)

    for at in range(1, MEMBERS):
        for group in range(2):
            signal_copy(group, at).wait_send()
            back_copy(group, at).wait_send()
        ask_copy(at).wait_send()
        context_copy(at).wait_send()
    for at in range(MEMBERS):
        quarter, side = chosen_head(at)

        @pl.when(quarter + 4 * side != member)
        def _(head=quarter + 4 * side, at=at):
            head_copy(member, head, at).wait_send()

    rows.sent()
    outs.sent()


def by_heads(
    signal,
    position_kernel,
    position_bias,
    layer_gain,
    layer_shift,
    query_weight,
    query_bias,
    key_weight,
    value_weight,
    value_bias,
    output_weight,
    output_bias,
    key_blocks,
    global_blocks,
):
    frame_count, width = signal.shape
    frames = MEMBERS * frame_count
    share = 2 * GROUP
    vmem = pl.BlockSpec(memory_space=pltpu.VMEM)
    smem = pl.BlockSpec(memory_space=pltpu.SMEM)
    hbm = pl.BlockSpec(memory_space=pl.ANY)
    dma = pltpu.SemaphoreType.DMA
    return pl.pallas_call(
        whole_kernel,
        out_shape=jax.ShapeDtypeStruct((frame_count, width), BF16),
        in_specs=[smem, smem, hbm, hbm] + [vmem] * 3 + [hbm] * 3 + [vmem] * 2 + [hbm, vmem],
        out_specs=vmem,
        scratch_shapes=[
            pltpu.VMEM((frame_count, width), BF16),
            pltpu.VMEM((share, HEADS * HEAD), BF16),
            pltpu.VMEM((share, HEADS * HEAD), BF16),
            pltpu.VMEM((share, HEADS * HEAD), BF16),
            pltpu.VMEM((share, HEADS * HEAD), BF16),
            pltpu.VMEM((share, GROUP, LANES), BF16),
            pltpu.VMEM((share * PADDED, LANES), F32),
            pltpu.VMEM((2, STEPS * PHASES * GROUP, 2 * LANES), BF16),
            pltpu.VMEM((2, MEMBERS, PACKED, LANES), BF16),
            pltpu.VMEM((2, MEMBERS, PACKED, LANES), BF16),
            pltpu.VMEM((frames + 160, LANES), F32),
            pltpu.VMEM((STEPS * 2, 16, 2 * LANES), BF16),
            pltpu.VMEM((SPAN * 16, PHASES * GROUP), F32),
            pltpu.VMEM((frames + 32, LANES), F32),
            pltpu.VMEM((2, MEMBERS, PACKED, LANES), BF16),
            pltpu.VMEM((2, MEMBERS, PACKED, LANES), BF16),
            pltpu.VMEM((frame_count, width), F32),
            pltpu.VMEM((frame_count, width), BF16),
            pltpu.VMEM((2 * HEADS, width, LANES), BF16),
            pltpu.VMEM((MEMBERS, 832, LANES), BF16),
            pltpu.VMEM((HEADS, 2 * LANES), F32),
            pltpu.VMEM((MEMBERS, frame_count + 64, LANES), BF16),
            pltpu.VMEM((MEMBERS, frame_count + 64, LANES), BF16),
            pltpu.VMEM((MEMBERS, 192, LANES), BF16),
            pltpu.VMEM((MEMBERS, 192, LANES), BF16),
            pltpu.VMEM((frames + GLOBALS * BLOCK, LANES), BF16),
            pltpu.VMEM((frames + GLOBALS * BLOCK, LANES), BF16),
            pltpu.VMEM((GLOBALS * BLOCK, frames), BF16),
            pltpu.VMEM((MEMBERS, PACKED, LANES), BF16),
            pltpu.VMEM((MEMBERS, PACKED, LANES), BF16),
            dma((6,)),
            dma((14,)),
            dma((14,)),
            dma((14,)),
            dma((14,)),
            dma((28,)),
            dma((28,)),
            dma((28,)),
            dma((28,)),
            dma((8,)),
            dma((8,)),
            dma((7,)),
            dma((7,)),
            dma((7,)),
            dma((7,)),
        ],
        compiler_params=pltpu.CompilerParams(
            collective_id=0, has_side_effects=True, vmem_limit_bytes=60 * 1024 * 1024
        ),
    )(
        key_blocks,
        global_blocks,
        signal,
        position_kernel,
        position_bias,
        layer_gain,
        layer_shift,
        query_weight,
        key_weight,
        value_weight,
        query_bias,
        value_bias,
        output_weight.T,
        output_bias,
    )


def body(*operands):
    share, width, taps = operands[1].shape
    fits = lax.axis_size("tm") == MEMBERS and lax.axis_size("rec") == QUARTERS
    fits = fits and (share, width, taps) == (2 * GROUP, GROUP, LANES)
    fits = fits and operands[0].shape[0] == 2 * BLOCK
    return (by_heads if fits else general)(*operands)


def solution(mesh):
    placed = (
        P(("rec", "tm"), None),
        P("tm", None, None),
        P("tm"),
        P(),
        P(),
        P("tm", None),
        P(),
        P("tm", None),
        P("tm", None),
        P(),
        P(None, "tm"),
        P(),
        P(("rec", "tm"), None),
        P("rec"),
    )
    return jax.shard_map(
        body, mesh=mesh, in_specs=placed, out_specs=P(("rec", "tm"), None), check_vma=False
    )
```

```python
import math

import jax
import jax.numpy as jnp
import numpy as np
from jax import lax
from jax.experimental import pallas as pl
from jax.experimental.pallas import tpu as pltpu
from jax.sharding import PartitionSpec as P

HEAD = 80
HEADS = 8
BLOCK = 128
GLOBALS = 4


EPSILON = 1e-05


def attend(queries, key_rows, value_rows, allowed):
    block_count, row_count, heads_width = queries.shape
    query_heads = queries.reshape(block_count, row_count, HEADS, HEAD)
    key_heads = key_rows.reshape(block_count, key_rows.shape[1], HEADS, HEAD)
    value_heads = value_rows.reshape(block_count, value_rows.shape[1], HEADS, HEAD)
    scores = jnp.einsum(
        "bqhe,bkhe->bhqk", query_heads, key_heads, preferred_element_type=jnp.float32
    ) * (1.0 / math.sqrt(HEAD))
    scores = jnp.where(allowed[:, None, None, :], scores, -jnp.inf)
    row_max = jnp.max(scores, axis=-1, keepdims=True)
    weights = jnp.exp(scores - row_max)
    row_total = jnp.sum(weights, axis=-1)
    probability = weights.astype(jnp.bfloat16)
    context_sum = jnp.einsum(
        "bhqk,bkhe->bqhe", probability, value_heads, preferred_element_type=jnp.float32
    )
    context = context_sum / jnp.transpose(row_total, (0, 2, 1))[..., None]
    return context.reshape(block_count, row_count, heads_width).astype(jnp.bfloat16)


def general(
    signal,
    position_kernel,
    position_bias,
    layer_gain,
    layer_shift,
    query_weight,
    query_bias,
    key_weight,
    value_weight,
    value_bias,
    output_weight,
    output_bias,
    key_blocks,
    global_blocks,
):
    devices = lax.axis_size("tm")
    frame_count, model_width = signal.shape
    channel_share, group_width, kernel_taps = position_kernel.shape
    inner_width = max(channel_share, group_width)
    folded = signal.T
    if channel_share >= group_width:
        outgoing = folded.reshape(devices, channel_share, frame_count)
    else:
        start_groups = np.arange(devices) * channel_share // group_width
        grouped = folded.reshape(model_width // group_width, group_width, frame_count)
        outgoing = jnp.stack(
            [grouped[at * channel_share // group_width] for at in range(devices)]
        )
    incoming = lax.all_to_all(outgoing, "tm", split_axis=0, concat_axis=2, tiled=True)
    outputs = channel_share if channel_share < group_width else group_width
    spread = jnp.pad(
        incoming.reshape(inner_width // group_width, group_width, -1),
        ((0, 0), (0, 0), (kernel_taps // 2, kernel_taps // 2 - 1)),
    )
    frames = incoming.shape[-1]
    by_tap = position_kernel.reshape(-1, outputs, group_width, kernel_taps).transpose(3, 0, 1, 2)

    def tap(at, total):
        window = lax.dynamic_slice_in_dim(spread, at, frames, axis=2)
        return total + jnp.einsum(
            "goi,git->got", by_tap[at], window, preferred_element_type=jnp.float32
        )

    response = lax.fori_loop(
        0, kernel_taps, tap, jnp.zeros((spread.shape[0], outputs, frames), jnp.float32)
    ).reshape(channel_share, frames)
    position = jax.nn.gelu(response + position_bias[:, None], approximate=False).astype(
        jnp.bfloat16
    )
    returned = lax.all_to_all(position, "tm", split_axis=1, concat_axis=0, tiled=True)
    hidden = signal.astype(jnp.float32) + returned.T.astype(jnp.float32)
    average = jnp.mean(hidden, axis=-1, keepdims=True)
    centered = hidden - average
    variance = jnp.mean(centered * centered, axis=-1, keepdims=True)
    normed = (centered * lax.rsqrt(variance + EPSILON) * layer_gain + layer_shift).astype(
        jnp.bfloat16
    )
    heads_width = query_weight.shape[1]
    zero_sums = jnp.zeros((frame_count, heads_width), jnp.float32)
    totals = (zero_sums, zero_sums, zero_sums)
    pieces = (
        lax.all_gather(query_weight, "tm", axis=0, tiled=True),
        lax.all_gather(key_weight, "tm", axis=0, tiled=True),
        lax.all_gather(value_weight, "tm", axis=0, tiled=True),
    )
    columns = lax.slice_in_dim(normed, 0, pieces[0].shape[0], axis=1)
    query_sum, key_sum, value_sum = tuple(
        (
            running + jnp.dot(columns, weight_rows, preferred_element_type=jnp.float32)
            for running, weight_rows in zip(totals, pieces)
        )
    )
    queries = (query_sum + query_bias).astype(jnp.bfloat16)
    key_part = key_sum.astype(jnp.bfloat16)
    value_part = (value_sum + value_bias).astype(jnp.bfloat16)
    key_value = jnp.stack((key_part, value_part), axis=1)
    per_device = frame_count // BLOCK
    repeated = jnp.any(global_blocks[None, :, None] == key_blocks[:, None, :], axis=-1)
    whole = lax.all_gather(key_value, "tm", axis=0, tiled=True)
    block_ids = jnp.concatenate(
        [key_blocks, jnp.broadcast_to(global_blocks[None, :], (per_device, GLOBALS))], axis=1
    )
    allowed = jnp.concatenate([key_blocks >= 0, jnp.logical_not(repeated)], axis=1)
    table = whole.reshape(-1, BLOCK, 2, heads_width)
    chosen = jnp.maximum(block_ids, 0)
    candidates = jnp.stack(
        [
            jnp.stack(
                [
                    lax.dynamic_index_in_dim(table, chosen[row, at], 0, keepdims=False)
                    for at in range(chosen.shape[1])
                ]
            )
            for row in range(per_device)
        ]
    )
    key_rows = candidates[:, :, :, 0].reshape(per_device, -1, heads_width)
    value_rows = candidates[:, :, :, 1].reshape(per_device, -1, heads_width)
    allowed_rows = jnp.repeat(allowed, BLOCK, axis=1)
    context = attend(
        queries.reshape(per_device, BLOCK, heads_width), key_rows, value_rows, allowed_rows
    ).reshape(frame_count, heads_width)
    projected = jnp.dot(
        context,
        lax.all_gather(output_weight, "tm", axis=1, tiled=True),
        preferred_element_type=jnp.float32,
    )
    return (hidden + projected + output_bias).astype(jnp.bfloat16)


PHASES = 3
GROUP = 80
MEMBERS = 8
QUARTERS = 4
LANES = 128
STEP = 4
STEPS = 44
SPAN = 43
PACKED = 160
PADDED = 145
MESH = pl.DeviceIdType.MESH
BIG = 1e30
F32 = jnp.float32
BF16 = jnp.bfloat16


def flip(member, bits):
    low = bits % 4
    if low == 1:
        turned = member + 1 - 2 * lax.rem(member, 2)
    elif low == 2:
        turned = member + 2 - 4 * lax.rem(lax.div(member, 2), 2)
    elif low == 3:
        turned = 4 * lax.div(member, 4) + 3 - lax.rem(member, 4)
    else:
        turned = member
    return lax.rem(turned + 4, MEMBERS) if bits >= 4 else turned


def loop(begin, end, body, unroll):
    turns = (end - begin) // unroll

    def turn(step, _):
        for at in range(unroll):
            body(begin + step * unroll + at)
        return 0

    if turns > 1:
        lax.fori_loop(0, turns, turn, 0)
    else:
        turns = 0
    for at in range(begin + turns * unroll, end):
        body(at)


def row_of(ref):
    return ref[...].reshape(1, -1)


def pack(value):
    return jnp.concatenate(
        [
            jnp.concatenate([value[:96], value[160:, :48]], axis=1),
            jnp.concatenate([value[96:128], value[160:192, 48:], value[224:, 48:64]], axis=1),
            jnp.concatenate([value[128:160], value[192:224, 48:], value[224:, 64:]], axis=1),
        ],
        axis=0,
    )


def unpack(ref, begin, end):
    if end <= 160:
        return ref[begin:end, :GROUP]
    if end <= 224:
        return jnp.concatenate(
            [ref[begin - 160 : end - 160, GROUP:], ref[begin - 64 : end - 64, GROUP:112]], axis=1
        )
    return jnp.concatenate(
        [ref[64:96, GROUP:], ref[96:128, 112:], ref[128:160, 112:]], axis=1
    )


def remote(source, target, send, receive, device):
    return pltpu.make_async_remote_copy(
        src_ref=source,
        dst_ref=target,
        send_sem=send,
        recv_sem=receive,
        device_id=device,
        device_id_type=MESH,
    )


class Spread:
    def __init__(self, piece, record, member, sends, receives):
        self.piece, self.record, self.member = piece, record, member
        self.sends, self.receives = sends, receives
        self.across = lax.rem(record + 2, QUARTERS)
        self.beside = record + 1 - 2 * lax.rem(record, 2)

    def copy(self, at, share, quarter, device):
        ref = self.piece(share, quarter)
        return remote(ref, ref, self.sends.at[at], self.receives.at[at], device)

    def plane(self, at):
        bits = at + 1
        if bits <= 4:
            return self.copy(at, self.member, self.record, (self.record, flip(self.member, bits)))
        share = flip(self.member, 4)
        return self.copy(at, share, self.record, (self.record, flip(self.member, bits - 4)))

    def other(self, at):
        return self.copy(7 + at, flip(self.member, at + 1), self.record, (self.across, self.member))

    def core(self, at):
        return self.copy(14 + at, flip(self.member, at + 1), self.record, (self.beside, self.member))

    def last(self, at):
        return self.copy(21 + at, flip(self.member, at + 1), self.across, (self.beside, self.member))

    def first(self):
        for at in (3, 0, 1, 2):
            self.plane(at).start()

    def second(self):
        for at in (0, 1, 2):
            self.plane(at).wait_recv()
            self.other(at).start()
            self.core(at).start()

    def second_far(self):
        self.plane(3).wait_recv()
        for at in (4, 5, 6):
            self.plane(at).start()
        self.other(3).start()
        self.core(3).start()

    def third(self):
        for at in (4, 5, 6):
            self.plane(at).wait_recv()
            self.other(at).start()
            self.core(at).start()

    def fourth(self, which):
        for at in which:
            self.other(at).wait_recv()
            self.last(at).start()

    def near(self):
        for at in range(7):
            self.core(at).wait_recv()

    def far(self):
        for at in range(7):
            self.last(at).wait_recv()

    def sent(self):
        for at in range(7):
            for copy in (self.plane(at), self.other(at), self.core(at), self.last(at)):
                copy.wait_send()


def whole_kernel(
    blocks_ref,
    globals_ref,
    signal_hbm,
    taps_hbm,
    tap_bias_ref,
    gain_ref,
    shift_ref,
    query_hbm,
    key_hbm,
    value_hbm,
    query_bias_ref,
    value_bias_ref,
    output_hbm,
    output_bias_ref,
    out_ref,
    signal_ref,
    query_ref,
    key_ref,
    value_ref,
    output_ref,
    taps_ref,
    turned_ref,
    matrix_ref,
    send_ref,
    got_ref,
    frames_ref,
    spread_ref,
    total_ref,
    natural_ref,
    back_ref,
    returned_ref,
    hidden_ref,
    normed_ref,
    rows_ref,
    output_rows_ref,
    bias_ref,
    slab_ref,
    headed_ref,
    asked_ref,
    asking_ref,
    keys_ref,
    values_ref,
    chosen_ref,
    context_ref,
    contexts_ref,
    load_sem,
    signal_send,
    signal_recv,
    back_send,
    back_recv,
    rows_send,
    rows_recv,
    outs_send,
    outs_recv,
    head_send,
    head_recv,
    ask_send,
    ask_recv,
    context_send,
    context_recv,
):
    record, member = lax.axis_index("rec"), lax.axis_index("tm")
    loads = [
        pltpu.make_async_copy(source, target, load_sem.at[at])
        for at, (source, target) in enumerate(
            (
                (signal_hbm, signal_ref),
                (query_hbm, query_ref),
                (key_hbm, key_ref),
                (value_hbm, value_ref),
                (taps_hbm, taps_ref),
                (output_hbm, output_ref),
            )
        )
    ]
    for load in loads:
        load.start()

    barrier = pltpu.get_barrier_semaphore()
    across = lax.rem(record + 2, QUARTERS)
    beside = record + 1 - 2 * lax.rem(record, 2)
    peers = [(record, lax.rem(member + at, MEMBERS)) for at in range(1, MEMBERS)]
    for peer in peers + [(across, member), (beside, member)]:
        pl.semaphore_signal(barrier, inc=1, device_id=peer, device_id_type=MESH)

    loads[0].wait()
    frame_count = signal_ref.shape[0]
    share = 2 * GROUP
    rest = share - LANES

    def signal_copy(group, at):
        to = lax.rem(member + at, MEMBERS)
        return remote(
            send_ref.at[group, to],
            got_ref.at[group, member],
            signal_send.at[group * 7 + at - 1],
            signal_recv.at[group * 7 + at - 1],
            (record, to),
        )

    def send_signal(group):
        for to in range(MEMBERS):
            begin = to * share + group * GROUP
            send_ref[group, to] = pack(signal_ref[:, begin : begin + GROUP])
        for at in (4, 3, 5, 2, 6, 1, 7):
            signal_copy(group, at).start()
        got_ref[group, member] = send_ref[group, member]


    for load in loads[1:4]:
        load.wait()
    mine = pl.ds(pl.multiple_of(member * share, 32), share)
    for head in range(HEADS):
        columns = slice(head * HEAD, (head + 1) * HEAD)
        joined = jnp.concatenate(
            [
                key_ref[:, columns],
                value_ref[:, columns],
                query_ref[:, columns],
                jnp.zeros((share, 16), BF16),
            ],
            axis=1,
        )
        tile = head % QUARTERS * 4 + head // QUARTERS * 2
        rows_ref[tile, mine, :] = joined[:, :LANES]
        rows_ref[tile + 1, mine, :] = joined[:, LANES:]
    def rows_piece(of, quarter):
        return rows_ref.at[
            pl.ds(quarter * 4, 4), pl.ds(pl.multiple_of(of * share, 32), share), :
        ]

    def output_piece(of, quarter):
        return output_rows_ref.at[of, pl.ds(pl.multiple_of(quarter * 208, 16), 208), :]

    rows = Spread(rows_piece, record, member, rows_send, rows_recv)
    outs = Spread(output_piece, record, member, outs_send, outs_recv)
    pl.semaphore_wait(barrier, 9)
    rows.first()
    send_signal(0)

    heads_width = HEADS * HEAD
    loads[5].wait()
    for at in range(heads_width // LANES):
        output_rows_ref[member, share * at : share * at + share, :] = output_ref[
            :, at * LANES : (at + 1) * LANES
        ]
    output_rows_ref[member, 5 * share :, :] = jnp.zeros((32, LANES), BF16)
    empty = jnp.zeros((1, HEAD), F32)
    for head in range(HEADS):
        columns = slice(head * HEAD, (head + 1) * HEAD)
        bias_ref[head : head + 1, :] = jnp.concatenate(
            [
                empty,
                row_of(value_bias_ref)[:, columns],
                row_of(query_bias_ref)[:, columns],
                empty[:, :16],
            ],
            axis=1,
        )


    loads[4].wait()
    empty = jnp.zeros((8, LANES), F32)

    def turn(channel):
        begin = channel * PADDED
        turned_ref[pl.ds(begin, 8), :] = empty
        turned_ref[pl.ds(begin + 136, 8), :] = empty
        turned_ref[pl.ds(begin + 8, LANES), :GROUP] = jnp.transpose(taps_ref[channel]).astype(F32)

    loop(0, share, turn, 16)
    send_signal(1)

    def lay(step):
        for group in range(2):
            taps = [
                turned_ref[
                    pl.ds(group * GROUP * PADDED + step * 3 + 6 + at, GROUP, stride=PADDED), :
                ].astype(BF16)[:, :GROUP]
                for at in range(5)
            ]
            for phase in range(PHASES):
                row = jnp.concatenate(
                    taps[2 - phase : 5 - phase] + [jnp.zeros((GROUP, 16), BF16)], axis=1
                )
                begin = pl.multiple_of((step * PHASES + phase) * GROUP, 16)
                matrix_ref[group, pl.ds(begin, GROUP), :] = row

    rows.second()
    loop(0, STEPS, lay, 4)
    rows.second_far()

    frames = MEMBERS * frame_count
    tail = 64 + frames + (64 + frames) // BLOCK

    def back_copy(group, at):
        to = lax.rem(member + at, MEMBERS)
        return remote(
            back_ref.at[group, to],
            returned_ref.at[group, member],
            back_send.at[group * 7 + at - 1],
            back_recv.at[group * 7 + at - 1],
            (record, to),
        )

    for group in range(2):
        frames_ref[:64, :] = jnp.zeros((64, LANES), F32)
        frames_ref[tail:, :] = jnp.zeros((frames_ref.shape[0] - tail, LANES), F32)
        for at in range(1, MEMBERS):
            signal_copy(group, at).wait_recv()

        def place(of, group=group):
            begin = of * (frame_count + 2) + 64
            packed = got_ref.at[group, of]
            for low, high, skew in (
                (0, 64, 0),
                (64, 160, 1),
                (160, 192, 1),
                (192, 224, 2),
                (224, 256, 2),
            ):
                frames_ref[pl.ds(begin + low + skew, high - low), :GROUP] = unpack(
                    packed, low, high
                ).astype(F32)

        loop(0, MEMBERS, place, 2)

        def widen(row):
            parts = []
            for phase in range(PHASES):
                at = row * PHASES + phase
                part = frames_ref[pl.ds(at + at // BLOCK, 16, stride=BLOCK + 1), :]
                parts.append(part.astype(BF16)[:, :GROUP])
            spread_ref[row] = jnp.concatenate(parts + [jnp.zeros((16, 16), BF16)], axis=1)

        loop(0, STEPS * 2, widen, 11)
        if group == 0:
            outs.first()
        window = jnp.concatenate(
            [
                spread_ref[step : step + SPAN].reshape(SPAN * 16, 2 * LANES)
                for step in range(STEPS)
            ],
            axis=1,
        )
        weights = jnp.concatenate(
            [matrix_ref[group, step * 240 : step * 240 + 240, :] for step in range(STEPS)],
            axis=1,
        )
        total_ref[...] = lax.dot_general(
            window, weights, (((1,), (1,)), ((), ())), preferred_element_type=F32
        )
        bias = row_of(tap_bias_ref)[:, group * GROUP : (group + 1) * GROUP]
        bias = jnp.concatenate([bias] * PHASES, axis=1)

        def activate(row, bias=bias):
            value = total_ref[pl.ds(pl.multiple_of(row * 16, 16), 16), :] + bias
            value = value * (1.0 + lax.erf(value * (0.5**0.5))) * 0.5
            for phase in range(PHASES):
                part = value[:, phase * GROUP : (phase + 1) * GROUP]
                part = jnp.concatenate([part, jnp.zeros((16, LANES - GROUP), F32)], axis=1)
                begin = row * PHASES + phase
                begin = begin + begin // BLOCK
                natural_ref[pl.ds(begin, 16, stride=BLOCK + 1), :] = part

        loop(0, SPAN, activate, 11)

        def pack_back(to, group=group):
            begin = 2 * to * (BLOCK + 1)
            halves = [
                natural_ref[pl.ds(begin + side * (BLOCK + 1), BLOCK), :].astype(BF16)[:, :GROUP]
                for side in range(2)
            ]
            back_ref[group, to] = pack(jnp.concatenate(halves, axis=0))

        loop(0, MEMBERS, pack_back, 4)
        for at in (4, 3, 5, 2, 6, 1, 7):
            back_copy(group, at).start()
        returned_ref[group, member] = back_ref[group, member]
        if group == 0:
            rows.third()

    for group in range(2):
        for at in range(1, MEMBERS):
            back_copy(group, at).wait_recv()
    for begin in range(0, frame_count, 32):
        pieces = [
            unpack(returned_ref.at[group, of], begin, begin + 32)
            for of in range(MEMBERS)
            for group in range(2)
        ]
        position = jnp.concatenate(pieces, axis=1)
        hidden = signal_ref[begin : begin + 32, :].astype(F32) + position.astype(F32)
        hidden_ref[begin : begin + 32, :] = hidden
        average = jnp.mean(hidden, axis=-1, keepdims=True)
        centered = hidden - average
        variance = jnp.mean(centered * centered, axis=-1, keepdims=True)
        normed_ref[begin : begin + 32, :] = (
            centered * lax.rsqrt(variance + EPSILON) * row_of(gain_ref) + row_of(shift_ref)
        ).astype(BF16)

    rows.fourth((0, 1, 2, 3))
    rows.near()
    lane = lax.broadcasted_iota(jnp.int32, (BLOCK, 2 * LANES), 1) - 3 * HEAD
    masks = []
    for block in range(2):
        unlisted = jnp.where(lane >= 0, 1.0, 0.0)
        for at in range(blocks_ref.shape[1]):
            unlisted = jnp.where(lane == jnp.where(lane >= 0, blocks_ref[block, at], -1000), 0.0, unlisted)
        masks.append(unlisted)
    mask = jnp.concatenate(masks, axis=0)

    rest = share - LANES

    def head_copy(source, to, at):
        return remote(
            slab_ref.at[to],
            headed_ref.at[source],
            head_send.at[at],
            head_recv.at[source],
            (record, to),
        )

    def ask_copy(source, to, at):
        return remote(
            asked_ref.at[to],
            asking_ref.at[source],
            ask_send.at[at],
            ask_recv.at[source],
            (record, to),
        )

    def chosen_head(at):
        turned = lax.rem(member + at, 4)
        first = jnp.where(at < 4, record, across)
        second = first + 1 - 2 * lax.rem(first, 2)
        quarter = jnp.where(turned < 2, first, second)
        return quarter, lax.rem(turned, 2)

    def project(at):
        quarter, side = chosen_head(at)
        head, tile = quarter + 4 * side, 4 * quarter + 2 * side
        weights = jnp.concatenate([rows_ref[tile], rows_ref[tile + 1]], axis=1)
        slab = jnp.dot(normed_ref[...], weights, preferred_element_type=F32)
        slab = (slab + bias_ref[pl.ds(head, 1), :] + mask).astype(BF16)
        slab_ref[head, :frame_count, :] = slab[:, :LANES]
        slab_ref[head, frame_count:, :] = jnp.concatenate(
            [slab[64 * part : 64 * part + 64, LANES:share] for part in range(4)], axis=1
        )
        asked = slab[:, share:]
        asked_ref[head] = jnp.concatenate(
            [
                asked[:192],
                jnp.concatenate(
                    [asked[192:, part * 32 : part * 32 + 32] for part in range(3)], axis=0
                ),
            ],
            axis=1,
        )

        @pl.when(head != member)
        def _():
            head_copy(member, head, at).start()

        @pl.when(head == member)
        def _():
            headed_ref[member] = slab_ref[head]

    def send_asked(at):
        quarter, side = chosen_head(at)
        head = quarter + 4 * side

        @pl.when(head != member)
        def _():
            ask_copy(member, head, at).start()

    for at in range(4):
        project(at)
    for at in range(4):
        send_asked(at)
    rows.fourth((4, 5, 6))
    outs.second()
    outs.second_far()
    rows.far()
    for at in range(4, 8):
        project(at)
    for at in range(4, 8):
        send_asked(at)
    asking_ref[member] = asked_ref[member]
    outs.third()

    place_row = lax.broadcasted_iota(jnp.int32, (BLOCK, frames), 0)
    place_column = lax.broadcasted_iota(jnp.int32, (BLOCK, frames), 1)
    for at in range(GLOBALS):
        chosen_ref[at * BLOCK : (at + 1) * BLOCK, :] = jnp.where(
            place_row + globals_ref[at] * BLOCK == place_column, 1.0, 0.0
        ).astype(BF16)

    def arrange(of):
        slab = headed_ref[of]
        begin = pl.multiple_of(of * frame_count, 256)
        row = lax.broadcasted_iota(jnp.int32, (frame_count, 16), 0)
        block = 2 * of + jnp.where(row >= BLOCK, 1, 0)
        here = lax.broadcasted_iota(jnp.int32, (frame_count, 16), 1) == block
        keys_ref[pl.ds(begin, frame_count), :] = jnp.concatenate(
            [
                slab[:frame_count, :HEAD],
                jnp.where(here, -BIG, 0.0).astype(BF16),
                jnp.zeros((frame_count, 32), BF16),
            ],
            axis=1,
        )
        side = jnp.concatenate(
            [slab[frame_count:, rest * part : rest * part + rest] for part in range(4)], axis=0
        )
        values_ref[pl.ds(begin, frame_count), :] = jnp.concatenate(
            [
                slab[:frame_count, HEAD:],
                side,
                jnp.ones((frame_count, 16), BF16),
                jnp.zeros((frame_count, 32), BF16),
            ],
            axis=1,
        )

    arrange(member)
    for at in range(1, MEMBERS):
        of = lax.rem(member + at, MEMBERS)
        head_copy(of, member, 0).wait_recv()
        arrange(of)
    lane = lax.broadcasted_iota(jnp.int32, (BLOCK, LANES), 1)
    picked = jnp.dot(
        chosen_ref[...],
        jnp.concatenate([keys_ref[:frames, :], values_ref[:frames, :]], axis=1),
        preferred_element_type=F32,
    )
    for at in range(GLOBALS):
        rows_at = slice(at * BLOCK, (at + 1) * BLOCK)
        keys_ref[frames + at * BLOCK : frames + (at + 1) * BLOCK, :] = jnp.where(
            lane < HEAD,
            picked[rows_at, :LANES],
            jnp.where(lane == HEAD + 16 + globals_ref[at], -BIG, 0.0),
        ).astype(BF16)
        values_ref[frames + at * BLOCK : frames + (at + 1) * BLOCK, :] = picked[
            rows_at, LANES:
        ].astype(BF16)

    factor = (1.0 / math.sqrt(HEAD)) * math.log2(math.e)

    def context_copy(bits):
        to = flip(member, bits)
        return remote(
            context_ref.at[to],
            contexts_ref.at[member],
            context_send.at[bits - 1],
            context_recv.at[bits - 1],
            (record, to),
        )

    def attend_tile(of):
        asked = asking_ref[of]
        last = jnp.concatenate(
            [asked[64 * part : 64 * part + 64, 96:] for part in range(3)], axis=1
        )
        asked = jnp.concatenate([asked[:, :96], last], axis=0)
        queries = jnp.concatenate(
            [asked, 1.0 - asked[:, HEAD:], jnp.zeros((frame_count, 16), BF16)], axis=1
        )
        low = jnp.minimum(jnp.maximum(2 * of - 2, 0), 10)
        window = pl.ds(pl.multiple_of(low * BLOCK, BLOCK), 6 * BLOCK)
        keys = jnp.concatenate([keys_ref[window, :], keys_ref[frames:, :]], axis=0)
        scores = lax.dot_general(
            queries, keys, (((1,), (1,)), ((), ())), preferred_element_type=F32
        )
        peak = jnp.max(scores, axis=1, keepdims=True)
        weights = jnp.exp2(scores * factor - peak * factor).astype(BF16)
        values = jnp.concatenate([values_ref[window, :], values_ref[frames:, :]], axis=0)
        summed = jnp.dot(weights, values, preferred_element_type=F32)
        return pack((summed[:, :HEAD] / summed[:, HEAD : HEAD + 1]).astype(BF16))

    contexts_ref[member] = attend_tile(member)
    for pair in ((1,), (2, 3), (4, 5), (6, 7)):
        for bits in pair:
            ask_copy(flip(member, bits), member, 0).wait_recv()
        for bits in pair:
            of = flip(member, bits)
            context_ref[of] = attend_tile(of)
            context_copy(bits).start()
    outs.fourth(range(7))

    for at in range(1, MEMBERS):
        context_copy(at).wait_recv()
    outs.near()
    outs.far()
    context = jnp.concatenate(
        [
            jnp.concatenate(
                [
                    unpack(contexts_ref.at[of], 0, 160),
                    unpack(contexts_ref.at[of], 160, 224),
                    unpack(contexts_ref.at[of], 224, 256),
                ],
                axis=0,
            )
            for of in range(HEADS)
        ],
        axis=1,
    )
    columns = jnp.concatenate(
        [
            jnp.concatenate(
                [output_rows_ref[of, share * at : share * at + share, :] for at in range(5)], axis=1
            )
            for of in range(MEMBERS)
        ],
        axis=0,
    )
    projected = lax.dot_general(
        context, columns, (((1,), (1,)), ((), ())), preferred_element_type=F32
    )
    out_ref[...] = (hidden_ref[...] + projected + row_of(output_bias_ref)).astype(BF16)

    for at in range(1, MEMBERS):
        for group in range(2):
            signal_copy(group, at).wait_send()
            back_copy(group, at).wait_send()
        context_copy(at).wait_send()
    for at in range(MEMBERS):
        quarter, side = chosen_head(at)

        @pl.when(quarter + 4 * side != member)
        def _(head=quarter + 4 * side, at=at):
            head_copy(member, head, at).wait_send()
            ask_copy(member, head, at).wait_send()

    rows.sent()
    outs.sent()


def by_heads(
    signal,
    position_kernel,
    position_bias,
    layer_gain,
    layer_shift,
    query_weight,
    query_bias,
    key_weight,
    value_weight,
    value_bias,
    output_weight,
    output_bias,
    key_blocks,
    global_blocks,
):
    frame_count, width = signal.shape
    frames = MEMBERS * frame_count
    share = 2 * GROUP
    vmem = pl.BlockSpec(memory_space=pltpu.VMEM)
    smem = pl.BlockSpec(memory_space=pltpu.SMEM)
    hbm = pl.BlockSpec(memory_space=pl.ANY)
    dma = pltpu.SemaphoreType.DMA
    return pl.pallas_call(
        whole_kernel,
        out_shape=jax.ShapeDtypeStruct((frame_count, width), BF16),
        in_specs=[smem, smem, hbm, hbm] + [vmem] * 3 + [hbm] * 3 + [vmem] * 2 + [hbm, vmem],
        out_specs=vmem,
        scratch_shapes=[
            pltpu.VMEM((frame_count, width), BF16),
            pltpu.VMEM((share, HEADS * HEAD), BF16),
            pltpu.VMEM((share, HEADS * HEAD), BF16),
            pltpu.VMEM((share, HEADS * HEAD), BF16),
            pltpu.VMEM((share, HEADS * HEAD), BF16),
            pltpu.VMEM((share, GROUP, LANES), BF16),
            pltpu.VMEM((share * PADDED, LANES), F32),
            pltpu.VMEM((2, STEPS * PHASES * GROUP, 2 * LANES), BF16),
            pltpu.VMEM((2, MEMBERS, PACKED, LANES), BF16),
            pltpu.VMEM((2, MEMBERS, PACKED, LANES), BF16),
            pltpu.VMEM((frames + 160, LANES), F32),
            pltpu.VMEM((STEPS * 2, 16, 2 * LANES), BF16),
            pltpu.VMEM((SPAN * 16, PHASES * GROUP), F32),
            pltpu.VMEM((frames + 32, LANES), F32),
            pltpu.VMEM((2, MEMBERS, PACKED, LANES), BF16),
            pltpu.VMEM((2, MEMBERS, PACKED, LANES), BF16),
            pltpu.VMEM((frame_count, width), F32),
            pltpu.VMEM((frame_count, width), BF16),
            pltpu.VMEM((2 * HEADS, width, LANES), BF16),
            pltpu.VMEM((MEMBERS, 832, LANES), BF16),
            pltpu.VMEM((HEADS, 2 * LANES), F32),
            pltpu.VMEM((MEMBERS, frame_count + 64, LANES), BF16),
            pltpu.VMEM((MEMBERS, frame_count + 64, LANES), BF16),
            pltpu.VMEM((MEMBERS, 192, LANES), BF16),
            pltpu.VMEM((MEMBERS, 192, LANES), BF16),
            pltpu.VMEM((frames + GLOBALS * BLOCK, LANES), BF16),
            pltpu.VMEM((frames + GLOBALS * BLOCK, LANES), BF16),
            pltpu.VMEM((GLOBALS * BLOCK, frames), BF16),
            pltpu.VMEM((MEMBERS, PACKED, LANES), BF16),
            pltpu.VMEM((MEMBERS, PACKED, LANES), BF16),
            dma((6,)),
            dma((14,)),
            dma((14,)),
            dma((14,)),
            dma((14,)),
            dma((28,)),
            dma((28,)),
            dma((28,)),
            dma((28,)),
            dma((8,)),
            dma((8,)),
            dma((8,)),
            dma((8,)),
            dma((7,)),
            dma((7,)),
        ],
        compiler_params=pltpu.CompilerParams(
            collective_id=0, has_side_effects=True, vmem_limit_bytes=60 * 1024 * 1024
        ),
    )(
        key_blocks,
        global_blocks,
        signal,
        position_kernel,
        position_bias,
        layer_gain,
        layer_shift,
        query_weight,
        key_weight,
        value_weight,
        query_bias,
        value_bias,
        output_weight.T,
        output_bias,
    )


def body(*operands):
    share, width, taps = operands[1].shape
    fits = lax.axis_size("tm") == MEMBERS and lax.axis_size("rec") == QUARTERS
    fits = fits and (share, width, taps) == (2 * GROUP, GROUP, LANES)
    fits = fits and operands[0].shape[0] == 2 * BLOCK
    return (by_heads if fits else general)(*operands)


def solution(mesh):
    placed = (
        P(("rec", "tm"), None),
        P("tm", None, None),
        P("tm"),
        P(),
        P(),
        P("tm", None),
        P(),
        P("tm", None),
        P("tm", None),
        P(),
        P(None, "tm"),
        P(),
        P(("rec", "tm"), None),
        P("rec"),
    )
    return jax.shard_map(
        body, mesh=mesh, in_specs=placed, out_specs=P(("rec", "tm"), None), check_vma=False
    )
```
